32 devices in a mesh: nodes: 16 (over z, y, core), hid: 2 (over x).
Axes of the slice: x: 2, y: 2, z: 4, core: 2. Of those that a mesh axis runs over, the one named last changes fastest.
Arguments:
- features: bfloat16 [24576, 512], P(('nodes', 'hid')), may hold values from -6 to 6
- levels: int32 [24576], P(('nodes', 'hid')), may hold values from 0 to 1
- neighbour_index: int32 [24576, 16], P(('nodes', 'hid')), may hold values from 0 to 24575, as said below
- neighbour_count: int32 [24576], P(('nodes', 'hid')), may hold values from 2 to 16
- cotangent: bfloat16 [24576, 512], P(('nodes', 'hid')), may hold values from -6 to 6
- attention_weight: float32 [4, 512, 512], replicated
- up_weight: float32 [512, 2048], P(None, 'hid'), may hold values from -0.25 to 0.25
- down_weight: float32 [2048, 512], P('hid'), may hold values from -0.125 to 0.125
- modulation: float32 [2, 4, 512], replicated, may hold values from -0.5 to 0.5
- attention_moment: float32 [4, 512, 512], P(None, 'hid')
- up_moment: float32 [512, 2048], P(None, 'hid')
- down_moment: float32 [2048, 512], P('hid')
- modulation_moment: float32 [2, 4, 512], P(None, 'hid')
Outputs:
- output: bfloat16 [24576, 512], P(('nodes', 'hid'))
- features_grad: float32 [24576, 512], P(('nodes', 'hid'))
- attention_moment_new: float32 [4, 512, 512], P(None, 'hid')
- attention_new: float32 [4, 512, 512], P(None, 'hid')
- up_moment_new: float32 [512, 2048], P(None, 'hid')
- up_new: float32 [512, 2048], P(None, 'hid')
- down_moment_new: float32 [2048, 512], P('hid')
- down_new: float32 [2048, 512], P('hid')
- modulation_moment_new: float32 [2, 4, 512], P(None, 'hid')
- modulation_new: float32 [2, 4, 512], P(None, 'hid')
The draws below stay inside these ranges and needn't reach their ends.
Inputs may be any that keep to these rules, and one draw needn't show every extreme that they name: `neighbour_index`: slot 0 of every node names the node itself; every slot names a node whose index is at most 192 from the node's own, and slot 1 names the node exactly 192 away wherever that index exists. Slots past a node's count also hold valid indices.
All inputs are finite; a program needn't handle non-finite values.
Results may differ from the reference program's by a relative error of at most 0.018.
The reference program's roundings to bfloat16 on the way count: a program that leaves them out, or rounds other values in their place, can miss the bound.
Values may be sent and summed in bfloat16 or wider, within the bound.
No kernel may reach another device: no remote copies, remote signals or barrier semaphores. Data moves between devices by JAX's collectives and lax.ppermute only.
A program may use at most 192 MiB of HBM per device.

```python
import math
import jax
import jax.numpy as jnp
from jax import lax

D = 512
HEADS = 4
HD = 128
FF = 2048
K = 16
LEVELS = 2
NS_STEPS = 4
HALO = 192
NODES = 24576
N_HID = 2


def draw_neighbour_index(key, part):
    node_ids = jnp.arange(NODES, dtype=jnp.int32)
    offsets = jax.random.randint(jax.random.fold_in(key, 11), (NODES, K), -HALO, HALO + 1, dtype=jnp.int32)
    side_offset = jnp.where(node_ids % 2 == 0, -HALO, HALO).astype(jnp.int32)
    slot_ids = jnp.arange(K, dtype=jnp.int32)[None, :]
    offsets = jnp.where(slot_ids == 0, 0, jnp.where(slot_ids == 1, side_offset[:, None], offsets))
    return jnp.clip(node_ids[:, None] + offsets, 0, NODES - 1).astype(jnp.int32)


def draw_neighbour_count(key, part):
    node_ids = jnp.arange(NODES, dtype=jnp.int32)
    drawn_count = jax.random.randint(jax.random.fold_in(key, 23), (NODES,), 2, K + 1, dtype=jnp.int32)
    return jnp.where(node_ids % 8 == 0, K, jnp.where(node_ids % 8 == 1, 2, drawn_count)).astype(jnp.int32)


def draw_attention_weight(key, part):
    noise = jax.random.normal(jax.random.fold_in(key, 31), (4, D, D), dtype=jnp.float32)
    spread = jnp.where(jnp.arange(4) < 3, (2.0 / D) ** 0.5, (4.0 / D) ** 0.5).astype(jnp.float32)
    return noise * spread[:, None, None]


def moment_draw(key, array_shape, factor):
    return jax.random.normal(key, array_shape, dtype=jnp.float32) * (factor * NODES ** 0.5)


def draw_attention_moment(key, part):
    return moment_draw(jax.random.fold_in(key, 41), (4, D, D), 1.0)


def draw_up_moment(key, part):
    return moment_draw(jax.random.fold_in(key, 43), (D, FF), 0.5)


def draw_down_moment(key, part):
    return moment_draw(jax.random.fold_in(key, 47), (FF, D), 0.5)


def draw_modulation_moment(key, part):
    return moment_draw(jax.random.fold_in(key, 53), (LEVELS, 4, D), 1.0)


def plant(array, key, low, top_value):
    longest = array.shape.index(max(array.shape))
    spots = []
    for shift in (0, 1):
        where = [jax.random.randint(jax.random.fold_in(key, axis), (), 0, length) for axis, length in enumerate(array.shape)]
        where[longest] = (where[longest] + shift) % array.shape[longest]
        spots.append(tuple(where))
    return array.at[spots[0]].set(low).at[spots[1]].set(top_value)


def level_of(key, dims, cuts, least, largest):
    level = 1.0
    for position, shards_of in cuts:
        steps = jax.random.uniform(jax.random.fold_in(jax.random.fold_in(key, 6), position), (shards_of,), jnp.float32, least / len(cuts), largest / len(cuts))
        level = level * jnp.repeat(jnp.exp(steps), dims[position] // shards_of).reshape((-1,) + (1,) * (len(dims) - 1 - position))
    return level


def gaussian(own_key, extent, deviation, most, split=(), kind=jnp.bfloat16):
    entries = jax.random.normal(own_key, extent, jnp.float32) * deviation
    if len(split) > 0:
        entries = level_of(own_key, extent, split, -0.22, 0.18) * entries
    return jnp.clip(entries, min=-most, max=most).astype(kind)


def setup_inputs(seed: int = 0) -> dict:
    streams_of = jax.random.split(jax.random.key(seed), 14)
    features = gaussian(streams_of[0], (NODES, D), 1.0, 6.0, ((0, 32),))
    levels = plant(jax.random.randint(streams_of[1], (NODES,), 0, LEVELS), jax.random.fold_in(streams_of[1], 1), 0, LEVELS - 1).astype(jnp.int32)
    neighbour_index = draw_neighbour_index(jax.random.fold_in(streams_of[13], 71), 0)
    neighbour_count = draw_neighbour_count(jax.random.fold_in(streams_of[13], 71), 0)
    cotangent = gaussian(streams_of[4], (NODES, D), 1.0, 6.0, ((0, 32),))
    attention_weight = draw_attention_weight(jax.random.fold_in(streams_of[13], 71), 0)
    up_weight = gaussian(streams_of[6], (D, FF), D ** -0.5, 0.25, ((1, 2),), jnp.float32)
    down_weight = gaussian(streams_of[7], (FF, D), FF ** -0.5, 0.125, ((0, 2),), jnp.float32)
    modulation = jnp.clip(jax.random.uniform(streams_of[8], (LEVELS, 4, D), jnp.float32, -0.5, 0.5), -0.5, 0.5)
    attention_moment = draw_attention_moment(jax.random.fold_in(streams_of[13], 71), 0)
    up_moment = draw_up_moment(jax.random.fold_in(streams_of[13], 71), 0)
    down_moment = draw_down_moment(jax.random.fold_in(streams_of[13], 71), 0)
    modulation_moment = draw_modulation_moment(jax.random.fold_in(streams_of[13], 71), 0)
    return dict(features=features, levels=levels, neighbour_index=neighbour_index, neighbour_count=neighbour_count, cotangent=cotangent, attention_weight=attention_weight, up_weight=up_weight, down_weight=down_weight, modulation=modulation, attention_moment=attention_moment, up_moment=up_moment, down_moment=down_moment, modulation_moment=modulation_moment)


@jax.custom_vjp
def low(v):
    return lax.optimization_barrier(v.astype(jnp.bfloat16)).astype(jnp.float32)

@jax.custom_vjp
def low_back(v):
    return v

def low_keep(v):
    return (low(v), None)

def low_pass(kept, grad):
    return (grad,)

def back_keep(v):
    return (v, None)

def back_low(kept, grad):
    return (low(grad),)
low.defvjp(low_keep, low_pass)
low_back.defvjp(back_keep, back_low)
highest = lax.Precision.HIGHEST
ns_first = 3.4445
ns_second = -4.775
ns_third = 2.0315
momentum_rate = 0.95
vector_rate = 0.9
muon_rate = 0.2
decay_rate = 0.1

def product(left, right):
    return jnp.dot(left, right, precision=highest, preferred_element_type=jnp.float32)

def modulate(field, picked, modulation, column):
    average = lax.optimization_barrier(jnp.mean(field, axis=-1, keepdims=True))
    centred = field - average
    variance = lax.optimization_barrier(jnp.mean(centred * centred, axis=-1, keepdims=True))
    normed = centred * lax.rsqrt(variance + 1e-06)
    scale_rows = product(picked, modulation[:, column, :])
    shift_rows = product(picked, modulation[:, column + 1, :])
    return normed * (1.0 + scale_rows) + shift_rows

def attend_block(queries, neighbour_index, neighbour_count, keys, values):
    row_count = queries.shape[0]
    near_keys = keys[neighbour_index].reshape(row_count, K, HEADS, HD)
    near_values = values[neighbour_index].reshape(row_count, K, HEADS, HD)
    scores = jnp.einsum('bhd,bkhd->bhk', queries.reshape(row_count, HEADS, HD), near_keys, precision=highest) * (1.0 / math.sqrt(HD))
    scores = low_back(scores)
    live_slots = (jnp.arange(K, dtype=jnp.int32)[None, :] < neighbour_count[:, None])[:, None, :]
    masked = jnp.where(live_slots, scores, -1e+30)
    peak_score = lax.optimization_barrier(jnp.max(masked, axis=-1, keepdims=True))
    exponent = jnp.where(live_slots, jnp.exp(masked - peak_score), 0.0)
    weights = low(exponent / lax.optimization_barrier(jnp.sum(exponent, axis=-1, keepdims=True)))
    attended = jnp.einsum('bhk,bkhd->bhd', weights, near_values, precision=highest)
    return attended.reshape(row_count, HEADS * HD)

def block_layer(stream, attention_weight, up_weight, down_weight, modulation, picked, neighbour_index, neighbour_count):
    weights = low(attention_weight)
    first_in = low(modulate(stream, picked, modulation, 0))
    queries = low_back(low(product(first_in, weights[0])))
    keys = low_back(low(product(first_in, weights[1])))
    values = low_back(low(product(first_in, weights[2])))
    block_rows = math.gcd(NODES, 2048)
    block_count = NODES // block_rows

    def one_block(inputs):
        return attend_block(inputs[0], inputs[1], inputs[2], keys, values)
    attended = lax.map(jax.checkpoint(one_block), (queries.reshape(block_count, block_rows, D), neighbour_index.reshape(block_count, block_rows, K), neighbour_count.reshape(block_count, block_rows)))
    attended = low_back(low(attended.reshape(NODES, D)))
    hidden_state = stream + low_back(product(attended, weights[3]))
    second_in = low(modulate(hidden_state, picked, modulation, 2))
    preact = low_back(product(second_in, low(up_weight)))
    activation = low(jax.nn.silu(preact))
    return hidden_state + low_back(product(activation, low(down_weight)))

def orthogonalize(matrix, by_rows):
    row_count, col_count = matrix.shape
    frob_norm = jnp.sqrt(jnp.sum(matrix * matrix))
    current = low(matrix / (frob_norm + 1e-07))
    for repeat in range(NS_STEPS):
        if by_rows:
            blocks = current.reshape(N_HID, row_count // N_HID, col_count)
            partials = jnp.einsum('prc,prd->pcd', blocks, blocks, precision=highest)
        else:
            blocks = current.reshape(row_count, N_HID, col_count // N_HID)
            partials = jnp.einsum('rpc,spc->prs', blocks, blocks, precision=highest)
        gram_sum = low(lax.optimization_barrier(jnp.sum(low(partials), axis=0)))
        polynomial = low(ns_second * gram_sum + ns_third * product(gram_sum, gram_sum))
        if by_rows:
            current = low(ns_first * current + product(current, polynomial))
        else:
            current = low(ns_first * current + product(polynomial, current))
    return current

def muon_step(weight, gradient, moment, by_rows):
    moment_new = momentum_rate * moment + gradient
    ortho = orthogonalize(gradient + momentum_rate * moment_new, by_rows)
    longest = max(weight.shape)
    return (moment_new, weight - muon_rate * (0.2 * math.sqrt(longest) * ortho + decay_rate * weight))

def reference(features, levels, neighbour_index, neighbour_count, cotangent, attention_weight, up_weight, down_weight, modulation, attention_moment, up_moment, down_moment, modulation_moment):
    picked = (levels[:, None] == jnp.arange(LEVELS, dtype=jnp.int32)[None, :]).astype(jnp.float32)

    def forward(stream, attn_w, up_w, down_w, mod_w):
        return block_layer(stream, attn_w, up_w, down_w, mod_w, picked, neighbour_index, neighbour_count)
    result, pullback = jax.vjp(forward, features.astype(jnp.float32), attention_weight, up_weight, down_weight, modulation)
    features_grad, attention_grad, up_grad, down_grad, modulation_grad = pullback(cotangent.astype(jnp.float32))
    moments_new = []
    weights_new = []
    for which in range(4):
        moment_new, weight_new = muon_step(attention_weight[which], attention_grad[which], attention_moment[which], True)
        moments_new.append(moment_new)
        weights_new.append(weight_new)
    up_moment_new, up_new = muon_step(up_weight, up_grad, up_moment, False)
    down_moment_new, down_new = muon_step(down_weight, down_grad, down_moment, True)
    modulation_moment_new = vector_rate * modulation_moment + modulation_grad
    modulation_new = modulation - 0.2 / math.sqrt(NODES) * modulation_moment_new
    return (result.astype(jnp.bfloat16), features_grad, jnp.stack(moments_new), jnp.stack(weights_new), up_moment_new, up_new, down_moment_new, down_new, modulation_moment_new, modulation_new)
```

```python
import functools
import math

import jax
import jax.numpy as jnp
from jax import lax
from jax.experimental import pallas as pl
from jax.experimental.pallas import tpu as pltpu
from jax.sharding import PartitionSpec as P

D = 512
HEADS = 4
HD = 128
FF = 2048
K = 16
NS_STEPS = 4
HALO = 192
BLOCK = 128
SPAN = BLOCK + 2 * HALO
RIM = 256
CHUNK = 512
TABLE_ROWS = 16

f32 = jnp.float32
bf16 = jnp.bfloat16
ns_first = 3.4445
ns_second = -4.775
ns_third = 2.0315
momentum_rate = 0.95
vector_rate = 0.9
muon_rate = 0.2
decay_rate = 0.1
score_scale = 1.0 / math.sqrt(HD)
AXES = ("nodes", "hid")
VMEM = pl.BlockSpec(memory_space=pltpu.VMEM)
SMEM = pl.BlockSpec(memory_space=pltpu.SMEM)


def nn(a, b):
    return lax.dot_general(a, b, (((1,), (0,)), ((), ())), preferred_element_type=f32)


def nt(a, b):
    return lax.dot_general(a, b, (((1,), (1,)), ((), ())), preferred_element_type=f32)


def tn(a, b):
    return lax.dot_general(a, b, (((0,), (0,)), ((), ())), preferred_element_type=f32)


def struct(shape, dtype):
    return jax.ShapeDtypeStruct(shape, dtype)


def rows_of(start, size):
    return pl.ds(pl.multiple_of(start, size), size)


def cost(flops, data):
    return pl.CostEstimate(flops=int(flops), bytes_accessed=int(data), transcendentals=0)


def norm_parts(field):
    average = jnp.mean(field, axis=-1, keepdims=True)
    centred = field - average
    variance = jnp.mean(centred * centred, axis=-1, keepdims=True)
    inverse = lax.rsqrt(variance + 1e-06)
    return centred * inverse, inverse


def table_rows(mod_ref, level, column):
    return jnp.where(level > 0.5, mod_ref[4 + column : 5 + column, :], mod_ref[column : column + 1, :])


def modulated(field, level, mod_ref, column):
    normed, _ = norm_parts(field)
    return normed * (1.0 + table_rows(mod_ref, level, column)) + table_rows(
        mod_ref, level, column + 1
    )


def norm_back(grad_out, field, level, mod_ref, column):
    normed, inverse = norm_parts(field)
    grad_norm = grad_out * (1.0 + table_rows(mod_ref, level, column))
    grad_in = inverse * (
        grad_norm
        - jnp.mean(grad_norm, axis=-1, keepdims=True)
        - normed * jnp.mean(grad_norm * normed, axis=-1, keepdims=True)
    )
    return grad_in, grad_out * normed


def add_table(table_ref, column, level, scale_term, shift_term):
    upper = level > 0.5
    for term, place in ((scale_term, column), (shift_term, column + 1)):
        low_part = jnp.sum(jnp.where(upper, 0.0, term), axis=0, keepdims=True)
        high_part = jnp.sum(jnp.where(upper, term, 0.0), axis=0, keepdims=True)
        table_ref[place : place + 1, :] += low_part
        table_ref[4 + place : 5 + place, :] += high_part


def slot_counts(pack, row_count, width, shift):
    pieces = []
    for left in range(0, width, 128):
        lanes = lax.broadcasted_iota(jnp.int32, (row_count, 128), 1)
        rows = lax.broadcasted_iota(jnp.int32, (row_count, 128), 0)
        place = (lanes - rows + (left - shift)).astype(f32)
        total = jnp.zeros((row_count, 128), f32)
        for slot in range(K):
            total = total + jnp.where(place == pack[:, slot : slot + 1], 1.0, 0.0)
        pieces.append(total)
    return jnp.concatenate(pieces, axis=1).astype(bf16)


def project_kernel(features, pack, mod, weights, first_in, qkv, counts):
    blocks = features.shape[0] // BLOCK

    def step(b, carry):
        rows = rows_of(b * BLOCK, BLOCK)
        level = pack[rows, K : K + 1]
        first_in[rows, :] = modulated(features[rows, :].astype(f32), level, mod, 0).astype(bf16)
        return carry

    lax.fori_loop(0, blocks, step, 0)
    for p in range(3):
        qkv[p] = nn(first_in[...], weights[p]).astype(bf16)

    def count_step(b, carry):
        rows = rows_of(b * BLOCK, BLOCK)
        counts[rows, :] = slot_counts(pack[rows, :], BLOCK, SPAN, HALO)
        return carry

    lax.fori_loop(0, blocks, count_step, 0)


def forward_kernel(
    rim_low,
    rim_high,
    features,
    pack,
    mod,
    weights,
    qkv,
    counts,
    attended,
    stream,
    second_in,
    padded,
    rim_queries,
    rim_counts,
    log_totals,
    rim_in,
):
    row_count = features.shape[0]
    for side, rim in enumerate((rim_low, rim_high)):
        for start in range(0, HALO, 64):
            rows = slice(start, start + 64)
            info = rim[rows, D:].astype(f32)
            rim_in[side * HALO + start : side * HALO + start + 64, :] = modulated(
                rim[rows, :D].astype(f32), info[:, K : K + 1], mod, 0
            ).astype(bf16)
            rim_counts[side * HALO + start : side * HALO + start + 64, :] = slot_counts(
                info, 64, RIM, start + (-HALO if side == 0 else RIM)
            )
    rim_queries[...] = nn(rim_in[...], weights[0]).astype(bf16)
    for p in range(2):
        piece = nn(rim_in[...], weights[1 + p]).astype(bf16)
        padded[p, :HALO, :] = piece[:HALO]
        padded[p, HALO + row_count :, :] = piece[HALO:]
        padded[p, HALO : HALO + row_count, :] = qkv[1 + p]

    def step(b, carry):
        rows = rows_of(b * BLOCK, BLOCK)
        span = pl.ds(pl.multiple_of(b * BLOCK, BLOCK), SPAN)
        count = counts[rows, :].astype(f32)
        live = count > 0.0
        lanes = lax.broadcasted_iota(jnp.int32, (BLOCK, 128), 1)
        stats = jnp.zeros((BLOCK, 128), f32)
        for h in range(HEADS):
            cols = slice(h * HD, (h + 1) * HD)
            scores = nt(qkv[0, rows, cols], padded[0, span, cols]) * score_scale
            masked = jnp.where(live, scores, -1e30)
            peak = jnp.max(masked, axis=-1, keepdims=True)
            exponent = jnp.exp(masked - peak)
            total = jnp.sum(exponent * count, axis=-1, keepdims=True)
            probs = (exponent / total).astype(bf16)
            spread = (probs.astype(f32) * count).astype(bf16)
            attended[rows, cols] = nn(spread, padded[1, span, cols]).astype(bf16)
            stats = jnp.where(lanes == h, peak + jnp.log(total), stats)
        log_totals[rows, :] = stats
        return carry

    lax.fori_loop(0, row_count // BLOCK, step, 0)

    def tail(b, carry):
        rows = rows_of(b * 256, 256)
        field = features[rows, :].astype(f32) + nn(attended[rows, :], weights[3])
        stream[rows, :] = field
        second_in[rows, :] = modulated(field, pack[rows, K : K + 1], mod, 2).astype(bf16)
        return carry

    lax.fori_loop(0, row_count // 256, tail, 0)


def mlp_chunk(scalars, second_in, cotangent, up, down, branch, grad_second, acts, grads, out_up, out_down):
    row_count = second_in.shape[0]

    def step(b, carry):
        rows = rows_of(b * 256, 256)
        preact = nn(second_in[rows, :], up)
        sigmoid = 1.0 / (1.0 + jnp.exp(-preact))
        act = (preact * sigmoid).astype(bf16)
        acts[rows, :] = act
        branch[rows, :] += nn(act, down)
        grad_act = nt(cotangent[rows, :], down)
        grad_pre = (grad_act * (sigmoid * (1.0 + preact * (1.0 - sigmoid)))).astype(bf16)
        grads[rows, :] = grad_pre
        grad_second[rows, :] += nt(grad_pre, up)
        return carry

    lax.fori_loop(0, row_count // 256, step, 0)
    z1, z2 = scalars[2], scalars[3]
    for left, right, out in ((second_in, grads, out_up), (cotangent, acts, out_down)):
        product = tn(left[...], right[...])
        for q in range(4):
            out[0, (q // 2) ^ z1, (q % 2) ^ z2] = product[q * 128 : (q + 1) * 128].astype(bf16)


def mlp_own_kernel(
    scalars, second_in, cotangent, up, down, branch, grad_second, out_up, out_down, acts, grads
):
    @pl.when(pl.program_id(0) == 0)
    def _():
        branch[...] = jnp.zeros_like(branch)
        grad_second[...] = jnp.zeros_like(grad_second)

    mlp_chunk(
        scalars,
        second_in,
        cotangent,
        up[...].astype(bf16),
        down[...].astype(bf16),
        branch,
        grad_second,
        acts,
        grads,
        out_up,
        out_down,
    )


def mlp_rest_kernel(
    scalars,
    second_in,
    cotangent,
    near,
    far,
    branch_in,
    grad_in,
    stream,
    pack,
    mod,
    weights,
    attended,
    log_totals,
    out_up,
    out_down,
    output,
    grad_stream,
    grad_attended,
    stats,
    edge_low,
    edge_high,
    table,
    branch,
    grad_second,
    acts,
    grads,
):
    row_count = second_in.shape[0]
    turn = pl.program_id(0)

    @pl.when(turn == 0)
    def _():
        branch[...] = branch_in[...]
        grad_second[...] = grad_in[...]
        mlp_chunk(
            scalars, second_in, cotangent, near[0], near[1], branch, grad_second, acts, grads, out_up, out_down
        )

    @pl.when(turn == 1)
    def _():
        mlp_chunk(
            scalars, second_in, cotangent, far[0], far[1], branch, grad_second, acts, grads, out_up, out_down
        )
        table[...] = jnp.zeros_like(table)

        def step(b, carry):
            rows = rows_of(b * BLOCK, BLOCK)
            field = stream[rows, :]
            level = pack[rows, K : K + 1]
            output[rows, :] = (field + branch[rows, :]).astype(bf16)
            gradient = grad_second[rows, :]
            grad_field, scale_term = norm_back(gradient, field, level, mod, 2)
            add_table(table, 2, level, scale_term, gradient)
            total = cotangent[rows, :].astype(f32) + grad_field
            grad_stream[rows, :] = total
            back = nt(total.astype(bf16), weights[3]).astype(bf16)
            grad_attended[rows, :] = back
            product = back.astype(f32) * attended[rows, :].astype(f32)
            lanes = lax.broadcasted_iota(jnp.int32, (BLOCK, 128), 1)
            kept = log_totals[rows, :]
            for h in range(HEADS):
                delta = jnp.sum(product[:, h * HD : (h + 1) * HD], axis=-1, keepdims=True)
                kept = jnp.where(lanes == HEADS + h, delta, kept)
            stats[rows, :] = kept
            return carry

        lax.fori_loop(0, row_count // BLOCK, step, 0)
        for edge, first in ((edge_low, 0), (edge_high, row_count - HALO)):
            rows = slice(first, first + HALO)
            edge[:, :D] = grad_attended[rows, :]
            kept = stats[rows, :]
            upper = kept.astype(bf16)
            lower = (kept - upper.astype(f32)).astype(bf16).astype(f32)
            edge[:, D:] = (upper.astype(f32) + pltpu.roll(lower, 2 * HEADS, 1)).astype(bf16)


def attention_terms(query, key, value, grad, count, log_total, delta):
    scores = nt(query, key) * score_scale
    probs = jnp.exp(jnp.where(count > 0.0, scores, -1e30) - log_total)
    grad_probs = nt(grad, value)
    slopes = (probs * (grad_probs - delta)).astype(bf16).astype(f32)
    spread = (probs.astype(bf16).astype(f32) * count).astype(bf16)
    return (slopes * count).astype(bf16), spread


def backward_kernel(
    head,
    query,
    padded,
    grad,
    stats,
    counts,
    rim_query,
    rim_counts,
    grad_low,
    info_low,
    grad_high,
    info_high,
    grad_query,
    grad_key,
    grad_value,
    keys_total,
    values_total,
):
    row_count = query.shape[1]
    keys_total[...] = jnp.zeros_like(keys_total)
    values_total[...] = jnp.zeros_like(values_total)

    def step(b, carry):
        rows = rows_of(b * BLOCK, BLOCK)
        span = pl.ds(pl.multiple_of(b * BLOCK, BLOCK), SPAN)
        slopes, spread = attention_terms(
            query[0, rows, :],
            padded[0, span, :],
            padded[1, span, :],
            grad[rows, :],
            counts[rows, :].astype(f32),
            stats[rows, head : head + 1],
            stats[rows, HEADS + head : HEADS + head + 1],
        )
        grad_query[rows, :] = (nn(slopes, padded[0, span, :]) * score_scale).astype(bf16)
        keys_total[span, :] += tn(slopes, query[0, rows, :])
        values_total[span, :] += tn(spread, grad[rows, :])
        return carry

    lax.fori_loop(0, row_count // BLOCK, step, 0)
    for side, (grads, info) in enumerate(((grad_low, info_low), (grad_high, info_high))):
        first = HALO if side == 0 else HALO + row_count - RIM
        span = slice(first, first + RIM)
        rows = slice(side * HALO, (side + 1) * HALO)
        known = info[...].astype(f32)
        log_total = known[:, head : head + 1] + known[:, 2 * HEADS + head : 2 * HEADS + head + 1]
        delta = known[:, HEADS + head : HEADS + head + 1] + known[:, 3 * HEADS + head : 3 * HEADS + head + 1]
        slopes, spread = attention_terms(
            rim_query[rows, :],
            padded[0, span, :],
            padded[1, span, :],
            grads[...],
            rim_counts[rows, :].astype(f32),
            log_total,
            delta,
        )
        keys_total[span, :] += tn(slopes, rim_query[rows, :])
        values_total[span, :] += tn(spread, grads[...])
    own = slice(HALO, HALO + row_count)
    grad_key[...] = (keys_total[own, :] * score_scale).astype(bf16)
    grad_value[...] = values_total[own, :].astype(bf16)


def weights_kernel(*refs):
    scalars = refs[0]
    pieces = refs[1 : 1 + 3 * HEADS]
    (first_in, attended, grad_stream, features, pack, mod, weights, table_two, features_grad, blocks, gathered, table) = refs[
        1 + 3 * HEADS :
    ]
    row_count = first_in.shape[0]
    for p in range(3):
        for h in range(HEADS):
            gathered[p, :, h * HD : (h + 1) * HD] = pieces[p * HEADS + h][...]
    table[...] = table_two[...]

    def step(b, carry):
        rows = rows_of(b * 256, 256)
        level = pack[rows, K : K + 1]
        gradient = nt(gathered[0, rows, :], weights[0])
        for p in range(1, 3):
            gradient = gradient + nt(gathered[p, rows, :], weights[p])
        grad_field, scale_term = norm_back(gradient, features[rows, :].astype(f32), level, mod, 0)
        add_table(table, 0, level, scale_term, gradient)
        total = grad_stream[rows, :]
        features_grad[rows, :] = total + grad_field
        gathered[3, rows, :] = total.astype(bf16)
        return carry

    lax.fori_loop(0, row_count // 256, step, 0)
    core, slot_bit, z1, z2, hid = (scalars[i] for i in range(5))
    for p in range(4):
        left = first_in if p < 3 else attended
        product = tn(left[...], gathered[p])
        target, slot = p // 2, p % 2
        for half in range(2):
            for q in range(4):
                index = block_index(target, 2, slot ^ slot_bit, half ^ hid, (q // 2) ^ z1, (q % 2) ^ z2)
                start = half * 256 + q * 64
                where_to = (target ^ core,) + tuple(index)
                blocks[where_to + (slice(0, 64),)] = product[start : start + 64].astype(bf16)
                if p == 0:
                    row = (q // 2) * 4 + 2 * half + q % 2
                    extra = jnp.broadcast_to(table[row : row + 1, :], (TABLE_ROWS, D))
                    blocks[where_to + (slice(64, 80),)] = extra.astype(bf16)
                else:
                    blocks[where_to + (slice(64, 80),)] = jnp.zeros((TABLE_ROWS, D), bf16)


def block_index(target, phase, slot, hid, row_half, row_quarter):
    if phase == 1:
        return (slot, hid, row_half, row_quarter) if target == 0 else (row_half, slot, hid, row_quarter)
    return (hid, slot, row_half, row_quarter) if target == 0 else (slot, row_half, hid, row_quarter)


def newton_schulz(read, write, scratch, parts, rows_first, scale):
    squared = scale * scale
    grams = []
    for half in range(2):
        total = None
        for part in parts[half]:
            block = read(part)
            term = tn(block, block) if rows_first else nt(block, block)
            total = term if total is None else total + term
        grams.append((total * squared).astype(bf16))
    gram = (grams[0].astype(f32) + grams[1].astype(f32)).astype(bf16)
    scratch[...] = (ns_second * gram.astype(f32) + ns_third * nn(gram, gram)).astype(bf16)
    for half in range(2):
        for part in parts[half]:
            block = read(part)
            other = nn(block, scratch[...]) if rows_first else nn(scratch[...], block)
            write(part, ((ns_first * block.astype(f32) + other) * scale).astype(bf16))


def large_kernel(scalars, kept, got, result, blend, work, poly):
    core, slot_bit, z1, z2 = (scalars[i] for i in range(4))
    total = jnp.zeros((8, D), f32)
    for n in range(16):
        b1, b2, b3, b4 = n // 8, (n // 4) % 2, (n // 2) % 2, n % 2
        source = kept if b1 == 0 else got
        block = source[b2, b3, b4]
        value = block.astype(f32)
        total = total + jnp.sum((value * value).reshape(16, 8, D), axis=0)
        slot = jnp.where(core == 0, b1, b2)
        half = jnp.where(core == 0, b2, b3)
        row_half = jnp.where(core == 0, b3, b1)
        start = ((row_half ^ z1) * 2 + (b4 ^ z2)) * 128
        work[half * 2 + (slot ^ slot_bit), rows_of(start, 128), :] = block
    scale = 1.0 / (jnp.sqrt(jnp.sum(total)) + 1e-07)
    for s in range(2):
        blend[s] = work[s]

    def write(part, value):
        work[part] = value

    def step(i, factor):
        newton_schulz(lambda part: work[part], write, poly, ((0, 1), (2, 3)), False, factor)
        return jnp.ones((), f32)

    lax.fori_loop(0, NS_STEPS, step, scale)
    for s in range(2):
        result[s] = work[s]


def small_kernel(scalars, kept, got, result, work, poly):
    core, slot_bit, z1, z2 = (scalars[i] for i in range(4))
    totals = [jnp.zeros((8, D), f32), jnp.zeros((8, D), f32)]
    for n in range(16):
        b1, b2, b3, b4 = n // 8, (n // 4) % 2, (n // 2) % 2, n % 2
        source = kept if b1 == 0 else got
        block = source[b2, b3, b4]
        rows = block[:64]
        slot = jnp.where(core == 0, b2, b1) ^ slot_bit
        half = jnp.where(core == 0, b1, b3)
        row_half = jnp.where(core == 0, b3, b2)
        quarter = (row_half ^ z1) * 2 + (b4 ^ z2)
        work[slot, half, rows_of(quarter * 64, 64), :] = rows

        @pl.when((half == 0) & (slot == 0))
        def _():
            result[4, rows_of(quarter * TABLE_ROWS, TABLE_ROWS), :] = block[64:]

    result[4, 64:, :] = jnp.zeros((192, D), bf16)
    for s in range(2):
        total = jnp.zeros((8, D), f32)
        for half in range(2):
            value = work[s, half].astype(f32)
            total = total + jnp.sum((value * value).reshape(32, 8, D), axis=0)
        scale = 1.0 / (jnp.sqrt(jnp.sum(total)) + 1e-07)
        result[2 + s] = work[s, 0]

        def write(part, value):
            work[s, part] = value

        def step(i, factor):
            newton_schulz(lambda part: work[s, part], write, poly, ((0,), (1,)), True, factor)
            return jnp.ones((), f32)

        lax.fori_loop(0, NS_STEPS, step, scale)
        result[s] = work[s, 0]


def new_moment(blend, moment):
    share = 1.0 / (1.0 + momentum_rate)
    return share * blend + (momentum_rate - share * momentum_rate * momentum_rate) * moment


def new_weight(weight, ortho, longest):
    return weight - muon_rate * (0.2 * math.sqrt(longest) * ortho + decay_rate * weight)


def large_out_kernel(
    scalars, own, got, up_weight, up_moment, down_weight, down_moment, up_moment_new, up_new, down_moment_new, down_new
):
    first = scalars[0] == 0
    ups = [jnp.where(first, own[i, 0].astype(f32), got[i, 0].astype(f32)) for i in range(2)]
    downs = [jnp.where(first, got[i, 0].astype(f32), own[i, 0].astype(f32)) for i in range(2)]
    up_new[...] = new_weight(up_weight[...], ups[0], FF)
    up_moment_new[...] = new_moment(ups[1], up_moment[...])
    down_new[...] = new_weight(down_weight[...], downs[0].T, FF)
    down_moment_new[...] = new_moment(downs[1].T, down_moment[...])


def small_out_kernel(scalars, own, got, weight, moment, moment_new, weight_new):
    mine = scalars[0] == pl.program_id(0) // 2
    ortho = jnp.where(mine, own[0, 0].astype(f32), got[0, 0].astype(f32))
    blend = jnp.where(mine, own[1, 0].astype(f32), got[1, 0].astype(f32))
    weight_new[0] = new_weight(weight[0], ortho, D)
    moment_new[0] = new_moment(blend, moment[0])


def on_device(
    features,
    levels,
    neighbour_index,
    neighbour_count,
    cotangent,
    attention_weight,
    up_weight,
    down_weight,
    modulation,
    attention_moment,
    up_moment,
    down_moment,
    modulation_moment,
):
    row_count = features.shape[0]
    device_count = lax.axis_size(AXES)
    me = lax.axis_index(AXES)
    first_row = me * row_count

    def bit(mask):
        return (me // mask) % 2

    hid, core, slot_bit, z1, z2 = bit(1), bit(2), bit(4), bit(8), bit(16)
    scalars = jnp.stack([core, slot_bit, z1, z2, hid]).astype(jnp.int32)
    is_first = core == 0

    def along(value, distance):
        pairs = [(i, i + distance) for i in range(device_count) if 0 <= i + distance < device_count]
        return lax.ppermute(value, AXES, pairs)

    def swap(value, mask, other=None):
        masks = (mask, mask if other is None else other)
        pairs = [(i, i ^ masks[(i // 2) % 2]) for i in range(device_count)]
        return lax.ppermute(value, AXES, pairs)

    live = jnp.arange(K, dtype=jnp.int32)[None, :] < neighbour_count[:, None]
    row_ids = first_row + jnp.arange(row_count, dtype=jnp.int32)[:, None]
    offsets = jnp.where(live, neighbour_index - row_ids, 512)
    pack = jnp.concatenate(
        [offsets, levels[:, None], jnp.zeros((row_count, 128 - K - 1), jnp.int32)], axis=1
    ).astype(f32)
    rims = jnp.concatenate([features, pack.astype(bf16)], axis=1)
    rim_low = along(rims[row_count - HALO :], 1)
    rim_high = along(rims[:HALO], -1)
    quarter = jnp.stack(
        [
            lax.dynamic_slice(up_weight, (0, core * CHUNK), (D, CHUNK)),
            lax.dynamic_slice(down_weight, (core * CHUNK, 0), (CHUNK, D)),
        ]
    ).astype(bf16)
    near = swap(quarter, 1)
    far = swap(near, 2)

    attn_bf = attention_weight.astype(bf16)
    mod = modulation.reshape(8, D)
    first_in, qkv, counts = pl.pallas_call(
        project_kernel,
        out_shape=(
            struct((row_count, D), bf16),
            struct((3, row_count, D), bf16),
            struct((row_count, SPAN), bf16),
        ),
        in_specs=[VMEM] * 4,
        out_specs=(VMEM,) * 3,
        cost_estimate=cost(4e9, 4e6),
        name="project",
    )(features, pack, mod, attn_bf)

    attended, stream, second_in, padded, rim_queries, rim_counts, log_totals = pl.pallas_call(
        forward_kernel,
        out_shape=(
            struct((row_count, D), bf16),
            struct((row_count, D), f32),
            struct((row_count, D), bf16),
            struct((2, row_count + 2 * HALO, D), bf16),
            struct((2 * HALO, D), bf16),
            struct((2 * HALO, RIM), bf16),
            struct((row_count, 128), f32),
        ),
        in_specs=[VMEM] * 8,
        out_specs=(VMEM,) * 7,
        scratch_shapes=[pltpu.VMEM((2 * HALO, D), bf16)],
        cost_estimate=cost(6e9, 8e6),
        name="attend",
    )(rim_low, rim_high, features, pack, mod, attn_bf, qkv, counts)

    def whole(*shape):
        return pl.BlockSpec(shape, lambda g, s: (0,) * len(shape))

    chunk_shape = struct((2, 2, 2, 128, CHUNK), bf16)
    branch, grad_second, own_up, own_down = pl.pallas_call(
        mlp_own_kernel,
        out_shape=(struct((row_count, D), f32), struct((row_count, D), f32), chunk_shape, chunk_shape),
        grid_spec=pltpu.PrefetchScalarGridSpec(
            num_scalar_prefetch=1,
            grid=(2,),
            in_specs=[
                whole(row_count, D),
                whole(row_count, D),
                pl.BlockSpec((D, CHUNK), lambda g, s: (0, g)),
                pl.BlockSpec((CHUNK, D), lambda g, s: (g, 0)),
            ],
            out_specs=(
                whole(row_count, D),
                whole(row_count, D),
                pl.BlockSpec((1, 2, 2, 128, CHUNK), lambda g, s: (g ^ s[1], 0, 0, 0, 0)),
                pl.BlockSpec((1, 2, 2, 128, CHUNK), lambda g, s: (g ^ s[1], 0, 0, 0, 0)),
            ),
            scratch_shapes=[pltpu.VMEM((row_count, CHUNK), bf16)] * 2,
        ),
        cost_estimate=cost(5e9, 8e6),
        name="mlp_own",
    )(scalars, second_in, cotangent, up_weight, down_weight)

    (
        rest_up,
        rest_down,
        output,
        grad_stream,
        grad_attended,
        stats,
        edge_low,
        edge_high,
        table_two,
    ) = pl.pallas_call(
        mlp_rest_kernel,
        out_shape=(
            chunk_shape,
            chunk_shape,
            struct((row_count, D), bf16),
            struct((row_count, D), f32),
            struct((row_count, D), bf16),
            struct((row_count, 128), f32),
            struct((HALO, D + 128), bf16),
            struct((HALO, D + 128), bf16),
            struct((8, D), f32),
        ),
        grid_spec=pltpu.PrefetchScalarGridSpec(
            num_scalar_prefetch=1,
            grid=(2,),
            in_specs=[
                whole(row_count, D),
                whole(row_count, D),
                whole(2, D, CHUNK),
                whole(2, D, CHUNK),
                whole(row_count, D),
                whole(row_count, D),
                whole(row_count, D),
                whole(row_count, 128),
                whole(8, D),
                whole(4, D, D),
                whole(row_count, D),
                whole(row_count, 128),
            ],
            out_specs=(
                pl.BlockSpec((1, 2, 2, 128, CHUNK), lambda g, s: (g ^ s[0] ^ s[1], 0, 0, 0, 0)),
                pl.BlockSpec((1, 2, 2, 128, CHUNK), lambda g, s: (g ^ s[0] ^ s[1], 0, 0, 0, 0)),
                whole(row_count, D),
                whole(row_count, D),
                whole(row_count, D),
                whole(row_count, 128),
                whole(HALO, D + 128),
                whole(HALO, D + 128),
                whole(8, D),
            ),
            scratch_shapes=[
                pltpu.VMEM((row_count, D), f32),
                pltpu.VMEM((row_count, D), f32),
                pltpu.VMEM((row_count, CHUNK), bf16),
                pltpu.VMEM((row_count, CHUNK), bf16),
            ],
        ),
        cost_estimate=cost(6e9, 12e6),
        name="mlp_rest",
    )(
        scalars,
        second_in,
        cotangent,
        near,
        far,
        branch,
        grad_second,
        stream,
        pack,
        mod,
        attn_bf,
        attended,
        log_totals,
    )

    grad_low = along(edge_high, 1)
    grad_high = along(edge_low, -1)

    def kept_of(first, second):
        return jnp.where(is_first, first, second)

    own_sum = kept_of(own_up, own_down).astype(f32) + swap(kept_of(own_down, own_up), 2).astype(f32)
    rest_sum = kept_of(rest_up, rest_down).astype(f32) + swap(kept_of(rest_down, rest_up), 2).astype(f32)

    def halved(first_send, first_keep, routes):
        keep, send = first_keep, first_send
        for number, route in enumerate(routes):
            keep = keep + swap(send.astype(bf16), *route).astype(f32)
            if number + 1 < len(routes):
                keep, send = keep[0], keep[1]
        mask = 32
        while mask < device_count:
            rounded = keep.astype(bf16)
            keep = rounded.astype(f32) + swap(rounded, mask).astype(f32)
            mask *= 2
        return keep

    def doubled(shard, routes):
        pieces = shard
        for route in routes[:0:-1]:
            pieces = jnp.stack([pieces, swap(pieces, *route)])
        return pieces, swap(pieces, *routes[0])

    blend_rate = 1.0 + momentum_rate
    past_rate = momentum_rate * momentum_rate
    large_routes = ((4, 8), (1, 4), (8, 1), (16, 16))
    large_keep = kept_of(
        jnp.stack([own_sum[0], rest_sum[0]]),
        jnp.stack([own_sum[:, 0], rest_sum[:, 0]], axis=1),
    )
    large_send = kept_of(
        jnp.stack([own_sum[1], rest_sum[1]]),
        jnp.stack([own_sum[:, 1], rest_sum[:, 1]], axis=1),
    )
    large_shard = halved(large_send, large_keep, large_routes)
    row_start = (z1 * 2 + z2) * 128
    large_past = kept_of(
        lax.dynamic_slice(up_moment, (row_start, slot_bit * CHUNK), (128, CHUNK)),
        lax.dynamic_slice(down_moment, (slot_bit * CHUNK, row_start), (CHUNK, 128)).T,
    )
    large_blend = (blend_rate * large_shard + past_rate * large_past).astype(bf16)
    large_kept, large_got = doubled(large_blend, large_routes)

    def column(h):
        return pl.BlockSpec((row_count, HD), lambda g: (0, h))

    pieces = []
    for h in range(HEADS):
        pieces.append(
            pl.pallas_call(
                functools.partial(backward_kernel, h),
                grid=(1,),
                out_shape=(struct((row_count, HD), bf16),) * 3,
                in_specs=[
                    pl.BlockSpec((1, row_count, HD), lambda g, h=h: (0, 0, h)),
                    pl.BlockSpec((2, row_count + 2 * HALO, HD), lambda g, h=h: (0, 0, h)),
                    pl.BlockSpec((row_count, HD), lambda g, h=h: (0, h)),
                    pl.BlockSpec((row_count, 128), lambda g: (0, 0)),
                    pl.BlockSpec((row_count, SPAN), lambda g: (0, 0)),
                    pl.BlockSpec((2 * HALO, HD), lambda g, h=h: (0, h)),
                    pl.BlockSpec((2 * HALO, RIM), lambda g: (0, 0)),
                    pl.BlockSpec((HALO, HD), lambda g, h=h: (0, h)),
                    pl.BlockSpec((HALO, 128), lambda g: (0, HEADS)),
                    pl.BlockSpec((HALO, HD), lambda g, h=h: (0, h)),
                    pl.BlockSpec((HALO, 128), lambda g: (0, HEADS)),
                ],
                out_specs=(pl.BlockSpec((row_count, HD), lambda g: (0, 0)),) * 3,
                scratch_shapes=[pltpu.VMEM((row_count + 2 * HALO, HD), f32)] * 2,
                cost_estimate=cost(1e9, 3e6),
                name="attend_back",
            )(
                qkv,
                padded,
                grad_attended,
                stats,
                counts,
                rim_queries,
                rim_counts,
                grad_low,
                grad_low,
                grad_high,
                grad_high,
            )
        )
    ordered = [pieces[h][p] for p in range(3) for h in range(HEADS)]
    features_grad, attn_blocks = pl.pallas_call(
        weights_kernel,
        out_shape=(struct((row_count, D), f32), struct((2, 2, 2, 2, 2, 80, D), bf16)),
        in_specs=[SMEM] + [VMEM] * (3 * HEADS + 8),
        out_specs=(VMEM, VMEM),
        scratch_shapes=[pltpu.VMEM((4, row_count, D), bf16), pltpu.VMEM((8, D), f32)],
        cost_estimate=cost(4e9, 9e6),
        name="attend_weights",
    )(
        scalars,
        *ordered,
        first_in,
        attended,
        grad_stream,
        features,
        pack,
        mod,
        attn_bf,
        table_two,
    )

    small_routes = ((1, 4), (4, 8), (8, 1), (16, 16))
    small_sum = attn_blocks[0].astype(f32) + swap(attn_blocks[1], 2).astype(f32)
    small_shard = halved(small_sum[1], small_sum[0], small_routes)
    small_past = lax.dynamic_slice(
        attention_moment, (core * 2 + slot_bit, (z1 * 2 + z2) * 64, 0), (1, 64, D)
    )[0]
    small_blend = jnp.concatenate(
        [
            (blend_rate * small_shard[:64] + past_rate * small_past).astype(bf16),
            small_shard[64:].astype(bf16),
        ]
    )
    small_kept, small_got = doubled(small_blend, small_routes)

    large_result, large_mix = pl.pallas_call(
        large_kernel,
        out_shape=(struct((2, D, CHUNK), bf16), struct((2, D, CHUNK), bf16)),
        in_specs=[SMEM, VMEM, VMEM],
        out_specs=(VMEM, VMEM),
        scratch_shapes=[pltpu.VMEM((4, D, CHUNK), bf16), pltpu.VMEM((D, D), bf16)],
        cost_estimate=cost(1e10, 6e6),
        name="ortho_large",
    )(scalars, large_kept, large_got)
    large_own = jnp.stack([large_result, large_mix])
    large_other = swap(large_own, 2)
    up_moment_new, up_new, down_moment_new, down_new = pl.pallas_call(
        large_out_kernel,
        grid=(2,),
        out_shape=(struct((D, 2 * CHUNK), f32),) * 2 + (struct((2 * CHUNK, D), f32),) * 2,
        in_specs=[
            SMEM,
            pl.BlockSpec((2, 1, D, CHUNK), lambda g: (0, g, 0, 0)),
            pl.BlockSpec((2, 1, D, CHUNK), lambda g: (0, g, 0, 0)),
            pl.BlockSpec((D, CHUNK), lambda g: (0, g)),
            pl.BlockSpec((D, CHUNK), lambda g: (0, g)),
            pl.BlockSpec((CHUNK, D), lambda g: (g, 0)),
            pl.BlockSpec((CHUNK, D), lambda g: (g, 0)),
        ],
        out_specs=(
            pl.BlockSpec((D, CHUNK), lambda g: (0, g)),
            pl.BlockSpec((D, CHUNK), lambda g: (0, g)),
            pl.BlockSpec((CHUNK, D), lambda g: (g, 0)),
            pl.BlockSpec((CHUNK, D), lambda g: (g, 0)),
        ),
        cost_estimate=cost(1e7, 2e7),
        name="update_large",
    )(scalars, large_own, large_other, up_weight, up_moment, down_weight, down_moment)

    small_own = pl.pallas_call(
        small_kernel,
        out_shape=struct((5, 256, D), bf16),
        in_specs=[SMEM, VMEM, VMEM],
        out_specs=VMEM,
        scratch_shapes=[pltpu.VMEM((2, 2, 256, D), bf16), pltpu.VMEM((D, D), bf16)],
        cost_estimate=cost(6e9, 4e6),
        name="ortho_small",
    )(scalars, small_kept, small_got)
    small_other = swap(small_own, 2)

    def pair(g, s):
        return (0, g % 2, 0, 0)

    def per_matrix(index):
        return pl.BlockSpec((1, 256, D), index)

    attention_moment_new, attention_new = pl.pallas_call(
        small_out_kernel,
        grid_spec=pltpu.PrefetchScalarGridSpec(
            num_scalar_prefetch=1,
            grid=(4,),
            in_specs=[
                pl.BlockSpec((2, 1, 256, D), pair),
                pl.BlockSpec((2, 1, 256, D), pair),
                per_matrix(lambda g, s: (g, s[4], 0)),
                per_matrix(lambda g, s: (g, 0, 0)),
            ],
            out_specs=(per_matrix(lambda g, s: (g, 0, 0)),) * 2,
        ),
        out_shape=(struct((4, 256, D), f32),) * 2,
        cost_estimate=cost(1e7, 1e7),
        name="update_small",
    )(
        scalars,
        small_own[:4].reshape(2, 2, 256, D),
        small_other[:4].reshape(2, 2, 256, D),
        attention_weight,
        attention_moment,
    )
    table_sum = kept_of(small_own[4], small_other[4])[: 4 * TABLE_ROWS : TABLE_ROWS].astype(f32)
    modulation_moment_new = vector_rate * modulation_moment + table_sum.reshape(2, 2, D)
    table_own = lax.dynamic_slice_in_dim(modulation, hid * 2, 2, 1)
    node_total = row_count * device_count
    modulation_new = table_own - 0.2 / math.sqrt(node_total) * modulation_moment_new
    return (
        output,
        features_grad,
        attention_moment_new,
        attention_new,
        up_moment_new,
        up_new,
        down_moment_new,
        down_new,
        modulation_moment_new,
        modulation_new,
    )


def solution(mesh):
    placed = (
        P(("nodes", "hid"), None),
        P(("nodes", "hid")),
        P(("nodes", "hid"), None),
        P(("nodes", "hid")),
        P(("nodes", "hid"), None),
        P(),
        P(None, "hid"),
        P("hid", None),
        P(),
        P(None, "hid", None),
        P(None, "hid"),
        P("hid", None),
        P(None, "hid", None),
    )
    return jax.shard_map(
        on_device,
        mesh=mesh,
        in_specs=placed,
        out_specs=(
            P(("nodes", "hid"), None),
            P(("nodes", "hid"), None),
            P(None, "hid", None),
            P(None, "hid", None),
            P(None, "hid"),
            P(None, "hid"),
            P("hid", None),
            P("hid", None),
            P(None, "hid", None),
            P(None, "hid", None),
        ),
        check_vma=False,
    )
```

```python
import functools
import math

import jax
import jax.numpy as jnp
from jax import lax
from jax.experimental import pallas as pl
from jax.experimental.pallas import tpu as pltpu
from jax.sharding import PartitionSpec as P

D = 512
HEADS = 4
HD = 128
FF = 2048
K = 16
NS_STEPS = 4
HALO = 192
BLOCK = 128
SPAN = BLOCK + 2 * HALO
RIM = 256
CHUNK = 512
TABLE_ROWS = 16

f32 = jnp.float32
bf16 = jnp.bfloat16
ns_first = 3.4445
ns_second = -4.775
ns_third = 2.0315
momentum_rate = 0.95
vector_rate = 0.9
muon_rate = 0.2
decay_rate = 0.1
score_scale = 1.0 / math.sqrt(HD)
AXES = ("nodes", "hid")
VMEM = pl.BlockSpec(memory_space=pltpu.VMEM)
SMEM = pl.BlockSpec(memory_space=pltpu.SMEM)


def nn(a, b):
    return lax.dot_general(a, b, (((1,), (0,)), ((), ())), preferred_element_type=f32)


def nt(a, b):
    return lax.dot_general(a, b, (((1,), (1,)), ((), ())), preferred_element_type=f32)


def tn(a, b):
    return lax.dot_general(a, b, (((0,), (0,)), ((), ())), preferred_element_type=f32)


def struct(shape, dtype):
    return jax.ShapeDtypeStruct(shape, dtype)


def rows_of(start, size):
    return pl.ds(pl.multiple_of(start, size), size)


def cost(flops, data):
    return pl.CostEstimate(flops=int(flops), bytes_accessed=int(data), transcendentals=0)


def room(mebibytes):
    return pltpu.CompilerParams(vmem_limit_bytes=mebibytes << 20)


def norm_parts(field):
    average = jnp.mean(field, axis=-1, keepdims=True)
    centred = field - average
    variance = jnp.mean(centred * centred, axis=-1, keepdims=True)
    inverse = lax.rsqrt(variance + 1e-06)
    return centred * inverse, inverse


def table_rows(mod_ref, level, column):
    return jnp.where(level > 0.5, mod_ref[4 + column : 5 + column, :], mod_ref[column : column + 1, :])


def modulated(field, level, mod_ref, column):
    normed, _ = norm_parts(field)
    return normed * (1.0 + table_rows(mod_ref, level, column)) + table_rows(
        mod_ref, level, column + 1
    )


def norm_back(grad_out, field, level, mod_ref, column):
    normed, inverse = norm_parts(field)
    grad_norm = grad_out * (1.0 + table_rows(mod_ref, level, column))
    grad_in = inverse * (
        grad_norm
        - jnp.mean(grad_norm, axis=-1, keepdims=True)
        - normed * jnp.mean(grad_norm * normed, axis=-1, keepdims=True)
    )
    return grad_in, grad_out * normed


def add_table(table_ref, column, level, scale_term, shift_term):
    upper = level > 0.5
    for term, place in ((scale_term, column), (shift_term, column + 1)):
        low_part = jnp.sum(jnp.where(upper, 0.0, term), axis=0, keepdims=True)
        high_part = jnp.sum(jnp.where(upper, term, 0.0), axis=0, keepdims=True)
        table_ref[place : place + 1, :] += low_part
        table_ref[4 + place : 5 + place, :] += high_part


def slot_counts(pack, row_count, width, shift):
    pieces = []
    for left in range(0, width, 128):
        lanes = lax.broadcasted_iota(jnp.int32, (row_count, 128), 1)
        rows = lax.broadcasted_iota(jnp.int32, (row_count, 128), 0)
        place = (lanes - rows + (left - shift)).astype(f32)
        total = jnp.zeros((row_count, 128), f32)
        for slot in range(K):
            total = total + jnp.where(place == pack[:, slot : slot + 1], 1.0, 0.0)
        pieces.append(total)
    return jnp.concatenate(pieces, axis=1).astype(bf16)


def project_kernel(features, pack, mod, weights, first_in, qkv, counts, rounded):
    row_count = features.shape[0]
    turn = pl.program_id(0)

    @pl.when(turn == 0)
    def _():
        for start in range(0, row_count, 256):
            rows = slice(start, start + 256)
            level = pack[rows, K : K + 1]
            first_in[rows, :] = modulated(features[rows, :].astype(f32), level, mod, 0).astype(bf16)

    weight = weights[0].astype(bf16)
    rounded[0] = weight

    @pl.when(turn < 3)
    def _():
        qkv[turn] = nn(first_in[...], weight).astype(bf16)
        share = row_count // BLOCK // 3

        def count_step(b, carry):
            rows = rows_of(b * BLOCK, BLOCK)
            counts[rows, :] = slot_counts(pack[rows, :], BLOCK, SPAN, HALO)
            return carry

        lax.fori_loop(turn * share, (turn + 1) * share, count_step, 0)


def forward_kernel(
    rim_low,
    rim_high,
    features,
    pack,
    mod,
    weights,
    qkv,
    counts,
    attended,
    stream,
    second_in,
    padded,
    rim_queries,
    rim_counts,
    log_totals,
    rim_in,
):
    row_count = features.shape[0]
    for side, rim in enumerate((rim_low, rim_high)):
        for start in range(0, HALO, 64):
            rows = slice(start, start + 64)
            info = rim[rows, D:].astype(f32)
            rim_in[side * HALO + start : side * HALO + start + 64, :] = modulated(
                rim[rows, :D].astype(f32), info[:, K : K + 1], mod, 0
            ).astype(bf16)
            rim_counts[side * HALO + start : side * HALO + start + 64, :] = slot_counts(
                info, 64, RIM, start + (-HALO if side == 0 else RIM)
            )
    rim_queries[...] = nn(rim_in[...], weights[0]).astype(bf16)
    for p in range(2):
        piece = nn(rim_in[...], weights[1 + p]).astype(bf16)
        padded[p, :HALO, :] = piece[:HALO]
        padded[p, HALO + row_count :, :] = piece[HALO:]
        padded[p, HALO : HALO + row_count, :] = qkv[1 + p]

    def step(b, carry):
        rows = rows_of(b * BLOCK, BLOCK)
        span = pl.ds(pl.multiple_of(b * BLOCK, BLOCK), SPAN)
        count = counts[rows, :].astype(f32)
        live = count > 0.0
        columns = [slice(h * HD, (h + 1) * HD) for h in range(HEADS)]
        scores = [nt(qkv[0, rows, cols], padded[0, span, cols]) * score_scale for cols in columns]
        lanes = lax.broadcasted_iota(jnp.int32, (BLOCK, 128), 1)
        stats = jnp.zeros((BLOCK, 128), f32)
        for h, cols in enumerate(columns):
            masked = jnp.where(live, scores[h], -1e30)
            peak = jnp.max(masked, axis=-1, keepdims=True)
            exponent = jnp.exp(masked - peak)
            total = jnp.sum(exponent * count, axis=-1, keepdims=True)
            probs = (exponent / total).astype(bf16)
            spread = (probs.astype(f32) * count).astype(bf16)
            attended[rows, cols] = nn(spread, padded[1, span, cols]).astype(bf16)
            stats = jnp.where(lanes == h, peak + jnp.log(total), stats)
        log_totals[rows, :] = stats
        return carry

    lax.fori_loop(0, row_count // BLOCK, step, 0)
    for start in range(0, row_count, 256):
        rows = slice(start, start + 256)
        field = features[rows, :].astype(f32) + nn(attended[rows, :], weights[3])
        stream[rows, :] = field
        second_in[rows, :] = modulated(field, pack[rows, K : K + 1], mod, 2).astype(bf16)


def mlp_chunk(scalars, second_in, cotangent, up, down, branch, grad_second, acts, grads, kept, sent):
    row_count = second_in.shape[0]
    for start in range(0, row_count, 256):
        rows = slice(start, start + 256)
        preact = nn(second_in[rows, :], up)
        grad_act = nt(cotangent[rows, :], down)
        sigmoid = 0.5 * jnp.tanh(0.5 * preact) + 0.5
        act = (preact * sigmoid).astype(bf16)
        acts[rows, :] = act
        grad_pre = (grad_act * (sigmoid * (1.0 + preact * (1.0 - sigmoid)))).astype(bf16)
        grads[rows, :] = grad_pre
        branch[rows, :] += nn(act, down)
        grad_second[rows, :] += nt(grad_pre, up)
    core, z1, z2 = scalars[0], scalars[2], scalars[3]
    for target in range(2):

        @pl.when(core == target)
        def _():
            outs = (kept, sent) if target == 0 else (sent, kept)
            for left, right, out in ((second_in, grads, outs[0]), (cotangent, acts, outs[1])):
                product = tn(left[...], right[...])
                for q in range(4):
                    out[0, (q // 2) ^ z1, (q % 2) ^ z2] = product[q * 128 : (q + 1) * 128].astype(bf16)


def mlp_own_kernel(
    scalars, second_in, cotangent, up, down, branch, grad_second, kept, sent, acts, grads
):
    @pl.when(pl.program_id(0) == 0)
    def _():
        branch[...] = jnp.zeros_like(branch)
        grad_second[...] = jnp.zeros_like(grad_second)

    mlp_chunk(
        scalars,
        second_in,
        cotangent,
        up[...].astype(bf16),
        down[...].astype(bf16),
        branch,
        grad_second,
        acts,
        grads,
        kept,
        sent,
    )


def mlp_rest_kernel(
    scalars,
    second_in,
    cotangent,
    near,
    far,
    branch_in,
    grad_in,
    stream,
    pack,
    mod,
    weights,
    attended,
    log_totals,
    kept,
    sent,
    output,
    grad_stream,
    grad_attended,
    stats,
    edge_low,
    edge_high,
    table,
    branch,
    grad_second,
    acts,
    grads,
):
    row_count = second_in.shape[0]
    turn = pl.program_id(0)

    @pl.when(turn == 0)
    def _():
        branch[...] = branch_in[...]
        grad_second[...] = grad_in[...]
        mlp_chunk(
            scalars, second_in, cotangent, near[0], near[1], branch, grad_second, acts, grads, kept, sent
        )

    @pl.when(turn == 1)
    def _():
        mlp_chunk(
            scalars, second_in, cotangent, far[0], far[1], branch, grad_second, acts, grads, kept, sent
        )
        table[...] = jnp.zeros_like(table)

        for start in range(0, row_count, 256):
            rows = slice(start, start + 256)
            field = stream[rows, :]
            level = pack[rows, K : K + 1]
            output[rows, :] = (field + branch[rows, :]).astype(bf16)
            gradient = grad_second[rows, :]
            grad_field, scale_term = norm_back(gradient, field, level, mod, 2)
            add_table(table, 2, level, scale_term, gradient)
            total = cotangent[rows, :].astype(f32) + grad_field
            grad_stream[rows, :] = total
            back = nt(total.astype(bf16), weights[3]).astype(bf16)
            grad_attended[rows, :] = back
            product = back.astype(f32) * attended[rows, :].astype(f32)
            lanes = lax.broadcasted_iota(jnp.int32, (256, 128), 1)
            kept_stats = log_totals[rows, :]
            for h in range(HEADS):
                delta = jnp.sum(product[:, h * HD : (h + 1) * HD], axis=-1, keepdims=True)
                kept_stats = jnp.where(lanes == HEADS + h, delta, kept_stats)
            stats[rows, :] = kept_stats
        for edge, first in ((edge_low, 0), (edge_high, row_count - HALO)):
            rows = slice(first, first + HALO)
            edge[:, :D] = grad_attended[rows, :]
            known = stats[rows, :]
            upper = known.astype(bf16)
            lower = (known - upper.astype(f32)).astype(bf16).astype(f32)
            edge[:, D:] = (upper.astype(f32) + pltpu.roll(lower, 2 * HEADS, 1)).astype(bf16)


def attention_terms(scores, grad_probs, count, log_total, delta):
    probs = jnp.exp(jnp.where(count > 0.0, scores * score_scale, -1e30) - log_total)
    slopes = (probs * (grad_probs - delta)).astype(bf16).astype(f32)
    spread = (probs.astype(bf16).astype(f32) * count).astype(bf16)
    return (slopes * count).astype(bf16), spread


def backward_kernel(first, last, *refs):
    if first == 0:
        qkv, padded, grad, stats, counts, grad_query, keys_total, values_total = refs
        keys_total[...] = jnp.zeros_like(keys_total)
        values_total[...] = jnp.zeros_like(values_total)
    else:
        qkv, padded, grad, stats, counts, _, _, grad_query, keys_total, values_total = refs

    def step(b, carry):
        rows = rows_of(b * BLOCK, BLOCK)
        span = pl.ds(pl.multiple_of(b * BLOCK, BLOCK), SPAN)
        count = counts[rows, :].astype(f32)
        columns = [slice(h * HD, (h + 1) * HD) for h in range(HEADS)]
        products = [
            (nt(qkv[0, rows, cols], padded[0, span, cols]), nt(grad[rows, cols], padded[1, span, cols]))
            for cols in columns
        ]
        terms = [
            attention_terms(
                *products[h],
                count,
                stats[rows, h : h + 1],
                stats[rows, HEADS + h : HEADS + h + 1],
            )
            for h in range(HEADS)
        ]
        target = rows_of((b - first) * BLOCK, BLOCK)
        for (slopes, spread), cols in zip(terms, columns):
            grad_query[target, cols] = (nn(slopes, padded[0, span, cols]) * score_scale).astype(bf16)
            keys_total[span, cols] += tn(slopes, qkv[0, rows, cols])
            values_total[span, cols] += tn(spread, grad[rows, cols])
        return carry

    lax.fori_loop(first, last, step, 0)


def weights_kernel(
    scalars,
    early,
    late,
    keys_in,
    values_in,
    padded,
    rim_query,
    rim_counts,
    grad_low,
    grad_high,
    first_in,
    attended,
    grad_stream,
    features,
    pack,
    mod,
    weights,
    table_two,
    features_grad,
    kept,
    sent,
    gathered,
    table,
    keys_total,
    values_total,
):
    row_count = first_in.shape[0]
    columns = [slice(h * HD, (h + 1) * HD) for h in range(HEADS)]
    own = slice(HALO, HALO + row_count)
    keys_total[...] = keys_in[own, :]
    values_total[...] = values_in[own, :]
    for side, grads in enumerate((grad_low, grad_high)):
        first = 0 if side == 0 else row_count - RIM
        own_span = slice(first, first + RIM)
        span = slice(HALO + first, HALO + first + RIM)
        rows = slice(side * HALO, (side + 1) * HALO)
        known = grads[:, D:].astype(f32)
        count = rim_counts[rows, :].astype(f32)
        products = [
            (nt(rim_query[rows, cols], padded[0, span, cols]), nt(grads[:, cols], padded[1, span, cols]))
            for cols in columns
        ]
        terms = []
        for h in range(HEADS):
            numbers = [known[:, i * HEADS + h : i * HEADS + h + 1] for i in range(4)]
            terms.append(
                attention_terms(*products[h], count, numbers[0] + numbers[2], numbers[1] + numbers[3])
            )
        for (slopes, spread), cols in zip(terms, columns):
            keys_total[own_span, cols] += tn(slopes, rim_query[rows, cols])
            values_total[own_span, cols] += tn(spread, grads[:, cols])
    half_rows = row_count // 2
    gathered[0, :half_rows, :] = early[...]
    gathered[0, half_rows:, :] = late[...]
    gathered[1] = (keys_total[...] * score_scale).astype(bf16)
    gathered[2] = values_total[...].astype(bf16)
    table[...] = table_two[...]
    for start in range(0, row_count, 256):
        rows = slice(start, start + 256)
        level = pack[rows, K : K + 1]
        gradient = nt(gathered[0, rows, :], weights[0])
        for p in range(1, 3):
            gradient = gradient + nt(gathered[p, rows, :], weights[p])
        grad_field, scale_term = norm_back(gradient, features[rows, :].astype(f32), level, mod, 0)
        add_table(table, 0, level, scale_term, gradient)
        total = grad_stream[rows, :]
        features_grad[rows, :] = total + grad_field
        gathered[3, rows, :] = total.astype(bf16)
    core, slot_bit, z1, z2, hid = (scalars[i] for i in range(5))
    for mine in range(2):

        @pl.when(core == mine)
        def _():
            for p in range(4):
                left = first_in if p < 3 else attended
                product = tn(left[...], gathered[p])
                target, slot = p // 2, p % 2
                out = kept if target == mine else sent
                for half in range(2):
                    for q in range(4):
                        index = block_index(
                            target, 2, slot ^ slot_bit, half ^ hid, (q // 2) ^ z1, (q % 2) ^ z2
                        )
                        start = half * 256 + q * 64
                        out[tuple(index) + (slice(0, 64),)] = product[start : start + 64].astype(bf16)
                        if p == 0:
                            row = (q // 2) * 4 + 2 * half + q % 2
                            extra = jnp.broadcast_to(table[row : row + 1, :], (TABLE_ROWS, D))
                            out[tuple(index) + (slice(64, 80),)] = extra.astype(bf16)
                        else:
                            out[tuple(index) + (slice(64, 80),)] = jnp.zeros((TABLE_ROWS, D), bf16)


def block_index(target, phase, slot, hid, row_half, row_quarter):
    if phase == 1:
        return (slot, hid, row_half, row_quarter) if target == 0 else (row_half, slot, hid, row_quarter)
    return (hid, slot, row_half, row_quarter) if target == 0 else (slot, row_half, hid, row_quarter)


def newton_schulz(groups, polys, rows_first, scales):
    blocks = [[[ref[i] for i in half] for half in halves] for ref, halves in groups]
    grams = []
    for halves, scale in zip(blocks, scales):
        sums = []
        for half in halves:
            total = None
            for block in half:
                term = tn(block, block) if rows_first else nt(block, block)
                total = term if total is None else total + term
            sums.append((total if scale is None else total * (scale * scale)).astype(bf16))
        grams.append((sums[0].astype(f32) + sums[1].astype(f32)).astype(bf16))
    for gram, poly in zip(grams, polys):
        poly[...] = (ns_second * gram.astype(f32) + ns_third * nn(gram, gram)).astype(bf16)
    for (ref, halves), values, poly, scale in zip(groups, blocks, polys, scales):
        for half, half_values in zip(halves, values):
            for i, block in zip(half, half_values):
                other = nn(block, poly[...]) if rows_first else nn(poly[...], block)
                total = ns_first * block.astype(f32) + other
                ref[i] = (total if scale is None else total * scale).astype(bf16)


def large_start_kernel(scalars, kept, got, work, poly):
    core, slot_bit, z1, z2 = (scalars[i] for i in range(4))
    total = jnp.zeros((8, D), f32)
    for n in range(16):
        b1, b2, b3, b4 = n // 8, (n // 4) % 2, (n // 2) % 2, n % 2
        source = kept if b1 == 0 else got
        block = source[b2, b3, b4]
        value = block.astype(f32)
        total = total + jnp.sum((value * value).reshape(16, 8, D), axis=0)
        slot = jnp.where(core == 0, b1, b2)
        half = jnp.where(core == 0, b2, b3)
        row_half = jnp.where(core == 0, b3, b1)
        start = ((row_half ^ z1) * 2 + (b4 ^ z2)) * 128
        work[half * 2 + (slot ^ slot_bit), rows_of(start, 128), :] = block
    return 1.0 / (jnp.sqrt(jnp.sum(total)) + 1e-07)


large_halves = ((0, 1), (2, 3))


def large_first_kernel(scalars, kept, got, work, blend, poly):
    scale = large_start_kernel(scalars, kept, got, work, poly)
    for s in range(2):
        blend[s] = work[s]
    newton_schulz([(work, large_halves)], [poly], False, [scale])


def large_next_kernel(given, work, poly):
    work[...] = given[...]
    newton_schulz([(work, large_halves)], [poly], False, [None])


def small_start_kernel(scalars, kept, got, work, blend, table):
    core, slot_bit, z1, z2 = (scalars[i] for i in range(4))
    for n in range(16):
        b1, b2, b3, b4 = n // 8, (n // 4) % 2, (n // 2) % 2, n % 2
        source = kept if b1 == 0 else got
        block = source[b2, b3, b4]
        slot = jnp.where(core == 0, b2, b1) ^ slot_bit
        half = jnp.where(core == 0, b1, b3)
        row_half = jnp.where(core == 0, b3, b2)
        quarter = (row_half ^ z1) * 2 + (b4 ^ z2)
        work[slot, half, rows_of(quarter * 64, 64), :] = block[:64]

        @pl.when((half == 0) & (slot == 0))
        def _():
            table[rows_of(quarter * TABLE_ROWS, TABLE_ROWS), :] = block[64:]

    for s in range(2):
        blend[s] = work[s, 0]


def small_kernel(given, result, first, second, poly_first, poly_second):
    works = (first, second)
    scales = []
    for s, work in enumerate(works):
        total = jnp.zeros((8, D), f32)
        for half in range(2):
            block = given[s, half]
            work[half] = block
            value = block.astype(f32)
            total = total + jnp.sum((value * value).reshape(32, 8, D), axis=0)
        scales.append(1.0 / (jnp.sqrt(jnp.sum(total)) + 1e-07))
    groups = [(work, ((0,), (1,))) for work in works]
    polys = [poly_first, poly_second]
    newton_schulz(groups, polys, True, scales)

    def step(i, carry):
        newton_schulz(groups, polys, True, [None, None])
        return carry

    lax.fori_loop(1, NS_STEPS, step, 0)
    for s, work in enumerate(works):
        result[s] = work[0]


def new_moment(blend, moment):
    share = 1.0 / (1.0 + momentum_rate)
    return share * blend + (momentum_rate - share * momentum_rate * momentum_rate) * moment


def new_weight(weight, ortho, longest):
    return weight - muon_rate * (0.2 * math.sqrt(longest) * ortho + decay_rate * weight)


def large_out_kernel(
    scalars, own, got, up_weight, up_moment, down_weight, down_moment, up_moment_new, up_new, down_moment_new, down_new
):
    first = scalars[0] == 0
    ups = [jnp.where(first, own[i, 0].astype(f32), got[i, 0].astype(f32)) for i in range(2)]
    downs = [jnp.where(first, got[i, 0].astype(f32), own[i, 0].astype(f32)) for i in range(2)]
    up_new[...] = new_weight(up_weight[...], ups[0], FF)
    up_moment_new[...] = new_moment(ups[1], up_moment[...])
    down_new[...] = new_weight(down_weight[...], downs[0].T, FF)
    down_moment_new[...] = new_moment(downs[1].T, down_moment[...])


def small_moment_kernel(scalars, own, got, moment, moment_new):
    mine = scalars[0] == pl.program_id(0) // 2
    blend = jnp.where(mine, own[0].astype(f32), got[0].astype(f32))
    moment_new[0] = new_moment(blend, moment[0])


def small_weight_kernel(scalars, own, got, weight, weight_new):
    mine = scalars[0] == pl.program_id(0) // 2
    ortho = jnp.where(mine, own[0].astype(f32), got[0].astype(f32))
    weight_new[0] = new_weight(weight[0], ortho, D)


def on_device(
    features,
    levels,
    neighbour_index,
    neighbour_count,
    cotangent,
    attention_weight,
    up_weight,
    down_weight,
    modulation,
    attention_moment,
    up_moment,
    down_moment,
    modulation_moment,
):
    row_count = features.shape[0]
    device_count = lax.axis_size(AXES)
    me = lax.axis_index(AXES)
    first_row = me * row_count

    def bit(mask):
        return (me // mask) % 2

    hid, core, slot_bit, z1, z2 = bit(1), bit(2), bit(4), bit(8), bit(16)
    scalars = jnp.stack([core, slot_bit, z1, z2, hid]).astype(jnp.int32)
    is_first = core == 0

    def along(value, distance):
        pairs = [(i, i + distance) for i in range(device_count) if 0 <= i + distance < device_count]
        return lax.ppermute(value, AXES, pairs)

    def after(value, *others):
        return lax.optimization_barrier((value,) + others)[0]

    def swap(value, mask, other=None):
        masks = (mask, mask if other is None else other)
        pairs = [(i, i ^ masks[(i // 2) % 2]) for i in range(device_count)]
        return lax.ppermute(value, AXES, pairs)

    live = jnp.arange(K, dtype=jnp.int32)[None, :] < neighbour_count[:, None]
    row_ids = first_row + jnp.arange(row_count, dtype=jnp.int32)[:, None]
    offsets = jnp.where(live, neighbour_index - row_ids, 512)
    pack = jnp.concatenate(
        [offsets, levels[:, None], jnp.zeros((row_count, 128 - K - 1), jnp.int32)], axis=1
    ).astype(f32)
    rims = jnp.concatenate([features, pack.astype(bf16)], axis=1)
    rim_low = along(rims[row_count - HALO :], 1)
    rim_high = along(rims[:HALO], -1)

    mod = modulation.reshape(8, D)
    first_in, qkv, counts, attn_bf = pl.pallas_call(
        project_kernel,
        grid=(4,),
        out_shape=(
            struct((row_count, D), bf16),
            struct((3, row_count, D), bf16),
            struct((row_count, SPAN), bf16),
            struct((4, D, D), bf16),
        ),
        in_specs=[
            pl.BlockSpec((row_count, D), lambda g: (0, 0)),
            pl.BlockSpec((row_count, 128), lambda g: (0, 0)),
            pl.BlockSpec((8, D), lambda g: (0, 0)),
            pl.BlockSpec((1, D, D), lambda g: (g, 0, 0)),
        ],
        out_specs=(
            pl.BlockSpec((row_count, D), lambda g: (0, 0)),
            pl.BlockSpec((3, row_count, D), lambda g: (0, 0, 0)),
            pl.BlockSpec((row_count, SPAN), lambda g: (0, 0)),
            pl.BlockSpec((1, D, D), lambda g: (g, 0, 0)),
        ),
        cost_estimate=cost(4e9, 4e6),
        name="project",
        compiler_params=room(24),
    )(features, pack, mod, attention_weight)

    quarter = jnp.stack(
        [
            lax.dynamic_slice(up_weight, (0, core * CHUNK), (D, CHUNK)),
            lax.dynamic_slice(down_weight, (core * CHUNK, 0), (CHUNK, D)),
        ]
    ).astype(bf16)
    near = swap(after(quarter, first_in), 1)
    far = swap(near, 2)

    attended, stream, second_in, padded, rim_queries, rim_counts, log_totals = pl.pallas_call(
        forward_kernel,
        out_shape=(
            struct((row_count, D), bf16),
            struct((row_count, D), f32),
            struct((row_count, D), bf16),
            struct((2, row_count + 2 * HALO, D), bf16),
            struct((2 * HALO, D), bf16),
            struct((2 * HALO, RIM), bf16),
            struct((row_count, 128), f32),
        ),
        in_specs=[VMEM] * 8,
        out_specs=(VMEM,) * 7,
        scratch_shapes=[pltpu.VMEM((2 * HALO, D), bf16)],
        cost_estimate=cost(6e9, 8e6),
        name="attend",
        compiler_params=room(30),
    )(rim_low, rim_high, features, pack, mod, attn_bf, qkv, counts)

    def whole(*shape):
        return pl.BlockSpec(shape, lambda g, s: (0,) * len(shape))

    chunk_shape = struct((2, 2, 2, 128, CHUNK), bf16)
    branch, grad_second, own_kept, own_sent = pl.pallas_call(
        mlp_own_kernel,
        out_shape=(struct((row_count, D), f32), struct((row_count, D), f32), chunk_shape, chunk_shape),
        grid_spec=pltpu.PrefetchScalarGridSpec(
            num_scalar_prefetch=1,
            grid=(2,),
            in_specs=[
                whole(row_count, D),
                whole(row_count, D),
                pl.BlockSpec((D, CHUNK), lambda g, s: (0, g)),
                pl.BlockSpec((CHUNK, D), lambda g, s: (g, 0)),
            ],
            out_specs=(
                whole(row_count, D),
                whole(row_count, D),
                pl.BlockSpec((1, 2, 2, 128, CHUNK), lambda g, s: (g ^ s[1], 0, 0, 0, 0)),
                pl.BlockSpec((1, 2, 2, 128, CHUNK), lambda g, s: (g ^ s[1], 0, 0, 0, 0)),
            ),
            scratch_shapes=[pltpu.VMEM((row_count, CHUNK), bf16)] * 2,
        ),
        cost_estimate=cost(5e9, 8e6),
        name="mlp_own",
        compiler_params=room(30),
    )(scalars, second_in, cotangent, up_weight, down_weight)

    (
        rest_kept,
        rest_sent,
        output,
        grad_stream,
        grad_attended,
        stats,
        edge_low,
        edge_high,
        table_two,
    ) = pl.pallas_call(
        mlp_rest_kernel,
        out_shape=(
            chunk_shape,
            chunk_shape,
            struct((row_count, D), bf16),
            struct((row_count, D), f32),
            struct((row_count, D), bf16),
            struct((row_count, 128), f32),
            struct((HALO, D + 128), bf16),
            struct((HALO, D + 128), bf16),
            struct((8, D), f32),
        ),
        grid_spec=pltpu.PrefetchScalarGridSpec(
            num_scalar_prefetch=1,
            grid=(2,),
            in_specs=[
                whole(row_count, D),
                whole(row_count, D),
                whole(2, D, CHUNK),
                whole(2, D, CHUNK),
                whole(row_count, D),
                whole(row_count, D),
                whole(row_count, D),
                whole(row_count, 128),
                whole(8, D),
                whole(4, D, D),
                whole(row_count, D),
                whole(row_count, 128),
            ],
            out_specs=(
                pl.BlockSpec((1, 2, 2, 128, CHUNK), lambda g, s: (g ^ s[0] ^ s[1], 0, 0, 0, 0)),
                pl.BlockSpec((1, 2, 2, 128, CHUNK), lambda g, s: (g ^ s[0] ^ s[1], 0, 0, 0, 0)),
                whole(row_count, D),
                whole(row_count, D),
                whole(row_count, D),
                whole(row_count, 128),
                whole(HALO, D + 128),
                whole(HALO, D + 128),
                whole(8, D),
            ),
            scratch_shapes=[
                pltpu.VMEM((row_count, D), f32),
                pltpu.VMEM((row_count, D), f32),
                pltpu.VMEM((row_count, CHUNK), bf16),
                pltpu.VMEM((row_count, CHUNK), bf16),
            ],
        ),
        cost_estimate=cost(6e9, 12e6),
        name="mlp_rest",
        compiler_params=room(40),
    )(
        scalars,
        second_in,
        cotangent,
        near,
        far,
        branch,
        grad_second,
        stream,
        pack,
        mod,
        attn_bf,
        attended,
        log_totals,
    )

    grad_low = along(edge_high, 1)
    grad_high = along(edge_low, -1)

    def kept_of(first, second):
        return jnp.where(is_first, first, second)

    own_sum = own_kept.astype(f32) + swap(own_sent, 2).astype(f32)
    rest_sum = rest_kept.astype(f32) + swap(rest_sent, 2).astype(f32)

    def take(keep, send, route):
        return keep + swap(send, *route).astype(f32)

    def parted(total):
        return total[0], total[1].astype(bf16)

    def spread_out(keep):
        mask = 32
        while mask < device_count:
            rounded = keep.astype(bf16)
            keep = rounded.astype(f32) + swap(rounded, mask).astype(f32)
            mask *= 2
        return keep

    def doubled(shard, routes):
        pieces = shard
        for route in routes[:0:-1]:
            pieces = jnp.stack([pieces, swap(pieces, *route)])
        return pieces, swap(pieces, *routes[0])

    blend_rate = 1.0 + momentum_rate
    past_rate = momentum_rate * momentum_rate
    large_routes = ((4, 8), (1, 4), (8, 1), (16, 16))
    large_keep = kept_of(
        jnp.stack([own_sum[0], rest_sum[0]]),
        jnp.stack([own_sum[:, 0], rest_sum[:, 0]], axis=1),
    )
    large_send = kept_of(
        jnp.stack([own_sum[1], rest_sum[1]]),
        jnp.stack([own_sum[:, 1], rest_sum[:, 1]], axis=1),
    )
    large_send = large_send.astype(bf16)

    padded_rows = row_count + 2 * HALO
    half_blocks = row_count // BLOCK // 2
    totals_shape = (struct((row_count // 2, D), bf16),) + (struct((padded_rows, D), f32),) * 2
    early, keys_total, values_total = pl.pallas_call(
        functools.partial(backward_kernel, 0, half_blocks),
        out_shape=totals_shape,
        in_specs=[VMEM] * 5,
        out_specs=(VMEM,) * 3,
        cost_estimate=cost(4e9, 9e6),
        name="attend_back",
        compiler_params=room(24),
    )(after(qkv, large_send), padded, grad_attended, stats, counts)
    late, keys_total, values_total = pl.pallas_call(
        functools.partial(backward_kernel, half_blocks, 2 * half_blocks),
        out_shape=totals_shape,
        in_specs=[VMEM] * 7,
        out_specs=(VMEM,) * 3,
        input_output_aliases={5: 1, 6: 2},
        cost_estimate=cost(4e9, 9e6),
        name="attend_back",
        compiler_params=room(24),
    )(qkv, padded, grad_attended, stats, counts, keys_total, values_total)
    large_keep, large_send = parted(take(large_keep, large_send, large_routes[0]))
    piece_shape = struct((2, 2, 2, 2, 80, D), bf16)
    features_grad, small_kept, small_sent = pl.pallas_call(
        weights_kernel,
        out_shape=(struct((row_count, D), f32), piece_shape, piece_shape),
        in_specs=[SMEM] + [VMEM] * 17,
        out_specs=(VMEM,) * 3,
        scratch_shapes=[
            pltpu.VMEM((4, row_count, D), bf16),
            pltpu.VMEM((8, D), f32),
            pltpu.VMEM((row_count, D), f32),
            pltpu.VMEM((row_count, D), f32),
        ],
        cost_estimate=cost(6e9, 9e6),
        name="attend_weights",
        compiler_params=room(34),
    )(
        scalars,
        early,
        after(late, large_send),
        keys_total,
        values_total,
        padded,
        rim_queries,
        rim_counts,
        grad_low,
        grad_high,
        first_in,
        attended,
        grad_stream,
        features,
        pack,
        mod,
        attn_bf,
        table_two,
    )
    large_keep, large_send = parted(take(large_keep, large_send, large_routes[1]))
    large_keep, large_send = parted(take(large_keep, large_send, large_routes[2]))
    large_shard = spread_out(take(large_keep, large_send, large_routes[3]))
    row_start = (z1 * 2 + z2) * 128
    large_past = kept_of(
        lax.dynamic_slice(up_moment, (row_start, slot_bit * CHUNK), (128, CHUNK)),
        lax.dynamic_slice(down_moment, (slot_bit * CHUNK, row_start), (CHUNK, 128)).T,
    )
    large_blend = (blend_rate * large_shard + past_rate * large_past).astype(bf16)
    large_kept, large_got = doubled(large_blend, large_routes)

    small_routes = ((1, 4), (4, 8), (8, 1), (16, 16))
    small_keep, small_send = parted(small_kept.astype(f32) + swap(small_sent, 2).astype(f32))
    for route in small_routes[:3]:
        small_keep, small_send = parted(take(small_keep, small_send, route))
    small_shard = spread_out(take(small_keep, small_send, small_routes[3]))
    small_past = lax.dynamic_slice(
        attention_moment, (core * 2 + slot_bit, (z1 * 2 + z2) * 64, 0), (1, 64, D)
    )[0]
    small_blend = jnp.concatenate(
        [
            (blend_rate * small_shard[:64] + past_rate * small_past).astype(bf16),
            small_shard[64:].astype(bf16),
        ]
    )
    small_kept, small_got = doubled(small_blend, small_routes)

    large_work, large_mix = pl.pallas_call(
        large_first_kernel,
        out_shape=(struct((4, D, CHUNK), bf16), struct((2, D, CHUNK), bf16)),
        in_specs=[SMEM, VMEM, VMEM],
        out_specs=(VMEM, VMEM),
        scratch_shapes=[pltpu.VMEM((D, D), bf16)],
        cost_estimate=cost(3e9, 6e6),
        name="ortho_large",
        compiler_params=room(24),
    )(scalars, large_kept, large_got)
    for _ in range(1, NS_STEPS):
        large_work = pl.pallas_call(
            large_next_kernel,
            out_shape=struct((4, D, CHUNK), bf16),
            in_specs=[VMEM],
            out_specs=VMEM,
            scratch_shapes=[pltpu.VMEM((D, D), bf16)],
            cost_estimate=cost(3e9, 4e6),
            name="ortho_large",
            compiler_params=room(24),
        )(large_work)
    large_result = large_work[:2]
    large_own = jnp.stack([large_result, large_mix])
    large_other = swap(large_own, 2)
    up_moment_new, up_new, down_moment_new, down_new = pl.pallas_call(
        large_out_kernel,
        grid=(2,),
        out_shape=(struct((D, 2 * CHUNK), f32),) * 2 + (struct((2 * CHUNK, D), f32),) * 2,
        in_specs=[
            SMEM,
            pl.BlockSpec((2, 1, D, CHUNK), lambda g: (0, g, 0, 0)),
            pl.BlockSpec((2, 1, D, CHUNK), lambda g: (0, g, 0, 0)),
            pl.BlockSpec((D, CHUNK), lambda g: (0, g)),
            pl.BlockSpec((D, CHUNK), lambda g: (0, g)),
            pl.BlockSpec((CHUNK, D), lambda g: (g, 0)),
            pl.BlockSpec((CHUNK, D), lambda g: (g, 0)),
        ],
        out_specs=(
            pl.BlockSpec((D, CHUNK), lambda g: (0, g)),
            pl.BlockSpec((D, CHUNK), lambda g: (0, g)),
            pl.BlockSpec((CHUNK, D), lambda g: (g, 0)),
            pl.BlockSpec((CHUNK, D), lambda g: (g, 0)),
        ),
        cost_estimate=cost(1e7, 2e7),
        name="update_large",
        compiler_params=room(24),
    )(scalars, large_own, large_other, up_weight, up_moment, down_weight, down_moment)

    small_work, small_mix, table_own = pl.pallas_call(
        small_start_kernel,
        out_shape=(
            struct((2, 2, 256, D), bf16),
            struct((2, 256, D), bf16),
            struct((4 * TABLE_ROWS, D), bf16),
        ),
        in_specs=[SMEM, VMEM, VMEM],
        out_specs=(VMEM,) * 3,
        cost_estimate=cost(1e6, 4e6),
        name="unpack_small",
        compiler_params=room(12),
    )(scalars, small_kept, small_got)
    small_result = pl.pallas_call(
        small_kernel,
        out_shape=struct((2, 256, D), bf16),
        in_specs=[VMEM],
        out_specs=VMEM,
        scratch_shapes=[pltpu.VMEM((2, 256, D), bf16)] * 2 + [pltpu.VMEM((D, D), bf16)] * 2,
        cost_estimate=cost(6e9, 4e6),
        name="ortho_small",
        compiler_params=room(16),
    )(small_work)
    small_other = swap(small_result, 2)
    mix_other = swap(small_mix, 2)
    table_other = swap(table_own, 2)

    def per_matrix(index):
        return pl.BlockSpec((1, 256, D), index)

    def update_small(kernel, own, other, held, index, name):
        return pl.pallas_call(
            kernel,
            grid_spec=pltpu.PrefetchScalarGridSpec(
                num_scalar_prefetch=1,
                grid=(4,),
                in_specs=[
                    per_matrix(lambda g, s: (g % 2, 0, 0)),
                    per_matrix(lambda g, s: (g % 2, 0, 0)),
                    per_matrix(index),
                ],
                out_specs=per_matrix(lambda g, s: (g, 0, 0)),
            ),
            out_shape=struct((4, 256, D), f32),
            cost_estimate=cost(1e7, 6e6),
            name=name,
            compiler_params=room(8),
        )(scalars, own, other, held)

    attention_moment_new = update_small(
        small_moment_kernel, small_mix, mix_other, attention_moment, lambda g, s: (g, 0, 0), "moment_small"
    )
    attention_new = update_small(
        small_weight_kernel,
        small_result,
        small_other,
        attention_weight,
        lambda g, s: (g, s[4], 0),
        "update_small",
    )
    table_sum = kept_of(table_own, table_other)[::TABLE_ROWS].astype(f32)
    modulation_moment_new = vector_rate * modulation_moment + table_sum.reshape(2, 2, D)
    held = lax.dynamic_slice_in_dim(modulation, hid * 2, 2, 1)
    node_total = row_count * device_count
    modulation_new = held - 0.2 / math.sqrt(node_total) * modulation_moment_new
    return (
        output,
        features_grad,
        attention_moment_new,
        attention_new,
        up_moment_new,
        up_new,
        down_moment_new,
        down_new,
        modulation_moment_new,
        modulation_new,
    )


def solution(mesh):
    placed = (
        P(("nodes", "hid"), None),
        P(("nodes", "hid")),
        P(("nodes", "hid"), None),
        P(("nodes", "hid")),
        P(("nodes", "hid"), None),
        P(),
        P(None, "hid"),
        P("hid", None),
        P(),
        P(None, "hid", None),
        P(None, "hid"),
        P("hid", None),
        P(None, "hid", None),
    )
    return jax.shard_map(
        on_device,
        mesh=mesh,
        in_specs=placed,
        out_specs=(
            P(("nodes", "hid"), None),
            P(("nodes", "hid"), None),
            P(None, "hid", None),
            P(None, "hid", None),
            P(None, "hid"),
            P(None, "hid"),
            P("hid", None),
            P("hid", None),
            P(None, "hid", None),
            P(None, "hid", None),
        ),
        check_vma=False,
    )
```

```python
import functools
import math

import jax
import jax.numpy as jnp
from jax import lax
from jax.experimental import pallas as pl
from jax.experimental.pallas import tpu as pltpu
from jax.sharding import PartitionSpec as P

D = 512
HEADS = 4
HD = 128
FF = 2048
K = 16
NS_STEPS = 4
HALO = 192
BLOCK = 128
SPAN = BLOCK + 2 * HALO
RIM = 256
CHUNK = 512
TABLE_ROWS = 16

f32 = jnp.float32
bf16 = jnp.bfloat16
ns_first = 3.4445
ns_second = -4.775
ns_third = 2.0315
momentum_rate = 0.95
vector_rate = 0.9
muon_rate = 0.2
decay_rate = 0.1
score_scale = 1.0 / math.sqrt(HD)
AXES = ("nodes", "hid")
VMEM = pl.BlockSpec(memory_space=pltpu.VMEM)
SMEM = pl.BlockSpec(memory_space=pltpu.SMEM)


def nn(a, b):
    return lax.dot_general(a, b, (((1,), (0,)), ((), ())), preferred_element_type=f32)


def nt(a, b):
    return lax.dot_general(a, b, (((1,), (1,)), ((), ())), preferred_element_type=f32)


def tn(a, b):
    return lax.dot_general(a, b, (((0,), (0,)), ((), ())), preferred_element_type=f32)


def struct(shape, dtype):
    return jax.ShapeDtypeStruct(shape, dtype)


def rows_of(start, size):
    return pl.ds(pl.multiple_of(start, size), size)


def cost(flops, data):
    return pl.CostEstimate(flops=int(flops), bytes_accessed=int(data), transcendentals=0)


def room(mebibytes):
    return pltpu.CompilerParams(vmem_limit_bytes=mebibytes << 20)


def norm_parts(field):
    average = jnp.mean(field, axis=-1, keepdims=True)
    centred = field - average
    variance = jnp.mean(centred * centred, axis=-1, keepdims=True)
    inverse = lax.rsqrt(variance + 1e-06)
    return centred * inverse, inverse


def table_rows(mod_ref, level, column):
    return jnp.where(level > 0.5, mod_ref[4 + column : 5 + column, :], mod_ref[column : column + 1, :])


def modulated(field, level, mod_ref, column):
    normed, _ = norm_parts(field)
    return normed * (1.0 + table_rows(mod_ref, level, column)) + table_rows(
        mod_ref, level, column + 1
    )


def norm_back(grad_out, field, level, mod_ref, column):
    normed, inverse = norm_parts(field)
    grad_norm = grad_out * (1.0 + table_rows(mod_ref, level, column))
    grad_in = inverse * (
        grad_norm
        - jnp.mean(grad_norm, axis=-1, keepdims=True)
        - normed * jnp.mean(grad_norm * normed, axis=-1, keepdims=True)
    )
    return grad_in, grad_out * normed


def add_table(table_ref, column, level, scale_term, shift_term):
    upper = level > 0.5
    for term, place in ((scale_term, column), (shift_term, column + 1)):
        low_part = jnp.sum(jnp.where(upper, 0.0, term), axis=0, keepdims=True)
        high_part = jnp.sum(jnp.where(upper, term, 0.0), axis=0, keepdims=True)
        table_ref[place : place + 1, :] += low_part
        table_ref[4 + place : 5 + place, :] += high_part


def slot_counts(pack, row_count, width, shift):
    pieces = []
    for left in range(0, width, 128):
        lanes = lax.broadcasted_iota(jnp.int32, (row_count, 128), 1)
        rows = lax.broadcasted_iota(jnp.int32, (row_count, 128), 0)
        place = (lanes - rows + (left - shift)).astype(f32)
        total = jnp.zeros((row_count, 128), f32)
        for slot in range(K):
            total = total + jnp.where(place == pack[:, slot : slot + 1], 1.0, 0.0)
        pieces.append(total)
    return jnp.concatenate(pieces, axis=1).astype(bf16)


def project_kernel(features, pack, mod, weights, first_in, qkv, counts, rounded):
    row_count = features.shape[0]
    turn = pl.program_id(0)

    @pl.when(turn == 0)
    def _():
        for start in range(0, row_count, 256):
            rows = slice(start, start + 256)
            level = pack[rows, K : K + 1]
            first_in[rows, :] = modulated(features[rows, :].astype(f32), level, mod, 0).astype(bf16)

    weight = weights[0].astype(bf16)
    rounded[0] = weight

    @pl.when(turn < 3)
    def _():
        qkv[turn] = nn(first_in[...], weight).astype(bf16)
        share = row_count // BLOCK // 3

        def count_step(b, carry):
            rows = rows_of(b * BLOCK, BLOCK)
            counts[rows, :] = slot_counts(pack[rows, :], BLOCK, SPAN, HALO)
            return carry

        lax.fori_loop(turn * share, (turn + 1) * share, count_step, 0)


def forward_kernel(
    rim_low,
    rim_high,
    features,
    pack,
    mod,
    weights,
    qkv,
    counts,
    attended,
    stream,
    second_in,
    padded,
    rim_queries,
    rim_counts,
    log_totals,
    rim_in,
):
    row_count = features.shape[0]
    for side, rim in enumerate((rim_low, rim_high)):
        for start in range(0, HALO, 64):
            rows = slice(start, start + 64)
            info = rim[rows, D:].astype(f32)
            rim_in[side * HALO + start : side * HALO + start + 64, :] = modulated(
                rim[rows, :D].astype(f32), info[:, K : K + 1], mod, 0
            ).astype(bf16)
            rim_counts[side * HALO + start : side * HALO + start + 64, :] = slot_counts(
                info, 64, RIM, start + (-HALO if side == 0 else RIM)
            )
    rim_queries[...] = nn(rim_in[...], weights[0]).astype(bf16)
    for p in range(2):
        piece = nn(rim_in[...], weights[1 + p]).astype(bf16)
        padded[p, :HALO, :] = piece[:HALO]
        padded[p, HALO + row_count :, :] = piece[HALO:]
        padded[p, HALO : HALO + row_count, :] = qkv[1 + p]

    def step(b, carry):
        rows = rows_of(b * BLOCK, BLOCK)
        span = pl.ds(pl.multiple_of(b * BLOCK, BLOCK), SPAN)
        count = counts[rows, :].astype(f32)
        live = count > 0.0
        columns = [slice(h * HD, (h + 1) * HD) for h in range(HEADS)]
        scores = [nt(qkv[0, rows, cols], padded[0, span, cols]) * score_scale for cols in columns]
        lanes = lax.broadcasted_iota(jnp.int32, (BLOCK, 128), 1)
        stats = jnp.zeros((BLOCK, 128), f32)
        for h, cols in enumerate(columns):
            masked = jnp.where(live, scores[h], -1e30)
            peak = jnp.max(masked, axis=-1, keepdims=True)
            exponent = jnp.exp(masked - peak)
            total = jnp.sum(exponent * count, axis=-1, keepdims=True)
            probs = (exponent / total).astype(bf16)
            spread = (probs.astype(f32) * count).astype(bf16)
            attended[rows, cols] = nn(spread, padded[1, span, cols]).astype(bf16)
            stats = jnp.where(lanes == h, peak + jnp.log(total), stats)
        log_totals[rows, :] = stats
        return carry

    lax.fori_loop(0, row_count // BLOCK, step, 0)
    for start in range(0, row_count, 256):
        rows = slice(start, start + 256)
        field = features[rows, :].astype(f32) + nn(attended[rows, :], weights[3])
        stream[rows, :] = field
        second_in[rows, :] = modulated(field, pack[rows, K : K + 1], mod, 2).astype(bf16)


def mlp_chunk(
    scalars, second_in, cotangent, up, down, branch_in, grad_in, branch, grad_second, acts, grads, kept, sent
):
    row_count = second_in.shape[0]
    for start in range(0, row_count, 256):
        rows = slice(start, start + 256)
        preact = nn(second_in[rows, :], up)
        grad_act = nt(cotangent[rows, :], down)
        sigmoid = 0.5 * jnp.tanh(0.5 * preact) + 0.5
        act = (preact * sigmoid).astype(bf16)
        acts[rows, :] = act
        grad_pre = (grad_act * (sigmoid * (1.0 + preact * (1.0 - sigmoid)))).astype(bf16)
        grads[rows, :] = grad_pre
        branch[rows, :] = branch_in[rows, :] + nn(act, down)
        grad_second[rows, :] = grad_in[rows, :] + nt(grad_pre, up)
    first, z1, z2 = scalars[0] == 0, scalars[2], scalars[3]
    for out, swapped in ((kept, False), (sent, True)):
        ups = jnp.logical_not(first) if swapped else first
        product = tn(
            jnp.where(ups, second_in[...], cotangent[...]), jnp.where(ups, grads[...], acts[...])
        )
        for q in range(4):
            out[0, (q // 2) ^ z1, (q % 2) ^ z2] = product[q * 128 : (q + 1) * 128].astype(bf16)


def mlp_own_kernel(
    scalars, second_in, cotangent, up, down, branch, grad_second, kept, sent, acts, grads
):
    @pl.when(pl.program_id(0) == 0)
    def _():
        branch[...] = jnp.zeros_like(branch)
        grad_second[...] = jnp.zeros_like(grad_second)

    mlp_chunk(
        scalars,
        second_in,
        cotangent,
        up[...].astype(bf16),
        down[...].astype(bf16),
        branch,
        grad_second,
        branch,
        grad_second,
        acts,
        grads,
        kept,
        sent,
    )


def mlp_near_kernel(
    scalars, second_in, cotangent, near, branch_in, grad_in, branch, grad_second, kept, sent, acts, grads
):
    mlp_chunk(
        scalars,
        second_in,
        cotangent,
        near[0],
        near[1],
        branch_in,
        grad_in,
        branch,
        grad_second,
        acts,
        grads,
        kept,
        sent,
    )


def mlp_far_kernel(
    scalars,
    second_in,
    cotangent,
    far,
    branch_in,
    grad_in,
    stream,
    pack,
    mod,
    weights,
    attended,
    log_totals,
    kept_in,
    sent_in,
    kept,
    sent,
    output,
    grad_stream,
    grad_attended,
    stats,
    edge_low,
    edge_high,
    table,
    branch,
    grad_second,
    acts,
    grads,
):
    row_count = second_in.shape[0]
    mlp_chunk(
        scalars,
        second_in,
        cotangent,
        far[0],
        far[1],
        branch_in,
        grad_in,
        branch,
        grad_second,
        acts,
        grads,
        kept,
        sent,
    )
    table[...] = jnp.zeros_like(table)
    for start in range(0, row_count, 256):
        rows = slice(start, start + 256)
        field = stream[rows, :]
        level = pack[rows, K : K + 1]
        output[rows, :] = (field + branch[rows, :]).astype(bf16)
        gradient = grad_second[rows, :]
        grad_field, scale_term = norm_back(gradient, field, level, mod, 2)
        add_table(table, 2, level, scale_term, gradient)
        total = cotangent[rows, :].astype(f32) + grad_field
        grad_stream[rows, :] = total
        back = nt(total.astype(bf16), weights[3]).astype(bf16)
        grad_attended[rows, :] = back
        product = back.astype(f32) * attended[rows, :].astype(f32)
        lanes = lax.broadcasted_iota(jnp.int32, (256, 128), 1)
        kept_stats = log_totals[rows, :]
        for h in range(HEADS):
            delta = jnp.sum(product[:, h * HD : (h + 1) * HD], axis=-1, keepdims=True)
            kept_stats = jnp.where(lanes == HEADS + h, delta, kept_stats)
        stats[rows, :] = kept_stats
    for edge, first in ((edge_low, 0), (edge_high, row_count - HALO)):
        rows = slice(first, first + HALO)
        edge[:, :D] = grad_attended[rows, :]
        known = stats[rows, :]
        upper = known.astype(bf16)
        lower = (known - upper.astype(f32)).astype(bf16).astype(f32)
        edge[:, D:] = (upper.astype(f32) + pltpu.roll(lower, 2 * HEADS, 1)).astype(bf16)


def attention_terms(scores, grad_probs, count, log_total, delta):
    probs = jnp.exp(jnp.where(count > 0.0, scores * score_scale, -1e30) - log_total)
    slopes = (probs * (grad_probs - delta)).astype(bf16).astype(f32)
    spread = (probs.astype(bf16).astype(f32) * count).astype(bf16)
    return (slopes * count).astype(bf16), spread


def backward_kernel(first, last, *refs):
    if first == 0:
        qkv, padded, grad, stats, counts, grad_query, keys_total, values_total = refs
        keys_total[...] = jnp.zeros_like(keys_total)
        values_total[...] = jnp.zeros_like(values_total)
    else:
        qkv, padded, grad, stats, counts, _, _, grad_query, keys_total, values_total = refs

    def step(b, carry):
        rows = rows_of(b * BLOCK, BLOCK)
        span = pl.ds(pl.multiple_of(b * BLOCK, BLOCK), SPAN)
        count = counts[rows, :].astype(f32)
        columns = [slice(h * HD, (h + 1) * HD) for h in range(HEADS)]
        products = [
            (nt(qkv[0, rows, cols], padded[0, span, cols]), nt(grad[rows, cols], padded[1, span, cols]))
            for cols in columns
        ]
        terms = [
            attention_terms(
                *products[h],
                count,
                stats[rows, h : h + 1],
                stats[rows, HEADS + h : HEADS + h + 1],
            )
            for h in range(HEADS)
        ]
        target = rows_of((b - first) * BLOCK, BLOCK)
        for (slopes, spread), cols in zip(terms, columns):
            grad_query[target, cols] = (nn(slopes, padded[0, span, cols]) * score_scale).astype(bf16)
            keys_total[span, cols] += tn(slopes, qkv[0, rows, cols])
            values_total[span, cols] += tn(spread, grad[rows, cols])
        return carry

    lax.fori_loop(first, last, step, 0)


def weights_kernel(
    scalars,
    early,
    late,
    keys_in,
    values_in,
    padded,
    rim_query,
    rim_counts,
    grad_low,
    grad_high,
    first_in,
    attended,
    grad_stream,
    features,
    pack,
    mod,
    weights,
    table_two,
    features_grad,
    kept,
    sent,
    gathered,
    table,
    keys_total,
    values_total,
):
    row_count = first_in.shape[0]
    columns = [slice(h * HD, (h + 1) * HD) for h in range(HEADS)]
    own = slice(HALO, HALO + row_count)
    keys_total[...] = keys_in[own, :]
    values_total[...] = values_in[own, :]
    for side, grads in enumerate((grad_low, grad_high)):
        first = 0 if side == 0 else row_count - RIM
        own_span = slice(first, first + RIM)
        span = slice(HALO + first, HALO + first + RIM)
        rows = slice(side * HALO, (side + 1) * HALO)
        known = grads[:, D:].astype(f32)
        count = rim_counts[rows, :].astype(f32)
        products = [
            (nt(rim_query[rows, cols], padded[0, span, cols]), nt(grads[:, cols], padded[1, span, cols]))
            for cols in columns
        ]
        terms = []
        for h in range(HEADS):
            numbers = [known[:, i * HEADS + h : i * HEADS + h + 1] for i in range(4)]
            terms.append(
                attention_terms(*products[h], count, numbers[0] + numbers[2], numbers[1] + numbers[3])
            )
        for (slopes, spread), cols in zip(terms, columns):
            keys_total[own_span, cols] += tn(slopes, rim_query[rows, cols])
            values_total[own_span, cols] += tn(spread, grads[:, cols])
    half_rows = row_count // 2
    gathered[0, :half_rows, :] = early[...]
    gathered[0, half_rows:, :] = late[...]
    gathered[1] = (keys_total[...] * score_scale).astype(bf16)
    gathered[2] = values_total[...].astype(bf16)
    table[...] = table_two[...]
    for start in range(0, row_count, 256):
        rows = slice(start, start + 256)
        level = pack[rows, K : K + 1]
        gradient = nt(gathered[0, rows, :], weights[0])
        for p in range(1, 3):
            gradient = gradient + nt(gathered[p, rows, :], weights[p])
        grad_field, scale_term = norm_back(gradient, features[rows, :].astype(f32), level, mod, 0)
        add_table(table, 0, level, scale_term, gradient)
        total = grad_stream[rows, :]
        features_grad[rows, :] = total + grad_field
        gathered[3, rows, :] = total.astype(bf16)
    core, slot_bit, z1, z2, hid = (scalars[i] for i in range(5))
    for out, away in ((kept, 0), (sent, 1)):
        target = core ^ away
        for slot in range(2):
            p = 2 * target + slot
            left = first_in[...] if slot == 0 else jnp.where(target == 0, first_in[...], attended[...])
            product = tn(left, gathered[p])
            for half in range(2):
                for q in range(4):
                    slot_at, hid_at, row_half = slot ^ slot_bit, half ^ hid, (q // 2) ^ z1
                    index = (
                        jnp.where(target == 0, hid_at, slot_at),
                        jnp.where(target == 0, slot_at, row_half),
                        jnp.where(target == 0, row_half, hid_at),
                        (q % 2) ^ z2,
                    )
                    start = half * 256 + q * 64
                    out[index + (slice(0, 64),)] = product[start : start + 64].astype(bf16)
                    extra = jnp.zeros((TABLE_ROWS, D), f32)
                    if slot == 0:
                        row = (q // 2) * 4 + 2 * half + q % 2
                        known = jnp.broadcast_to(table[row : row + 1, :], (TABLE_ROWS, D))
                        extra = jnp.where(target == 0, known, extra)
                    out[index + (slice(64, 80),)] = extra.astype(bf16)


def newton_schulz(groups, polys, rows_first, scales):
    blocks = [[[ref[i] for i in half] for half in halves] for ref, halves in groups]
    grams = []
    for halves, scale in zip(blocks, scales):
        sums = []
        for half in halves:
            total = None
            for block in half:
                term = tn(block, block) if rows_first else nt(block, block)
                total = term if total is None else total + term
            sums.append((total if scale is None else total * (scale * scale)).astype(bf16))
        grams.append((sums[0].astype(f32) + sums[1].astype(f32)).astype(bf16))
    for gram, poly in zip(grams, polys):
        poly[...] = (ns_second * gram.astype(f32) + ns_third * nn(gram, gram)).astype(bf16)
    for (ref, halves), values, poly, scale in zip(groups, blocks, polys, scales):
        for half, half_values in zip(halves, values):
            for i, block in zip(half, half_values):
                other = nn(block, poly[...]) if rows_first else nn(poly[...], block)
                total = ns_first * block.astype(f32) + other
                ref[i] = (total if scale is None else total * scale).astype(bf16)


def large_start_kernel(scalars, kept, got, work, poly):
    core, slot_bit, z1, z2 = (scalars[i] for i in range(4))
    total = jnp.zeros((8, D), f32)
    for n in range(16):
        b1, b2, b3, b4 = n // 8, (n // 4) % 2, (n // 2) % 2, n % 2
        source = kept if b1 == 0 else got
        block = source[b2, b3, b4]
        value = block.astype(f32)
        total = total + jnp.sum((value * value).reshape(16, 8, D), axis=0)
        slot = jnp.where(core == 0, b1, b2)
        half = jnp.where(core == 0, b2, b3)
        row_half = jnp.where(core == 0, b3, b1)
        start = ((row_half ^ z1) * 2 + (b4 ^ z2)) * 128
        work[half * 2 + (slot ^ slot_bit), rows_of(start, 128), :] = block
    return 1.0 / (jnp.sqrt(jnp.sum(total)) + 1e-07)


large_halves = ((0, 1), (2, 3))


def large_first_kernel(scalars, kept, got, work, blend, ready, poly):
    ready[...] = jnp.zeros_like(ready)
    scale = large_start_kernel(scalars, kept, got, work, poly)
    for s in range(2):
        blend[s] = work[s]

    def step(i, factor):
        newton_schulz([(work, large_halves)], [poly], False, [factor])
        return jnp.ones((), f32)

    lax.fori_loop(0, NS_STEPS // 2, step, scale)


def large_next_kernel(given, result, work, poly):
    work[...] = given[...]

    def step(i, carry):
        newton_schulz([(work, large_halves)], [poly], False, [None])
        return carry

    lax.fori_loop(NS_STEPS // 2, NS_STEPS, step, 0)
    for s in range(2):
        result[s] = work[s]


def small_start_kernel(scalars, kept, got, work, blend, table):
    core, slot_bit, z1, z2 = (scalars[i] for i in range(4))
    for n in range(16):
        b1, b2, b3, b4 = n // 8, (n // 4) % 2, (n // 2) % 2, n % 2
        source = kept if b1 == 0 else got
        block = source[b2, b3, b4]
        slot = jnp.where(core == 0, b2, b1) ^ slot_bit
        half = jnp.where(core == 0, b1, b3)
        row_half = jnp.where(core == 0, b3, b2)
        quarter = (row_half ^ z1) * 2 + (b4 ^ z2)
        work[slot, half, rows_of(quarter * 64, 64), :] = block[:64]

        @pl.when((half == 0) & (slot == 0))
        def _():
            table[pl.ds(quarter, 1), :] = block[64:].astype(f32)[:1]

    table[4:, :] = jnp.zeros((4, D), f32)
    for s in range(2):
        blend[s] = work[s, 0]


def small_kernel(given, result, first, second, poly_first, poly_second):
    works = (first, second)
    scales = []
    for s, work in enumerate(works):
        total = jnp.zeros((8, D), f32)
        for half in range(2):
            block = given[s, half]
            work[half] = block
            value = block.astype(f32)
            total = total + jnp.sum((value * value).reshape(32, 8, D), axis=0)
        scales.append(1.0 / (jnp.sqrt(jnp.sum(total)) + 1e-07))
    groups = [(work, ((0,), (1,))) for work in works]
    polys = [poly_first, poly_second]

    def step(i, factors):
        newton_schulz(groups, polys, True, factors)
        return (jnp.ones((), f32),) * 2

    lax.fori_loop(0, NS_STEPS, step, tuple(scales))
    for s, work in enumerate(works):
        result[s] = work[0]


def new_moment(blend, moment):
    share = 1.0 / (1.0 + momentum_rate)
    return share * blend + (momentum_rate - share * momentum_rate * momentum_rate) * moment


def new_weight(weight, ortho, longest):
    return weight - muon_rate * (0.2 * math.sqrt(longest) * ortho + decay_rate * weight)


def large_moment_kernel(scalars, own, got, up_moment, down_moment, up_moment_new, down_moment_new):
    first = scalars[0] == 0
    mine, other = own[0].astype(f32), got[0].astype(f32)
    up_moment_new[...] = new_moment(jnp.where(first, mine, other), up_moment[...])
    down_moment_new[...] = new_moment(jnp.where(first, other, mine).T, down_moment[...])


def large_weight_kernel(scalars, own, got, up_weight, down_weight, up_new, down_new):
    first = scalars[0] == 0
    mine, other = own[0].astype(f32), got[0].astype(f32)
    up_new[...] = new_weight(up_weight[...], jnp.where(first, mine, other), FF)
    down_new[...] = new_weight(down_weight[...], jnp.where(first, other, mine).T, FF)


def table_kernel(scalars, own, got, held, moment, moment_new, held_new, *, nodes):
    total = jnp.where(scalars[0] == 0, own[...], got[...])
    for level in range(2):
        for column in range(2):
            row = level * 2 + column
            at = (slice(level, level + 1), slice(column, column + 1))
            value = vector_rate * moment[at] + total[row : row + 1, :].reshape(1, 1, D)
            moment_new[at] = value
            held_new[at] = held[at] - 0.2 / math.sqrt(nodes) * value


def small_moment_kernel(scalars, own, got, moment, moment_new):
    mine = scalars[0] == pl.program_id(0) // 2
    blend = jnp.where(mine, own[0].astype(f32), got[0].astype(f32))
    moment_new[0] = new_moment(blend, moment[0])


def small_weight_kernel(scalars, own, got, weight, weight_new):
    mine = scalars[0] == pl.program_id(0) // 2
    ortho = jnp.where(mine, own[0].astype(f32), got[0].astype(f32))
    weight_new[0] = new_weight(weight[0], ortho, D)


def on_device(
    features,
    levels,
    neighbour_index,
    neighbour_count,
    cotangent,
    attention_weight,
    up_weight,
    down_weight,
    modulation,
    attention_moment,
    up_moment,
    down_moment,
    modulation_moment,
):
    row_count = features.shape[0]
    device_count = lax.axis_size(AXES)
    me = lax.axis_index(AXES)
    first_row = me * row_count

    def bit(place):
        return (me >> place) & 1

    hid, core, slot_bit, z1, z2 = (bit(place) for place in range(5))
    scalars = jnp.stack([core, slot_bit, z1, z2, hid]).astype(jnp.int32)
    is_first = core == 0

    def along(value, distance):
        pairs = [(i, i + distance) for i in range(device_count) if 0 <= i + distance < device_count]
        return lax.ppermute(value, AXES, pairs)

    def after(value, *others):
        return lax.optimization_barrier((value,) + others)[0]

    def swap(value, mask, other=None):
        masks = (mask, mask if other is None else other)
        pairs = [(i, i ^ masks[(i // 2) % 2]) for i in range(device_count)]
        return lax.ppermute(value, AXES, pairs)

    live = jnp.arange(K, dtype=jnp.int32)[None, :] < neighbour_count[:, None]
    row_ids = first_row + jnp.arange(row_count, dtype=jnp.int32)[:, None]
    offsets = jnp.where(live, neighbour_index - row_ids, 512)
    pack = jnp.concatenate(
        [offsets, levels[:, None], jnp.zeros((row_count, 128 - K - 1), jnp.int32)], axis=1
    ).astype(f32)
    rims = jnp.concatenate([features, pack.astype(bf16)], axis=1)
    rim_low = along(rims[row_count - HALO :], 1)
    rim_high = along(rims[:HALO], -1)

    mod = modulation.reshape(8, D)
    row_start = (z1 * 2 + z2) * 128
    large_past = jnp.where(
        is_first,
        lax.dynamic_slice(up_moment, (row_start, slot_bit * CHUNK), (128, CHUNK)),
        lax.dynamic_slice(down_moment, (slot_bit * CHUNK, row_start), (CHUNK, 128)).T,
    )
    small_past = lax.dynamic_slice(
        attention_moment, (core * 2 + slot_bit, (z1 * 2 + z2) * 64, 0), (1, 64, D)
    )[0]
    held = lax.dynamic_slice_in_dim(modulation, hid * 2, 2, 1)
    quarter = jnp.stack(
        [
            lax.dynamic_slice(up_weight, (0, core * CHUNK), (D, CHUNK)),
            lax.dynamic_slice(down_weight, (core * CHUNK, 0), (CHUNK, D)),
        ]
    ).astype(bf16)
    pack, mod, scalars, is_first, large_past, small_past, held, quarter = lax.optimization_barrier(
        (pack, mod, scalars, is_first, large_past, small_past, held, quarter)
    )
    first_in, qkv, counts, attn_bf = pl.pallas_call(
        project_kernel,
        grid=(4,),
        out_shape=(
            struct((row_count, D), bf16),
            struct((3, row_count, D), bf16),
            struct((row_count, SPAN), bf16),
            struct((4, D, D), bf16),
        ),
        in_specs=[
            pl.BlockSpec((row_count, D), lambda g: (0, 0)),
            pl.BlockSpec((row_count, 128), lambda g: (0, 0)),
            pl.BlockSpec((8, D), lambda g: (0, 0)),
            pl.BlockSpec((1, D, D), lambda g: (g, 0, 0)),
        ],
        out_specs=(
            pl.BlockSpec((row_count, D), lambda g: (0, 0)),
            pl.BlockSpec((3, row_count, D), lambda g: (0, 0, 0)),
            pl.BlockSpec((row_count, SPAN), lambda g: (0, 0)),
            pl.BlockSpec((1, D, D), lambda g: (g, 0, 0)),
        ),
        cost_estimate=cost(4e9, 4e6),
        name="project",
        compiler_params=room(12),
    )(features, pack, mod, attention_weight)

    near = swap(after(quarter, rim_low, rim_high), 1)

    attended, stream, second_in, padded, rim_queries, rim_counts, log_totals = pl.pallas_call(
        forward_kernel,
        out_shape=(
            struct((row_count, D), bf16),
            struct((row_count, D), f32),
            struct((row_count, D), bf16),
            struct((2, row_count + 2 * HALO, D), bf16),
            struct((2 * HALO, D), bf16),
            struct((2 * HALO, RIM), bf16),
            struct((row_count, 128), f32),
        ),
        in_specs=[VMEM] * 8,
        out_specs=(VMEM,) * 7,
        scratch_shapes=[pltpu.VMEM((2 * HALO, D), bf16)],
        cost_estimate=cost(6e9, 8e6),
        name="attend",
        compiler_params=room(14),
    )(rim_low, rim_high, features, pack, mod, attn_bf, qkv, counts)

    def whole(*shape):
        return pl.BlockSpec(shape, lambda g, s: (0,) * len(shape))

    chunk_shape = struct((2, 2, 2, 128, CHUNK), bf16)
    branch, grad_second, own_kept, own_sent = pl.pallas_call(
        mlp_own_kernel,
        out_shape=(struct((row_count, D), f32), struct((row_count, D), f32), chunk_shape, chunk_shape),
        grid_spec=pltpu.PrefetchScalarGridSpec(
            num_scalar_prefetch=1,
            grid=(2,),
            in_specs=[
                whole(row_count, D),
                whole(row_count, D),
                pl.BlockSpec((D, CHUNK), lambda g, s: (0, g)),
                pl.BlockSpec((CHUNK, D), lambda g, s: (g, 0)),
            ],
            out_specs=(
                whole(row_count, D),
                whole(row_count, D),
                pl.BlockSpec((1, 2, 2, 128, CHUNK), lambda g, s: (g ^ s[1], 0, 0, 0, 0)),
                pl.BlockSpec((1, 2, 2, 128, CHUNK), lambda g, s: (g ^ s[1], 0, 0, 0, 0)),
            ),
            scratch_shapes=[pltpu.VMEM((row_count, CHUNK), bf16)] * 2,
        ),
        cost_estimate=cost(5e9, 8e6),
        name="mlp_own",
        compiler_params=room(18),
    )(scalars, second_in, cotangent, up_weight, down_weight)

    def part(away):
        return pl.BlockSpec(
            (1, 2, 2, 128, CHUNK), lambda g, s: (away ^ s[0] ^ s[1], 0, 0, 0, 0)
        )

    branch, grad_second, near_kept, near_sent = pl.pallas_call(
        mlp_near_kernel,
        out_shape=(struct((row_count, D), f32), struct((row_count, D), f32), chunk_shape, chunk_shape),
        grid_spec=pltpu.PrefetchScalarGridSpec(
            num_scalar_prefetch=1,
            grid=(1,),
            in_specs=[
                whole(row_count, D),
                whole(row_count, D),
                whole(2, D, CHUNK),
                whole(row_count, D),
                whole(row_count, D),
            ],
            out_specs=(whole(row_count, D), whole(row_count, D), part(0), part(0)),
            scratch_shapes=[pltpu.VMEM((row_count, CHUNK), bf16)] * 2,
        ),
        cost_estimate=cost(2.5e9, 4e6),
        name="mlp_near",
        compiler_params=room(14),
    )(scalars, second_in, cotangent, near, branch, grad_second)
    far = swap(after(near, own_kept), 2)
    (
        rest_kept,
        rest_sent,
        output,
        grad_stream,
        grad_attended,
        stats,
        edge_low,
        edge_high,
        table_two,
    ) = pl.pallas_call(
        mlp_far_kernel,
        out_shape=(
            chunk_shape,
            chunk_shape,
            struct((row_count, D), bf16),
            struct((row_count, D), f32),
            struct((row_count, D), bf16),
            struct((row_count, 128), f32),
            struct((HALO, D + 128), bf16),
            struct((HALO, D + 128), bf16),
            struct((8, D), f32),
        ),
        grid_spec=pltpu.PrefetchScalarGridSpec(
            num_scalar_prefetch=1,
            grid=(1,),
            in_specs=[
                whole(row_count, D),
                whole(row_count, D),
                whole(2, D, CHUNK),
                whole(row_count, D),
                whole(row_count, D),
                whole(row_count, D),
                whole(row_count, 128),
                whole(8, D),
                whole(4, D, D),
                whole(row_count, D),
                whole(row_count, 128),
                pl.BlockSpec(memory_space=pl.ANY),
                pl.BlockSpec(memory_space=pl.ANY),
            ],
            out_specs=(
                part(1),
                part(1),
                whole(row_count, D),
                whole(row_count, D),
                whole(row_count, D),
                whole(row_count, 128),
                whole(HALO, D + 128),
                whole(HALO, D + 128),
                whole(8, D),
            ),
            scratch_shapes=[
                pltpu.VMEM((row_count, D), f32),
                pltpu.VMEM((row_count, D), f32),
                pltpu.VMEM((row_count, CHUNK), bf16),
                pltpu.VMEM((row_count, CHUNK), bf16),
            ],
        ),
        input_output_aliases={12: 0, 13: 1},
        cost_estimate=cost(4e9, 8e6),
        name="mlp_far",
        compiler_params=room(22),
    )(
        scalars,
        second_in,
        cotangent,
        far,
        branch,
        grad_second,
        stream,
        pack,
        mod,
        attn_bf,
        attended,
        log_totals,
        near_kept,
        near_sent,
    )

    grad_low = along(edge_high, 1)
    grad_high = along(edge_low, -1)

    def kept_of(first, second):
        return jnp.where(is_first, first, second)

    own_sum = own_kept.astype(f32) + swap(own_sent, 2).astype(f32)
    rest_sum = rest_kept.astype(f32) + swap(rest_sent, 2).astype(f32)

    def parted(total):
        return total[0], total[1].astype(bf16)

    def spread_out(keep):
        mask = 32
        while mask < device_count:
            rounded = keep.astype(bf16)
            keep = rounded.astype(f32) + swap(rounded, mask).astype(f32)
            mask *= 2
        return keep

    blend_rate = 1.0 + momentum_rate
    past_rate = momentum_rate * momentum_rate
    large_routes = ((4, 8), (1, 4), (8, 1), (16, 16))
    large_keep = kept_of(
        jnp.stack([own_sum[0], rest_sum[0]]),
        jnp.stack([own_sum[:, 0], rest_sum[:, 0]], axis=1),
    )
    large_send = kept_of(
        jnp.stack([own_sum[1], rest_sum[1]]),
        jnp.stack([own_sum[:, 1], rest_sum[:, 1]], axis=1),
    )
    large_send = large_send.astype(bf16)

    padded_rows = row_count + 2 * HALO
    half_blocks = row_count // BLOCK // 2
    totals_shape = (struct((row_count // 2, D), bf16),) + (struct((padded_rows, D), f32),) * 2
    early, keys_total, values_total = pl.pallas_call(
        functools.partial(backward_kernel, 0, half_blocks),
        out_shape=totals_shape,
        in_specs=[VMEM] * 5,
        out_specs=(VMEM,) * 3,
        cost_estimate=cost(4e9, 9e6),
        name="attend_back",
        compiler_params=room(14),
    )(after(qkv, large_send), padded, grad_attended, stats, counts)
    late, keys_total, values_total = pl.pallas_call(
        functools.partial(backward_kernel, half_blocks, 2 * half_blocks),
        out_shape=totals_shape,
        in_specs=[VMEM] * 7,
        out_specs=(VMEM,) * 3,
        input_output_aliases={5: 1, 6: 2},
        cost_estimate=cost(4e9, 9e6),
        name="attend_back",
        compiler_params=room(14),
    )(qkv, padded, grad_attended, stats, counts, keys_total, values_total)
    def received(total, got):
        return total + got.astype(f32)

    large_got = swap(large_send, *large_routes[0])
    large_keep, large_send = parted(received(large_keep, after(large_got, late)))
    large_got = swap(large_send, *large_routes[1])
    piece_shape = struct((2, 2, 2, 2, 80, D), bf16)
    features_grad, small_kept, small_sent = pl.pallas_call(
        weights_kernel,
        out_shape=(struct((row_count, D), f32), piece_shape, piece_shape),
        in_specs=[SMEM] + [VMEM] * 17,
        out_specs=(VMEM,) * 3,
        scratch_shapes=[
            pltpu.VMEM((4, row_count, D), bf16),
            pltpu.VMEM((8, D), f32),
            pltpu.VMEM((row_count, D), f32),
            pltpu.VMEM((row_count, D), f32),
        ],
        cost_estimate=cost(6e9, 9e6),
        name="attend_weights",
        compiler_params=room(18),
    )(
        scalars,
        early,
        after(late, large_send),
        keys_total,
        values_total,
        padded,
        rim_queries,
        rim_counts,
        grad_low,
        grad_high,
        first_in,
        attended,
        grad_stream,
        features,
        pack,
        mod,
        attn_bf,
        table_two,
    )
    small_got = swap(small_sent, 2)
    small_routes = ((1, 4), (4, 8), (8, 1), (16, 16))
    large_keep, large_send = parted(received(large_keep, after(large_got, small_sent)))
    large_got = swap(large_send, *large_routes[2])
    small_keep, small_send = parted(small_kept.astype(f32) + after(small_got, large_send).astype(f32))
    small_got = swap(small_send, *small_routes[0])
    large_keep, large_send = parted(received(large_keep, after(large_got, small_send)))
    large_got = swap(large_send, *large_routes[3])
    small_keep, small_send = parted(received(small_keep, after(small_got, large_send)))
    small_got = swap(small_send, *small_routes[1])
    large_shard = spread_out(received(large_keep, after(large_got, small_send)))
    large_part = (blend_rate * large_shard + past_rate * large_past).astype(bf16)

    def joined(part, got):
        return jnp.stack([part, got])

    large_got = swap(large_part, *large_routes[3])
    small_keep, small_send = parted(received(small_keep, after(small_got, large_part)))
    small_got = swap(small_send, *small_routes[2])
    large_part = joined(large_part, after(large_got, small_send))
    large_got = swap(large_part, *large_routes[2])
    small_keep, small_send = parted(received(small_keep, after(small_got, large_part)))
    small_got = swap(small_send, *small_routes[3])
    large_part = joined(large_part, after(large_got, small_send))
    large_got = swap(large_part, *large_routes[1])
    small_shard = spread_out(received(small_keep, after(small_got, large_part)))
    small_part = jnp.concatenate(
        [
            (blend_rate * small_shard[:64] + past_rate * small_past).astype(bf16),
            small_shard[64:].astype(bf16),
        ]
    )
    small_got = swap(small_part, *small_routes[3])
    large_part = joined(large_part, after(large_got, small_part))
    large_got = swap(large_part, *large_routes[0])
    small_part = joined(small_part, after(small_got, large_part))
    small_got = swap(small_part, *small_routes[2])
    small_part = joined(small_part, small_got)
    small_got = swap(small_part, *small_routes[1])

    large_work, large_mix, ready = pl.pallas_call(
        large_first_kernel,
        out_shape=(
            struct((4, D, CHUNK), bf16),
            struct((2, D, CHUNK), bf16),
            struct((8, 128), f32),
        ),
        in_specs=[SMEM, VMEM, VMEM],
        out_specs=(VMEM,) * 3,
        scratch_shapes=[pltpu.VMEM((D, D), bf16)],
        cost_estimate=cost(5e9, 6e6),
        name="ortho_large",
        compiler_params=room(12),
    )(scalars, after(large_part, small_part), large_got)
    mix_got = swap(large_mix, 2)
    small_part = joined(small_part, after(small_got, ready))
    small_got = swap(small_part, *small_routes[0])
    large_result = pl.pallas_call(
        large_next_kernel,
        out_shape=struct((2, D, CHUNK), bf16),
        in_specs=[VMEM],
        out_specs=VMEM,
        scratch_shapes=[pltpu.VMEM((4, D, CHUNK), bf16), pltpu.VMEM((D, D), bf16)],
        cost_estimate=cost(5e9, 4e6),
        name="ortho_large",
        compiler_params=room(12),
    )(after(large_work, small_part))
    result_got = swap(large_result, 2)

    across = pl.BlockSpec((1, D, CHUNK), lambda g: (g, 0, 0))
    left_right = pl.BlockSpec((D, CHUNK), lambda g: (0, g))
    top_bottom = pl.BlockSpec((CHUNK, D), lambda g: (g, 0))

    def update_large(kernel, own, other, first, second, name):
        return pl.pallas_call(
            kernel,
            grid=(2,),
            out_shape=(struct((D, 2 * CHUNK), f32), struct((2 * CHUNK, D), f32)),
            in_specs=[SMEM, across, across, left_right, top_bottom],
            out_specs=(left_right, top_bottom),
            cost_estimate=cost(1e7, 1e7),
            name=name,
            compiler_params=room(14),
        )(scalars, own, other, first, second)

    up_moment_new, down_moment_new = update_large(
        large_moment_kernel, large_mix, after(mix_got, large_result), up_moment, down_moment, "moment_large"
    )
    small_work, small_mix, table_own = pl.pallas_call(
        small_start_kernel,
        out_shape=(
            struct((2, 2, 256, D), bf16),
            struct((2, 256, D), bf16),
            struct((8, D), f32),
        ),
        in_specs=[SMEM, VMEM, VMEM],
        out_specs=(VMEM,) * 3,
        cost_estimate=cost(1e6, 4e6),
        name="unpack_small",
        compiler_params=room(6),
    )(scalars, after(small_part, up_moment_new), small_got)
    small_result = pl.pallas_call(
        small_kernel,
        out_shape=struct((2, 256, D), bf16),
        in_specs=[VMEM],
        out_specs=VMEM,
        scratch_shapes=[pltpu.VMEM((2, 256, D), bf16)] * 2 + [pltpu.VMEM((D, D), bf16)] * 2,
        cost_estimate=cost(6e9, 4e6),
        name="ortho_small",
        compiler_params=room(10),
    )(small_work)
    small_other = swap(small_result, 2)
    mix_other = swap(small_mix, 2)
    table_other = swap(table_own, 2)
    up_new, down_new = update_large(
        large_weight_kernel,
        large_result,
        after(result_got, small_result),
        up_weight,
        down_weight,
        "update_large",
    )

    def per_matrix(index):
        return pl.BlockSpec((1, 256, D), index)

    def update_small(kernel, own, other, held, index, name):
        return pl.pallas_call(
            kernel,
            grid_spec=pltpu.PrefetchScalarGridSpec(
                num_scalar_prefetch=1,
                grid=(4,),
                in_specs=[
                    per_matrix(lambda g, s: (g % 2, 0, 0)),
                    per_matrix(lambda g, s: (g % 2, 0, 0)),
                    per_matrix(index),
                ],
                out_specs=per_matrix(lambda g, s: (g, 0, 0)),
            ),
            out_shape=struct((4, 256, D), f32),
            cost_estimate=cost(1e7, 6e6),
            name=name,
            compiler_params=room(6),
        )(scalars, own, other, held)

    attention_moment_new = update_small(
        small_moment_kernel, small_mix, after(mix_other, small_result), attention_moment, lambda g, s: (g, 0, 0), "moment_small"
    )
    attention_new = update_small(
        small_weight_kernel,
        small_result,
        after(small_other, attention_moment_new, up_new),
        attention_weight,
        lambda g, s: (g, s[4], 0),
        "update_small",
    )
    modulation_moment_new, modulation_new = pl.pallas_call(
        functools.partial(table_kernel, nodes=row_count * device_count),
        out_shape=(struct((2, 2, D), f32),) * 2,
        in_specs=[SMEM] + [VMEM] * 4,
        out_specs=(VMEM,) * 2,
        cost_estimate=cost(1e4, 1e5),
        name="update_table",
        compiler_params=room(2),
    )(scalars, table_own, after(table_other, small_result), held, modulation_moment)
    return (
        output,
        features_grad,
        attention_moment_new,
        attention_new,
        up_moment_new,
        up_new,
        down_moment_new,
        down_new,
        modulation_moment_new,
        modulation_new,
    )


def solution(mesh):
    placed = (
        P(("nodes", "hid"), None),
        P(("nodes", "hid")),
        P(("nodes", "hid"), None),
        P(("nodes", "hid")),
        P(("nodes", "hid"), None),
        P(),
        P(None, "hid"),
        P("hid", None),
        P(),
        P(None, "hid", None),
        P(None, "hid"),
        P("hid", None),
        P(None, "hid", None),
    )
    return jax.shard_map(
        on_device,
        mesh=mesh,
        in_specs=placed,
        out_specs=(
            P(("nodes", "hid"), None),
            P(("nodes", "hid"), None),
            P(None, "hid", None),
            P(None, "hid", None),
            P(None, "hid"),
            P(None, "hid"),
            P("hid", None),
            P("hid", None),
            P(None, "hid", None),
            P(None, "hid", None),
        ),
        check_vma=False,
    )
```

```python
import functools
import math

import jax
import jax.numpy as jnp
from jax import lax
from jax.experimental import pallas as pl
from jax.experimental.pallas import tpu as pltpu
from jax.sharding import PartitionSpec as P

D = 512
HEADS = 4
HD = 128
FF = 2048
K = 16
NS_STEPS = 4
HALO = 192
BLOCK = 128
SPAN = BLOCK + 2 * HALO
RIM = 256
CHUNK = 512
TABLE_ROWS = 16

f32 = jnp.float32
bf16 = jnp.bfloat16
ns_first = 3.4445
ns_second = -4.775
ns_third = 2.0315
momentum_rate = 0.95
vector_rate = 0.9
muon_rate = 0.2
decay_rate = 0.1
score_scale = 1.0 / math.sqrt(HD)
AXES = ("nodes", "hid")
VMEM = pl.BlockSpec(memory_space=pltpu.VMEM)
SMEM = pl.BlockSpec(memory_space=pltpu.SMEM)


def nn(a, b):
    return lax.dot_general(a, b, (((1,), (0,)), ((), ())), preferred_element_type=f32)


def nt(a, b):
    return lax.dot_general(a, b, (((1,), (1,)), ((), ())), preferred_element_type=f32)


def tn(a, b):
    return lax.dot_general(a, b, (((0,), (0,)), ((), ())), preferred_element_type=f32)


def struct(shape, dtype):
    return jax.ShapeDtypeStruct(shape, dtype)


def rows_of(start, size):
    return pl.ds(pl.multiple_of(start, size), size)


def cost(flops, data):
    return pl.CostEstimate(flops=int(flops), bytes_accessed=int(data), transcendentals=0)


def room(mebibytes):
    return pltpu.CompilerParams(vmem_limit_bytes=mebibytes << 20)


def norm_parts(field):
    average = jnp.mean(field, axis=-1, keepdims=True)
    centred = field - average
    variance = jnp.mean(centred * centred, axis=-1, keepdims=True)
    inverse = lax.rsqrt(variance + 1e-06)
    return centred * inverse, inverse


def table_rows(mod_ref, level, column):
    return jnp.where(level > 0.5, mod_ref[1, column : column + 1, :], mod_ref[0, column : column + 1, :])


def modulated(field, level, mod_ref, column):
    normed, _ = norm_parts(field)
    return normed * (1.0 + table_rows(mod_ref, level, column)) + table_rows(
        mod_ref, level, column + 1
    )


def norm_back(grad_out, field, level, mod_ref, column):
    normed, inverse = norm_parts(field)
    grad_norm = grad_out * (1.0 + table_rows(mod_ref, level, column))
    grad_in = inverse * (
        grad_norm
        - jnp.mean(grad_norm, axis=-1, keepdims=True)
        - normed * jnp.mean(grad_norm * normed, axis=-1, keepdims=True)
    )
    return grad_in, grad_out * normed


def add_table(table_ref, column, level, scale_term, shift_term):
    upper = level > 0.5
    for term, place in ((scale_term, column), (shift_term, column + 1)):
        low_part = jnp.sum(jnp.where(upper, 0.0, term), axis=0, keepdims=True)
        high_part = jnp.sum(jnp.where(upper, term, 0.0), axis=0, keepdims=True)
        table_ref[place : place + 1, :] += low_part
        table_ref[4 + place : 5 + place, :] += high_part


def slot_counts(pack, row_count, width, shift):
    pieces = []
    for left in range(0, width, 128):
        lanes = lax.broadcasted_iota(jnp.int32, (row_count, 128), 1)
        rows = lax.broadcasted_iota(jnp.int32, (row_count, 128), 0)
        place = (lanes - rows + (left - shift)).astype(f32)
        total = jnp.zeros((row_count, 128), f32)
        for slot in range(K):
            total = total + jnp.where(place == pack[:, slot : slot + 1], 1.0, 0.0)
        pieces.append(total)
    return jnp.concatenate(pieces, axis=1).astype(bf16)


def quarter_kernel(scalars, up, down, rounded):
    rounded[0] = up[...].astype(bf16)
    rounded[1] = down[...].astype(bf16)


def past_kernel(scalars, up, down, attention, large_past, small_past):
    large_past[...] = jnp.where(scalars[0] == 0, up[...], down[...].T)
    small_past[...] = attention[0]


def project_kernel(features, pack, mod, weights, first_in, qkv, counts, rounded):
    row_count = features.shape[0]
    turn = pl.program_id(0)

    @pl.when(turn == 0)
    def _():
        for start in range(0, row_count, 256):
            rows = slice(start, start + 256)
            level = pack[rows, K : K + 1]
            first_in[rows, :] = modulated(features[rows, :].astype(f32), level, mod, 0).astype(bf16)

    weight = weights[0].astype(bf16)
    rounded[0] = weight

    @pl.when(turn < 3)
    def _():
        qkv[turn] = nn(first_in[...], weight).astype(bf16)
        share = row_count // BLOCK // 3

        def count_step(b, carry):
            rows = rows_of(b * BLOCK, BLOCK)
            counts[rows, :] = slot_counts(pack[rows, :], BLOCK, SPAN, HALO)
            return carry

        lax.fori_loop(turn * share, (turn + 1) * share, count_step, 0)


def forward_kernel(
    rim_low,
    rim_high,
    features,
    pack,
    mod,
    weights,
    qkv,
    counts,
    attended,
    stream,
    second_in,
    padded,
    rim_queries,
    rim_counts,
    log_totals,
    rim_in,
):
    row_count = features.shape[0]
    for side, rim in enumerate((rim_low, rim_high)):

        def rim_step(b, carry):
            rows = rows_of(b * 64, 64)
            target = pl.ds(pl.multiple_of(side * HALO + b * 64, 64), 64)
            info = rim[rows, D:].astype(f32)
            rim_in[target, :] = modulated(
                rim[rows, :D].astype(f32), info[:, K : K + 1], mod, 0
            ).astype(bf16)
            rim_counts[target, :] = slot_counts(
                info, 64, RIM, b * 64 + (-HALO if side == 0 else RIM)
            )
            return carry

        lax.fori_loop(0, HALO // 64, rim_step, 0)
    rim_queries[...] = nn(rim_in[...], weights[0]).astype(bf16)
    for p in range(2):
        piece = nn(rim_in[...], weights[1 + p]).astype(bf16)
        padded[p, :HALO, :] = piece[:HALO]
        padded[p, HALO + row_count :, :] = piece[HALO:]
        padded[p, HALO : HALO + row_count, :] = qkv[1 + p]

    def step(b, carry):
        rows = rows_of(b * BLOCK, BLOCK)
        span = pl.ds(pl.multiple_of(b * BLOCK, BLOCK), SPAN)
        count = counts[rows, :].astype(f32)
        live = count > 0.0
        columns = [slice(h * HD, (h + 1) * HD) for h in range(HEADS)]
        scores = [nt(qkv[0, rows, cols], padded[0, span, cols]) * score_scale for cols in columns]
        lanes = lax.broadcasted_iota(jnp.int32, (BLOCK, 128), 1)
        stats = jnp.zeros((BLOCK, 128), f32)
        for h, cols in enumerate(columns):
            masked = jnp.where(live, scores[h], -1e30)
            peak = jnp.max(masked, axis=-1, keepdims=True)
            exponent = jnp.exp(masked - peak)
            total = jnp.sum(exponent * count, axis=-1, keepdims=True)
            probs = (exponent / total).astype(bf16)
            spread = (probs.astype(f32) * count).astype(bf16)
            attended[rows, cols] = nn(spread, padded[1, span, cols]).astype(bf16)
            stats = jnp.where(lanes == h, peak + jnp.log(total), stats)
        log_totals[rows, :] = stats
        return carry

    lax.fori_loop(0, row_count // BLOCK, step, 0)
    for start in range(0, row_count, 256):
        rows = slice(start, start + 256)
        field = features[rows, :].astype(f32) + nn(attended[rows, :], weights[3])
        stream[rows, :] = field
        second_in[rows, :] = modulated(field, pack[rows, K : K + 1], mod, 2).astype(bf16)


def mlp_chunk(
    scalars, second_in, cotangent, up, down, branch_in, grad_in, branch, grad_second, acts, grads, kept, sent
):
    row_count = second_in.shape[0]
    for start in range(0, row_count, 256):
        rows = slice(start, start + 256)
        preact = nn(second_in[rows, :], up)
        grad_act = nt(cotangent[rows, :], down)
        sigmoid = 0.5 * jnp.tanh(0.5 * preact) + 0.5
        act = (preact * sigmoid).astype(bf16)
        acts[rows, :] = act
        grad_pre = (grad_act * (sigmoid * (1.0 + preact * (1.0 - sigmoid)))).astype(bf16)
        grads[rows, :] = grad_pre
        branch[rows, :] = branch_in[rows, :] + nn(act, down)
        grad_second[rows, :] = grad_in[rows, :] + nt(grad_pre, up)
    first, z1, z2 = scalars[0] == 0, scalars[2], scalars[3]
    for out, swapped in ((kept, False), (sent, True)):
        ups = jnp.logical_not(first) if swapped else first
        product = tn(
            jnp.where(ups, second_in[...], cotangent[...]), jnp.where(ups, grads[...], acts[...])
        )
        for q in range(4):
            out[0, (q // 2) ^ z1, (q % 2) ^ z2] = product[q * 128 : (q + 1) * 128].astype(bf16)


def mlp_own_kernel(
    scalars, second_in, cotangent, up, down, branch, grad_second, kept, sent, acts, grads
):
    @pl.when(pl.program_id(0) == 0)
    def _():
        branch[...] = jnp.zeros_like(branch)
        grad_second[...] = jnp.zeros_like(grad_second)

    mlp_chunk(
        scalars,
        second_in,
        cotangent,
        up[...].astype(bf16),
        down[...].astype(bf16),
        branch,
        grad_second,
        branch,
        grad_second,
        acts,
        grads,
        kept,
        sent,
    )


def mlp_near_kernel(
    scalars, second_in, cotangent, near, branch_in, grad_in, branch, grad_second, kept, sent, acts, grads
):
    mlp_chunk(
        scalars,
        second_in,
        cotangent,
        near[0],
        near[1],
        branch_in,
        grad_in,
        branch,
        grad_second,
        acts,
        grads,
        kept,
        sent,
    )


def mlp_far_kernel(
    scalars,
    second_in,
    cotangent,
    far,
    branch_in,
    grad_in,
    stream,
    pack,
    mod,
    weights,
    attended,
    log_totals,
    kept_in,
    sent_in,
    kept,
    sent,
    output,
    grad_stream,
    grad_attended,
    stats,
    edge_low,
    edge_high,
    table,
    branch,
    grad_second,
    acts,
    grads,
):
    row_count = second_in.shape[0]
    mlp_chunk(
        scalars,
        second_in,
        cotangent,
        far[0],
        far[1],
        branch_in,
        grad_in,
        branch,
        grad_second,
        acts,
        grads,
        kept,
        sent,
    )
    table[...] = jnp.zeros_like(table)

    for start in range(0, row_count, 256):
        rows = slice(start, start + 256)
        field = stream[rows, :]
        level = pack[rows, K : K + 1]
        output[rows, :] = (field + branch[rows, :]).astype(bf16)
        gradient = grad_second[rows, :]
        grad_field, scale_term = norm_back(gradient, field, level, mod, 2)
        add_table(table, 2, level, scale_term, gradient)
        total = cotangent[rows, :].astype(f32) + grad_field
        grad_stream[rows, :] = total
        back = nt(total.astype(bf16), weights[3]).astype(bf16)
        grad_attended[rows, :] = back
        product = back.astype(f32) * attended[rows, :].astype(f32)
        lanes = lax.broadcasted_iota(jnp.int32, (256, 128), 1)
        kept_stats = log_totals[rows, :]
        for h in range(HEADS):
            delta = jnp.sum(product[:, h * HD : (h + 1) * HD], axis=-1, keepdims=True)
            kept_stats = jnp.where(lanes == HEADS + h, delta, kept_stats)
        stats[rows, :] = kept_stats
    for edge, first in ((edge_low, 0), (edge_high, row_count - HALO)):
        rows = slice(first, first + HALO)
        edge[:, :D] = grad_attended[rows, :]
        known = stats[rows, :]
        upper = known.astype(bf16)
        lower = (known - upper.astype(f32)).astype(bf16).astype(f32)
        edge[:, D:] = (upper.astype(f32) + pltpu.roll(lower, 2 * HEADS, 1)).astype(bf16)


def attention_terms(scores, grad_probs, count, log_total, delta):
    probs = jnp.exp(jnp.where(count > 0.0, scores * score_scale, -1e30) - log_total)
    slopes = (probs * (grad_probs - delta)).astype(bf16).astype(f32)
    spread = (probs.astype(bf16).astype(f32) * count).astype(bf16)
    return (slopes * count).astype(bf16), spread


def backward_kernel(qkv, padded, grad, stats, counts, token, grad_query, keys_total, values_total):
    keys_total[...] = jnp.zeros_like(keys_total)
    values_total[...] = jnp.zeros_like(values_total)

    def step(b, carry):
        rows = rows_of(b * BLOCK, BLOCK)
        span = pl.ds(pl.multiple_of(b * BLOCK, BLOCK), SPAN)
        count = counts[rows, :].astype(f32)
        columns = [slice(h * HD, (h + 1) * HD) for h in range(HEADS)]
        products = [
            (nt(qkv[0, rows, cols], padded[0, span, cols]), nt(grad[rows, cols], padded[1, span, cols]))
            for cols in columns
        ]
        terms = [
            attention_terms(
                *products[h],
                count,
                stats[rows, h : h + 1],
                stats[rows, HEADS + h : HEADS + h + 1],
            )
            for h in range(HEADS)
        ]
        for (slopes, spread), cols in zip(terms, columns):
            grad_query[rows, cols] = (nn(slopes, padded[0, span, cols]) * score_scale).astype(bf16)
            keys_total[span, cols] += tn(slopes, qkv[0, rows, cols])
            values_total[span, cols] += tn(spread, grad[rows, cols])
        return carry

    lax.fori_loop(0, counts.shape[0] // BLOCK, step, 0)


def weights_kernel(
    scalars,
    token,
    queries_in,
    keys_in,
    values_in,
    padded,
    rim_query,
    rim_counts,
    grad_low,
    grad_high,
    first_in,
    attended,
    grad_stream,
    features,
    pack,
    mod,
    weights,
    table_two,
    features_grad,
    kept,
    sent,
    gathered,
    table,
    keys_total,
    values_total,
    blocks,
):
    row_count = first_in.shape[0]
    columns = [slice(h * HD, (h + 1) * HD) for h in range(HEADS)]
    own = slice(HALO, HALO + row_count)
    keys_total[...] = keys_in[own, :]
    values_total[...] = values_in[own, :]
    for side, grads in enumerate((grad_low, grad_high)):
        first = 0 if side == 0 else row_count - RIM
        own_span = slice(first, first + RIM)
        span = slice(HALO + first, HALO + first + RIM)
        rows = slice(side * HALO, (side + 1) * HALO)
        known = grads[:, D:].astype(f32)
        count = rim_counts[rows, :].astype(f32)
        products = [
            (nt(rim_query[rows, cols], padded[0, span, cols]), nt(grads[:, cols], padded[1, span, cols]))
            for cols in columns
        ]
        terms = []
        for h in range(HEADS):
            numbers = [known[:, i * HEADS + h : i * HEADS + h + 1] for i in range(4)]
            terms.append(
                attention_terms(*products[h], count, numbers[0] + numbers[2], numbers[1] + numbers[3])
            )
        for (slopes, spread), cols in zip(terms, columns):
            keys_total[own_span, cols] += tn(slopes, rim_query[rows, cols])
            values_total[own_span, cols] += tn(spread, grads[:, cols])
    gathered[0] = queries_in[...]
    gathered[1] = (keys_total[...] * score_scale).astype(bf16)
    gathered[2] = values_total[...].astype(bf16)
    table[...] = table_two[...]
    for start in range(0, row_count, 256):
        rows = slice(start, start + 256)
        level = pack[rows, K : K + 1]
        gradient = nt(gathered[0, rows, :], weights[0])
        for p in range(1, 3):
            gradient = gradient + nt(gathered[p, rows, :], weights[p])
        grad_field, scale_term = norm_back(gradient, features[rows, :].astype(f32), level, mod, 0)
        add_table(table, 0, level, scale_term, gradient)
        total = grad_stream[rows, :]
        features_grad[rows, :] = total + grad_field
        gathered[3, rows, :] = total.astype(bf16)
    core, slot_bit, z1, z2, hid = (scalars[i] for i in range(5))

    def product_step(n, carry):
        away, slot = n // 2, n % 2
        target = core ^ away
        p = 2 * target + slot
        product = tn(jnp.where(p < 3, first_in[...], attended[...]), gathered[p])
        for half in range(2):
            for q in range(4):
                slot_at, hid_at, row_half = slot ^ slot_bit, half ^ hid, (q // 2) ^ z1
                index = (
                    away,
                    jnp.where(target == 0, hid_at, slot_at),
                    jnp.where(target == 0, slot_at, row_half),
                    jnp.where(target == 0, row_half, hid_at),
                    (q % 2) ^ z2,
                )
                start = half * 256 + q * 64
                blocks[index + (slice(0, 64),)] = product[start : start + 64].astype(bf16)
                row = (q // 2) * 4 + 2 * half + q % 2
                known = jnp.broadcast_to(table[row : row + 1, :], (TABLE_ROWS, D))
                blocks[index + (slice(64, 80),)] = jnp.where(p == 0, known, 0.0).astype(bf16)
        return carry

    lax.fori_loop(0, 4, product_step, 0)
    kept[...] = blocks[0]
    sent[...] = blocks[1]


def large_sum_kernel(scalars, own, own_got, rest, rest_got, keep, send):
    first = scalars[0] == 0
    for away, out in ((0, keep), (1, send)):
        for source, got, h in ((own, own_got, 0), (rest, rest_got, 1)):
            for i in range(2):
                where_from = (jnp.where(first, away, i), jnp.where(first, i, away))
                where_to = (jnp.where(first, h, i), jnp.where(first, i, h))
                total = source[where_from].astype(f32) + got[where_from].astype(f32)
                out[where_to] = total.astype(out.dtype)


def receive_kernel(*refs):
    kept, got, keep, send = refs[0], refs[1], refs[-2], refs[-1]
    keep[...] = kept[0].astype(f32) + got[0].astype(f32)
    send[...] = (kept[1].astype(f32) + got[1].astype(f32)).astype(bf16)


def blend_kernel(*refs):
    kept, got, past, part = refs[0], refs[1], refs[2], refs[-1]
    rows = past.shape[0]
    total = kept[...] + got[...].astype(f32)
    blended = (1.0 + momentum_rate) * total[:rows] + momentum_rate * momentum_rate * past[...]
    part[:rows, :] = blended.astype(bf16)
    if rows < part.shape[0]:
        part[rows:, :] = total[rows:].astype(bf16)


def join_kernel(*refs):
    part, got, pieces = refs[0], refs[1], refs[-1]
    pieces[0] = part[...]
    pieces[1] = got[...]


def newton_schulz(groups, polys, rows_first, scales):
    blocks = [[[ref[i] for i in half] for half in halves] for ref, halves in groups]
    grams = []
    for halves, scale in zip(blocks, scales):
        sums = []
        for half in halves:
            total = None
            for block in half:
                term = tn(block, block) if rows_first else nt(block, block)
                total = term if total is None else total + term
            sums.append((total if scale is None else total * (scale * scale)).astype(bf16))
        grams.append((sums[0].astype(f32) + sums[1].astype(f32)).astype(bf16))
    for gram, poly in zip(grams, polys):
        poly[...] = (ns_second * gram.astype(f32) + ns_third * nn(gram, gram)).astype(bf16)
    for (ref, halves), values, poly, scale in zip(groups, blocks, polys, scales):
        for half, half_values in zip(halves, values):
            for i, block in zip(half, half_values):
                other = nn(block, poly[...]) if rows_first else nn(poly[...], block)
                total = ns_first * block.astype(f32) + other
                ref[i] = (total if scale is None else total * scale).astype(bf16)


def large_start_kernel(scalars, kept, got, work, poly):
    core, slot_bit, z1, z2 = (scalars[i] for i in range(4))
    total = jnp.zeros((8, D), f32)
    for n in range(16):
        b1, b2, b3, b4 = n // 8, (n // 4) % 2, (n // 2) % 2, n % 2
        source = kept if b1 == 0 else got
        block = source[b2, b3, b4]
        value = block.astype(f32)
        total = total + jnp.sum((value * value).reshape(16, 8, D), axis=0)
        slot = jnp.where(core == 0, b1, b2)
        half = jnp.where(core == 0, b2, b3)
        row_half = jnp.where(core == 0, b3, b1)
        start = ((row_half ^ z1) * 2 + (b4 ^ z2)) * 128
        work[half * 2 + (slot ^ slot_bit), rows_of(start, 128), :] = block
    return 1.0 / (jnp.sqrt(jnp.sum(total)) + 1e-07)


large_halves = ((0, 1), (2, 3))


def large_first_kernel(scalars, kept, got, token, work, blend, poly):
    scale = large_start_kernel(scalars, kept, got, work, poly)
    for s in range(2):
        blend[s] = work[s]

    def step(i, factor):
        newton_schulz([(work, large_halves)], [poly], False, [factor])
        return jnp.ones((), f32)

    lax.fori_loop(0, NS_STEPS // 2, step, scale)


def large_next_kernel(given, token, result, work, poly):
    work[...] = given[...]

    def step(i, carry):
        newton_schulz([(work, large_halves)], [poly], False, [None])
        return carry

    lax.fori_loop(NS_STEPS // 2, NS_STEPS, step, 0)
    for s in range(2):
        result[s] = work[s]


def small_start_kernel(scalars, kept, got, token, work, blend, table):
    core, slot_bit, z1, z2 = (scalars[i] for i in range(4))
    for n in range(16):
        b1, b2, b3, b4 = n // 8, (n // 4) % 2, (n // 2) % 2, n % 2
        source = kept if b1 == 0 else got
        block = source[b2, b3, b4]
        slot = jnp.where(core == 0, b2, b1) ^ slot_bit
        half = jnp.where(core == 0, b1, b3)
        row_half = jnp.where(core == 0, b3, b2)
        quarter = (row_half ^ z1) * 2 + (b4 ^ z2)
        work[slot, half, rows_of(quarter * 64, 64), :] = block[:64]

        @pl.when((half == 0) & (slot == 0))
        def _():
            table[pl.ds(quarter, 1), :] = block[64:].astype(f32)[:1]

    table[4:, :] = jnp.zeros((4, D), f32)
    for s in range(2):
        blend[s] = work[s, 0]


def small_kernel(given, result, first, second, poly_first, poly_second):
    works = (first, second)
    scales = []
    for s, work in enumerate(works):
        total = jnp.zeros((8, D), f32)
        for half in range(2):
            block = given[s, half]
            work[half] = block
            value = block.astype(f32)
            total = total + jnp.sum((value * value).reshape(32, 8, D), axis=0)
        scales.append(1.0 / (jnp.sqrt(jnp.sum(total)) + 1e-07))
    groups = [(work, ((0,), (1,))) for work in works]
    polys = [poly_first, poly_second]

    def step(i, factors):
        newton_schulz(groups, polys, True, factors)
        return (jnp.ones((), f32),) * 2

    lax.fori_loop(0, NS_STEPS, step, tuple(scales))
    for s, work in enumerate(works):
        result[s] = work[0]


def new_moment(blend, moment):
    share = 1.0 / (1.0 + momentum_rate)
    return share * blend + (momentum_rate - share * momentum_rate * momentum_rate) * moment


def new_weight(weight, ortho, longest):
    return weight - muon_rate * (0.2 * math.sqrt(longest) * ortho + decay_rate * weight)


def large_moment_kernel(scalars, own, got, up_moment, down_moment, token, up_moment_new, down_moment_new, done):
    done[...] = jnp.zeros_like(done)
    first = scalars[0] == 0
    mine, other = own[0].astype(f32), got[0].astype(f32)
    up_moment_new[...] = new_moment(jnp.where(first, mine, other), up_moment[...])
    down_moment_new[...] = new_moment(jnp.where(first, other, mine).T, down_moment[...])


def large_weight_kernel(
    scalars,
    own,
    got,
    up_weight,
    down_weight,
    mix,
    mix_got,
    moment,
    table,
    table_got,
    modulation,
    held_moment,
    token,
    up_new,
    down_new,
    moment_new,
    held_moment_new,
    held_new,
    done,
    *,
    nodes,
):
    done[...] = jnp.zeros_like(done)
    core, turn = scalars[0], pl.program_id(0)
    first = core == 0
    mine, other = own[0].astype(f32), got[0].astype(f32)
    up_new[...] = new_weight(up_weight[...], jnp.where(first, mine, other), FF)
    down_new[...] = new_weight(down_weight[...], jnp.where(first, other, mine).T, FF)
    blend = jnp.where(core == turn // 2, mix[0].astype(f32), mix_got[0].astype(f32))
    moment_new[0] = new_moment(blend, moment[0])

    @pl.when(turn == 0)
    def _():
        total = jnp.where(first, table[...], table_got[...])
        for level in range(2):
            for column in range(2):
                row = level * 2 + column
                at = (slice(level, level + 1), slice(column, column + 1))
                value = vector_rate * held_moment[at] + total[row : row + 1, :].reshape(1, 1, D)
                held = modulation[level : level + 1, pl.ds(scalars[4] * 2 + column, 1)]
                held_moment_new[at] = value
                held_new[at] = held - 0.2 / math.sqrt(nodes) * value


def small_weight_kernel(scalars, own, got, weight, token, weight_new):
    mine = scalars[0] == pl.program_id(0) // 2
    ortho = jnp.where(mine, own[0].astype(f32), got[0].astype(f32))
    weight_new[0] = new_weight(weight[0], ortho, D)


def on_device(
    features,
    levels,
    neighbour_index,
    neighbour_count,
    cotangent,
    attention_weight,
    up_weight,
    down_weight,
    modulation,
    attention_moment,
    up_moment,
    down_moment,
    modulation_moment,
):
    row_count = features.shape[0]
    device_count = lax.axis_size(AXES)
    me = lax.axis_index(AXES)
    first_row = me * row_count

    def bit(place):
        return (me >> place) & 1

    hid, core, slot_bit, z1, z2 = (bit(place) for place in range(5))
    scalars = jnp.stack([core, slot_bit, z1, z2, hid]).astype(jnp.int32)
    is_first = core == 0

    def along(value, distance):
        pairs = [(i, i + distance) for i in range(device_count) if 0 <= i + distance < device_count]
        return lax.ppermute(value, AXES, pairs)

    def after(value, *others):
        return lax.optimization_barrier((value,) + others)[0]

    def swap(value, mask, other=None):
        masks = (mask, mask if other is None else other)
        pairs = [(i, i ^ masks[(i // 2) % 2]) for i in range(device_count)]
        return lax.ppermute(value, AXES, pairs)

    live = jnp.arange(K, dtype=jnp.int32)[None, :] < neighbour_count[:, None]
    row_ids = first_row + jnp.arange(row_count, dtype=jnp.int32)[:, None]
    offsets = jnp.where(live, neighbour_index - row_ids, 512)
    pack = jnp.concatenate(
        [offsets, levels[:, None], jnp.zeros((row_count, 128 - K - 1), jnp.int32)], axis=1
    ).astype(f32)
    rims = jnp.concatenate([features, pack.astype(bf16)], axis=1)
    rim_low = along(rims[row_count - HALO :], 1)
    rim_high = along(rims[:HALO], -1)

    pack, scalars, is_first = lax.optimization_barrier((pack, scalars, is_first))
    mod = modulation

    def past_row(s):
        return s[2] * 2 + s[3]

    quarter = pl.pallas_call(
        quarter_kernel,
        grid_spec=pltpu.PrefetchScalarGridSpec(
            num_scalar_prefetch=1,
            grid=(1,),
            in_specs=[
                pl.BlockSpec((D, CHUNK), lambda g, s: (0, s[0])),
                pl.BlockSpec((CHUNK, D), lambda g, s: (s[0], 0)),
            ],
            out_specs=pl.BlockSpec((2, D, CHUNK), lambda g, s: (0, 0, 0)),
        ),
        out_shape=struct((2, D, CHUNK), bf16),
        cost_estimate=cost(1e6, 3e6),
        name="quarter",
        compiler_params=room(8),
    )(scalars, up_weight, down_weight)
    large_past, small_past = pl.pallas_call(
        past_kernel,
        grid_spec=pltpu.PrefetchScalarGridSpec(
            num_scalar_prefetch=1,
            grid=(1,),
            in_specs=[
                pl.BlockSpec((128, CHUNK), lambda g, s: (past_row(s), s[1])),
                pl.BlockSpec((CHUNK, 128), lambda g, s: (s[1], past_row(s))),
                pl.BlockSpec((1, 64, D), lambda g, s: (s[0] * 2 + s[1], past_row(s), 0)),
            ],
            out_specs=(
                pl.BlockSpec((128, CHUNK), lambda g, s: (0, 0)),
                pl.BlockSpec((64, D), lambda g, s: (0, 0)),
            ),
        ),
        out_shape=(struct((128, CHUNK), f32), struct((64, D), f32)),
        cost_estimate=cost(1e6, 1e6),
        name="past",
        compiler_params=room(4),
    )(scalars, up_moment, down_moment, attention_moment)
    first_in, qkv, counts, attn_bf = pl.pallas_call(
        project_kernel,
        grid=(4,),
        out_shape=(
            struct((row_count, D), bf16),
            struct((3, row_count, D), bf16),
            struct((row_count, SPAN), bf16),
            struct((4, D, D), bf16),
        ),
        in_specs=[
            pl.BlockSpec((row_count, D), lambda g: (0, 0)),
            pl.BlockSpec((row_count, 128), lambda g: (0, 0)),
            pl.BlockSpec((2, 4, D), lambda g: (0, 0, 0)),
            pl.BlockSpec((1, D, D), lambda g: (g, 0, 0)),
        ],
        out_specs=(
            pl.BlockSpec((row_count, D), lambda g: (0, 0)),
            pl.BlockSpec((3, row_count, D), lambda g: (0, 0, 0)),
            pl.BlockSpec((row_count, SPAN), lambda g: (0, 0)),
            pl.BlockSpec((1, D, D), lambda g: (g, 0, 0)),
        ),
        cost_estimate=cost(4e9, 4e6),
        name="project",
        compiler_params=room(10),
    )(features, pack, mod, attention_weight)

    near = swap(after(quarter, rim_low, rim_high, large_past), 1)

    attended, stream, second_in, padded, rim_queries, rim_counts, log_totals = pl.pallas_call(
        forward_kernel,
        out_shape=(
            struct((row_count, D), bf16),
            struct((row_count, D), f32),
            struct((row_count, D), bf16),
            struct((2, row_count + 2 * HALO, D), bf16),
            struct((2 * HALO, D), bf16),
            struct((2 * HALO, RIM), bf16),
            struct((row_count, 128), f32),
        ),
        in_specs=[VMEM] * 8,
        out_specs=(VMEM,) * 7,
        scratch_shapes=[pltpu.VMEM((2 * HALO, D), bf16)],
        cost_estimate=cost(6e9, 8e6),
        name="attend",
        compiler_params=room(12),
    )(rim_low, rim_high, features, pack, mod, attn_bf, qkv, counts)

    def whole(*shape):
        return pl.BlockSpec(shape, lambda g, s: (0,) * len(shape))

    chunk_shape = struct((2, 2, 2, 128, CHUNK), bf16)
    branch, grad_second, own_kept, own_sent = pl.pallas_call(
        mlp_own_kernel,
        out_shape=(struct((row_count, D), f32), struct((row_count, D), f32), chunk_shape, chunk_shape),
        grid_spec=pltpu.PrefetchScalarGridSpec(
            num_scalar_prefetch=1,
            grid=(2,),
            in_specs=[
                whole(row_count, D),
                whole(row_count, D),
                pl.BlockSpec((D, CHUNK), lambda g, s: (0, g)),
                pl.BlockSpec((CHUNK, D), lambda g, s: (g, 0)),
            ],
            out_specs=(
                whole(row_count, D),
                whole(row_count, D),
                pl.BlockSpec((1, 2, 2, 128, CHUNK), lambda g, s: (g ^ s[1], 0, 0, 0, 0)),
                pl.BlockSpec((1, 2, 2, 128, CHUNK), lambda g, s: (g ^ s[1], 0, 0, 0, 0)),
            ),
            scratch_shapes=[pltpu.VMEM((row_count, CHUNK), bf16)] * 2,
        ),
        cost_estimate=cost(5e9, 8e6),
        name="mlp_own",
        compiler_params=room(14),
    )(scalars, second_in, cotangent, up_weight, down_weight)

    def part(away):
        return pl.BlockSpec(
            (1, 2, 2, 128, CHUNK), lambda g, s: (away ^ s[0] ^ s[1], 0, 0, 0, 0)
        )

    branch, grad_second, near_kept, near_sent = pl.pallas_call(
        mlp_near_kernel,
        out_shape=(struct((row_count, D), f32), struct((row_count, D), f32), chunk_shape, chunk_shape),
        grid_spec=pltpu.PrefetchScalarGridSpec(
            num_scalar_prefetch=1,
            grid=(1,),
            in_specs=[
                whole(row_count, D),
                whole(row_count, D),
                whole(2, D, CHUNK),
                whole(row_count, D),
                whole(row_count, D),
            ],
            out_specs=(whole(row_count, D), whole(row_count, D), part(0), part(0)),
            scratch_shapes=[pltpu.VMEM((row_count, CHUNK), bf16)] * 2,
        ),
        cost_estimate=cost(2.5e9, 4e6),
        name="mlp_near",
        compiler_params=room(10),
    )(scalars, second_in, cotangent, near, branch, grad_second)
    far = swap(after(near, own_kept), 2)
    (
        rest_kept,
        rest_sent,
        output,
        grad_stream,
        grad_attended,
        stats,
        edge_low,
        edge_high,
        table_two,
    ) = pl.pallas_call(
        mlp_far_kernel,
        out_shape=(
            chunk_shape,
            chunk_shape,
            struct((row_count, D), bf16),
            struct((row_count, D), f32),
            struct((row_count, D), bf16),
            struct((row_count, 128), f32),
            struct((HALO, D + 128), bf16),
            struct((HALO, D + 128), bf16),
            struct((8, D), f32),
        ),
        grid_spec=pltpu.PrefetchScalarGridSpec(
            num_scalar_prefetch=1,
            grid=(1,),
            in_specs=[
                whole(row_count, D),
                whole(row_count, D),
                whole(2, D, CHUNK),
                whole(row_count, D),
                whole(row_count, D),
                whole(row_count, D),
                whole(row_count, 128),
                whole(2, 4, D),
                whole(4, D, D),
                whole(row_count, D),
                whole(row_count, 128),
                pl.BlockSpec(memory_space=pl.ANY),
                pl.BlockSpec(memory_space=pl.ANY),
            ],
            out_specs=(
                part(1),
                part(1),
                whole(row_count, D),
                whole(row_count, D),
                whole(row_count, D),
                whole(row_count, 128),
                whole(HALO, D + 128),
                whole(HALO, D + 128),
                whole(8, D),
            ),
            scratch_shapes=[
                pltpu.VMEM((row_count, D), f32),
                pltpu.VMEM((row_count, D), f32),
                pltpu.VMEM((row_count, CHUNK), bf16),
                pltpu.VMEM((row_count, CHUNK), bf16),
            ],
        ),
        input_output_aliases={12: 0, 13: 1},
        cost_estimate=cost(4e9, 8e6),
        name="mlp_far",
        compiler_params=room(16),
    )(
        scalars,
        second_in,
        cotangent,
        far,
        branch,
        grad_second,
        stream,
        pack,
        mod,
        attn_bf,
        attended,
        log_totals,
        near_kept,
        near_sent,
    )

    grad_low = along(edge_high, 1)
    grad_high = along(edge_low, -1)

    large_shape = (2, 2, 2, 128, CHUNK)
    large_keep, large_send = pl.pallas_call(
        large_sum_kernel,
        out_shape=(struct(large_shape, f32), struct(large_shape, bf16)),
        in_specs=[SMEM] + [VMEM] * 4,
        out_specs=(VMEM,) * 2,
        cost_estimate=cost(1e3, 1e3),
        name="large_sum",
        compiler_params=room(12),
    )(scalars, own_kept, swap(own_sent, 2), rest_kept, swap(rest_sent, 2))

    def ordered(kernel, values, tokens, shapes, name):
        return pl.pallas_call(
            kernel,
            out_shape=shapes,
            in_specs=[VMEM] * len(values) + [pl.BlockSpec(memory_space=pl.ANY)] * len(tokens),
            out_specs=jax.tree.map(lambda _: VMEM, shapes),
            cost_estimate=cost(3e10, 1e3),
            name=name,
            compiler_params=room(8),
        )(*values, *tokens)

    def receive(keep, got, *tokens):
        rows = math.prod(keep.shape[1:-1])
        flat = (2, rows, D)
        keep, send = ordered(
            receive_kernel,
            (keep.reshape(flat), got.reshape(flat)),
            tokens,
            (struct((rows, D), f32), struct((rows, D), bf16)),
            "receive",
        )
        half = (2, rows // 2, D) if rows > 128 else (rows, D)
        return keep.reshape(half), send.reshape(half)

    def blend(keep, got, past, *tokens):
        mask = 32
        if mask < device_count:
            keep = keep + got.astype(f32)
            while mask < device_count:
                rounded = keep.astype(bf16)
                keep, got = rounded.astype(f32), swap(rounded, mask)
                mask *= 2
                if mask < device_count:
                    keep = keep + got.astype(f32)
        return ordered(blend_kernel, (keep, got, past), tokens, struct(keep.shape, bf16), "blend")

    def join(part, got, *tokens):
        rows = math.prod(part.shape[:-1])
        return ordered(
            join_kernel,
            (part.reshape(rows, D), got.reshape(rows, D)),
            tokens,
            struct((2, rows, D), bf16),
            "join",
        ).reshape(2 * rows, D)

    large_routes = ((4, 8), (1, 4), (8, 1), (16, 16))
    small_routes = ((1, 4), (4, 8), (8, 1), (16, 16))

    padded_rows = row_count + 2 * HALO
    large_got = swap(large_send, *large_routes[0])
    grad_queries, keys_total, values_total = pl.pallas_call(
        backward_kernel,
        out_shape=(struct((row_count, D), bf16),) + (struct((padded_rows, D), f32),) * 2,
        in_specs=[VMEM] * 5 + [pl.BlockSpec(memory_space=pl.ANY)],
        out_specs=(VMEM,) * 3,
        cost_estimate=cost(8e9, 9e6),
        name="attend_back",
        compiler_params=room(10),
    )(qkv, padded, grad_attended, stats, counts, large_send)
    large_keep, large_send = receive(large_keep, large_got, grad_queries)
    large_got = swap(large_send, *large_routes[1])
    piece_shape = struct((2, 2, 2, 2, 80, D), bf16)
    features_grad, small_kept, small_sent = pl.pallas_call(
        weights_kernel,
        out_shape=(struct((row_count, D), f32), piece_shape, piece_shape),
        in_specs=[SMEM, pl.BlockSpec(memory_space=pl.ANY)] + [VMEM] * 16,
        out_specs=(VMEM,) * 3,
        scratch_shapes=[
            pltpu.VMEM((4, row_count, D), bf16),
            pltpu.VMEM((8, D), f32),
            pltpu.VMEM((row_count, D), f32),
            pltpu.VMEM((row_count, D), f32),
            pltpu.VMEM((2, 2, 2, 2, 2, 80, D), bf16),
        ],
        cost_estimate=cost(6e9, 9e6),
        name="attend_weights",
        compiler_params=room(16),
    )(
        scalars,
        large_send,
        grad_queries,
        keys_total,
        values_total,
        padded,
        rim_queries,
        rim_counts,
        grad_low,
        grad_high,
        first_in,
        attended,
        grad_stream,
        features,
        pack,
        mod,
        attn_bf,
        table_two,
    )
    def chain_large(step, *tokens):
        nonlocal large_keep, large_send, large_got
        large_keep, large_send = receive(large_keep, large_got, *tokens)
        large_got = swap(large_send, *large_routes[step])

    def chain_small(step, *tokens):
        nonlocal small_keep, small_send, small_got
        small_keep, small_send = receive(small_keep, small_got, *tokens)
        small_got = swap(small_send, *small_routes[step])

    small_keep, small_send = small_kept, small_sent
    small_got = swap(small_send, 2)
    chain_large(2, small_sent)
    chain_small(0, large_send)
    chain_large(3, small_send)
    chain_small(1, large_send)
    large_part = blend(large_keep, large_got, large_past, small_send)
    large_got = swap(large_part, *large_routes[3])
    chain_small(2, large_part)
    large_part = join(large_part, large_got, small_send)
    large_got = swap(large_part, *large_routes[2])
    chain_small(3, large_part)
    large_part = join(large_part, large_got, small_send)
    large_got = swap(large_part, *large_routes[1])
    small_part = blend(small_keep, small_got, small_past, large_part)
    small_got = swap(small_part, *small_routes[3])
    small_part = join(small_part, small_got, large_part)
    small_got = swap(small_part, *small_routes[2])
    large_part = join(large_part, large_got, small_part)
    large_got = swap(large_part, *large_routes[0])
    small_part = join(small_part, small_got, large_part)
    small_got = swap(small_part, *small_routes[1])

    any_space = pl.BlockSpec(memory_space=pl.ANY)
    gathered_shape = (2, 2, 2, 128, CHUNK)
    large_work, large_mix = pl.pallas_call(
        large_first_kernel,
        out_shape=(struct((4, D, CHUNK), bf16), struct((2, D, CHUNK), bf16)),
        in_specs=[SMEM, VMEM, VMEM, any_space],
        out_specs=(VMEM,) * 2,
        scratch_shapes=[pltpu.VMEM((D, D), bf16)],
        cost_estimate=cost(5e9, 6e6),
        name="ortho_large",
        compiler_params=room(10),
    )(scalars, large_part.reshape(gathered_shape), large_got.reshape(gathered_shape), small_part)
    small_part = join(small_part, small_got, large_work)
    small_got = swap(small_part, *small_routes[0])
    mix_got = swap(large_mix, 2)
    large_result = pl.pallas_call(
        large_next_kernel,
        out_shape=struct((2, D, CHUNK), bf16),
        in_specs=[VMEM, any_space],
        out_specs=VMEM,
        scratch_shapes=[pltpu.VMEM((4, D, CHUNK), bf16), pltpu.VMEM((D, D), bf16)],
        cost_estimate=cost(5e9, 4e6),
        name="ortho_large",
        compiler_params=room(10),
    )(large_work, small_part)
    result_got = swap(large_result, 2)

    across = pl.BlockSpec((1, D, 256), lambda g: (g // 2, 0, g % 2))
    left_right = pl.BlockSpec((D, 256), lambda g: (0, g))
    top_bottom = pl.BlockSpec((256, D), lambda g: (g, 0))
    large_shapes = (struct((D, 2 * CHUNK), f32), struct((2 * CHUNK, D), f32))
    small_token = struct((8, 128), f32)
    token_block = pl.BlockSpec((8, 128), lambda g: (0, 0))
    up_moment_new, down_moment_new, moments_done = pl.pallas_call(
        large_moment_kernel,
        grid=(4,),
        out_shape=large_shapes + (small_token,),
        in_specs=[SMEM, across, across, left_right, top_bottom, any_space],
        out_specs=(left_right, top_bottom, token_block),
        cost_estimate=cost(1e7, 1e7),
        name="moment_large",
        compiler_params=room(8),
    )(scalars, large_mix, mix_got, up_moment, down_moment, large_result)
    small_work, small_mix, table_own = pl.pallas_call(
        small_start_kernel,
        out_shape=(
            struct((2, 2, 256, D), bf16),
            struct((2, 256, D), bf16),
            struct((8, D), f32),
        ),
        in_specs=[SMEM, VMEM, VMEM, any_space],
        out_specs=(VMEM,) * 3,
        cost_estimate=cost(1e6, 4e6),
        name="unpack_small",
        compiler_params=room(6),
    )(
        scalars,
        small_part.reshape(2, 2, 2, 80, D),
        small_got.reshape(2, 2, 2, 80, D),
        moments_done,
    )
    small_result = pl.pallas_call(
        small_kernel,
        out_shape=struct((2, 256, D), bf16),
        in_specs=[VMEM],
        out_specs=VMEM,
        scratch_shapes=[pltpu.VMEM((2, 256, D), bf16)] * 2 + [pltpu.VMEM((D, D), bf16)] * 2,
        cost_estimate=cost(6e9, 4e6),
        name="ortho_small",
        compiler_params=room(10),
    )(small_work)
    small_other = swap(small_result, 2)
    mix_other = swap(small_mix, 2)
    table_other = swap(table_own, 2)

    def fixed(*shape):
        return pl.BlockSpec(shape, lambda g: (0,) * len(shape))

    def one(index):
        return pl.BlockSpec((1, 256, D), index)

    up_new, down_new, attention_moment_new, modulation_moment_new, modulation_new, large_done = pl.pallas_call(
        functools.partial(large_weight_kernel, nodes=row_count * device_count),
        grid=(4,),
        out_shape=large_shapes + (struct((4, 256, D), f32),) + (struct((2, 2, D), f32),) * 2 + (small_token,),
        in_specs=[
            SMEM,
            across,
            across,
            left_right,
            top_bottom,
            one(lambda g: (g % 2, 0, 0)),
            one(lambda g: (g % 2, 0, 0)),
            one(lambda g: (g, 0, 0)),
            fixed(8, D),
            fixed(8, D),
            fixed(2, 4, D),
            fixed(2, 2, D),
            any_space,
        ],
        out_specs=(left_right, top_bottom, one(lambda g: (g, 0, 0)), fixed(2, 2, D), fixed(2, 2, D), token_block),
        cost_estimate=cost(1e7, 2e7),
        name="update_large",
        compiler_params=room(12),
    )(
        scalars,
        large_result,
        result_got,
        up_weight,
        down_weight,
        small_mix,
        mix_other,
        attention_moment,
        table_own,
        table_other,
        modulation,
        modulation_moment,
        small_result,
    )
    attention_new = pl.pallas_call(
        small_weight_kernel,
        grid_spec=pltpu.PrefetchScalarGridSpec(
            num_scalar_prefetch=1,
            grid=(4,),
            in_specs=[
                pl.BlockSpec((1, 256, D), lambda g, s: (g % 2, 0, 0)),
                pl.BlockSpec((1, 256, D), lambda g, s: (g % 2, 0, 0)),
                pl.BlockSpec((1, 256, D), lambda g, s: (g, s[4], 0)),
                any_space,
            ],
            out_specs=pl.BlockSpec((1, 256, D), lambda g, s: (g, 0, 0)),
        ),
        out_shape=struct((4, 256, D), f32),
        cost_estimate=cost(1e7, 6e6),
        name="update_small",
        compiler_params=room(6),
    )(scalars, small_result, small_other, attention_weight, large_done)
    return (
        output,
        features_grad,
        attention_moment_new,
        attention_new,
        up_moment_new,
        up_new,
        down_moment_new,
        down_new,
        modulation_moment_new,
        modulation_new,
    )


def solution(mesh):
    placed = (
        P(("nodes", "hid"), None),
        P(("nodes", "hid")),
        P(("nodes", "hid"), None),
        P(("nodes", "hid")),
        P(("nodes", "hid"), None),
        P(),
        P(None, "hid"),
        P("hid", None),
        P(),
        P(None, "hid", None),
        P(None, "hid"),
        P("hid", None),
        P(None, "hid", None),
    )
    return jax.shard_map(
        on_device,
        mesh=mesh,
        in_specs=placed,
        out_specs=(
            P(("nodes", "hid"), None),
            P(("nodes", "hid"), None),
            P(None, "hid", None),
            P(None, "hid", None),
            P(None, "hid"),
            P(None, "hid"),
            P("hid", None),
            P("hid", None),
            P(None, "hid", None),
            P(None, "hid", None),
        ),
        check_vma=False,
    )
```

```python
import functools
import math

import jax
import jax.numpy as jnp
from jax import lax
from jax.experimental import pallas as pl
from jax.experimental.pallas import tpu as pltpu
from jax.sharding import PartitionSpec as P

D = 512
HEADS = 4
HD = 128
FF = 2048
K = 16
NS_STEPS = 4
HALO = 192
BLOCK = 128
SPAN = BLOCK + 2 * HALO
RIM = 256
CHUNK = 512
TABLE_ROWS = 16

f32 = jnp.float32
bf16 = jnp.bfloat16
ns_first = 3.4445
ns_second = -4.775
ns_third = 2.0315
momentum_rate = 0.95
vector_rate = 0.9
muon_rate = 0.2
decay_rate = 0.1
score_scale = 1.0 / math.sqrt(HD)
AXES = ("nodes", "hid")
VMEM = pl.BlockSpec(memory_space=pltpu.VMEM)
SMEM = pl.BlockSpec(memory_space=pltpu.SMEM)


def nn(a, b):
    return lax.dot_general(a, b, (((1,), (0,)), ((), ())), preferred_element_type=f32)


def nt(a, b):
    return lax.dot_general(a, b, (((1,), (1,)), ((), ())), preferred_element_type=f32)


def tn(a, b):
    return lax.dot_general(a, b, (((0,), (0,)), ((), ())), preferred_element_type=f32)


def struct(shape, dtype):
    return jax.ShapeDtypeStruct(shape, dtype)


def rows_of(start, size):
    return pl.ds(pl.multiple_of(start, size), size)


def cost(flops, data):
    return pl.CostEstimate(flops=int(flops), bytes_accessed=int(data), transcendentals=0)


def room(mebibytes):
    return pltpu.CompilerParams(vmem_limit_bytes=mebibytes << 20)


def norm_parts(field):
    average = jnp.mean(field, axis=-1, keepdims=True)
    centred = field - average
    variance = jnp.mean(centred * centred, axis=-1, keepdims=True)
    inverse = lax.rsqrt(variance + 1e-06)
    return centred * inverse, inverse


def table_rows(mod_ref, level, column):
    return jnp.where(level > 0.5, mod_ref[1, column : column + 1, :], mod_ref[0, column : column + 1, :])


def modulated(field, level, mod_ref, column):
    normed, _ = norm_parts(field)
    return normed * (1.0 + table_rows(mod_ref, level, column)) + table_rows(
        mod_ref, level, column + 1
    )


def norm_back(grad_out, field, level, mod_ref, column):
    normed, inverse = norm_parts(field)
    grad_norm = grad_out * (1.0 + table_rows(mod_ref, level, column))
    grad_in = inverse * (
        grad_norm
        - jnp.mean(grad_norm, axis=-1, keepdims=True)
        - normed * jnp.mean(grad_norm * normed, axis=-1, keepdims=True)
    )
    return grad_in, grad_out * normed


def add_table(table_ref, column, level, scale_term, shift_term):
    upper = level > 0.5
    for term, place in ((scale_term, column), (shift_term, column + 1)):
        low_part = jnp.sum(jnp.where(upper, 0.0, term), axis=0, keepdims=True)
        high_part = jnp.sum(jnp.where(upper, term, 0.0), axis=0, keepdims=True)
        table_ref[place : place + 1, :] += low_part
        table_ref[4 + place : 5 + place, :] += high_part


def slot_counts(pack, row_count, width, shift):
    pieces = []
    for left in range(0, width, 128):
        lanes = lax.broadcasted_iota(jnp.int32, (row_count, 128), 1)
        rows = lax.broadcasted_iota(jnp.int32, (row_count, 128), 0)
        place = (lanes - rows + (left - shift)).astype(f32)
        total = jnp.zeros((row_count, 128), f32)
        for slot in range(K):
            total = total + jnp.where(place == pack[:, slot : slot + 1], 1.0, 0.0)
        pieces.append(total)
    return jnp.concatenate(pieces, axis=1).astype(bf16)


def quarter_kernel(scalars, up, down, rounded):
    rounded[0] = up[...].astype(bf16)
    rounded[1] = down[...].astype(bf16)


def past_kernel(scalars, up, down, attention, large_past, small_past):
    z2 = scalars[3]
    large = jnp.where(scalars[0] == 0, up[...], down[...].T)
    for j in range(2):
        large_past[j ^ z2] = large[j * 128 : (j + 1) * 128]
        small_past[j ^ z2] = attention[0, j * 64 : (j + 1) * 64, :]


def project_kernel(features, pack, mod, weights, first_in, qkv, counts, rounded):
    row_count = features.shape[0]
    turn = pl.program_id(0)

    @pl.when(turn == 0)
    def _():
        for start in range(0, row_count, 256):
            rows = slice(start, start + 256)
            level = pack[rows, K : K + 1]
            first_in[rows, :] = modulated(features[rows, :].astype(f32), level, mod, 0).astype(bf16)

    weight = weights[0].astype(bf16)
    rounded[0] = weight

    @pl.when(turn < 3)
    def _():
        qkv[turn] = nn(first_in[...], weight).astype(bf16)
        share = row_count // BLOCK // 3

        def count_step(b, carry):
            rows = rows_of(b * BLOCK, BLOCK)
            counts[rows, :] = slot_counts(pack[rows, :], BLOCK, SPAN, HALO)
            return carry

        lax.fori_loop(turn * share, (turn + 1) * share, count_step, 0)


def forward_kernel(
    rim_low,
    rim_high,
    features,
    pack,
    mod,
    weights,
    qkv,
    counts,
    attended,
    stream,
    second_in,
    padded,
    rim_queries,
    rim_counts,
    log_totals,
    rim_in,
):
    row_count = features.shape[0]
    for side, rim in enumerate((rim_low, rim_high)):

        def rim_step(b, carry):
            rows = rows_of(b * 64, 64)
            target = pl.ds(pl.multiple_of(side * HALO + b * 64, 64), 64)
            info = rim[rows, D:].astype(f32)
            rim_in[target, :] = modulated(
                rim[rows, :D].astype(f32), info[:, K : K + 1], mod, 0
            ).astype(bf16)
            rim_counts[target, :] = slot_counts(
                info, 64, RIM, b * 64 + (-HALO if side == 0 else RIM)
            )
            return carry

        lax.fori_loop(0, HALO // 64, rim_step, 0)
    rim_queries[...] = nn(rim_in[...], weights[0]).astype(bf16)
    for p in range(2):
        piece = nn(rim_in[...], weights[1 + p]).astype(bf16)
        padded[p, :HALO, :] = piece[:HALO]
        padded[p, HALO + row_count :, :] = piece[HALO:]
        padded[p, HALO : HALO + row_count, :] = qkv[1 + p]

    def step(b, carry):
        rows = rows_of(b * BLOCK, BLOCK)
        span = pl.ds(pl.multiple_of(b * BLOCK, BLOCK), SPAN)
        count = counts[rows, :].astype(f32)
        live = count > 0.0
        columns = [slice(h * HD, (h + 1) * HD) for h in range(HEADS)]
        scores = [nt(qkv[0, rows, cols], padded[0, span, cols]) * score_scale for cols in columns]
        lanes = lax.broadcasted_iota(jnp.int32, (BLOCK, 128), 1)
        stats = jnp.zeros((BLOCK, 128), f32)
        for h, cols in enumerate(columns):
            masked = jnp.where(live, scores[h], -1e30)
            peak = jnp.max(masked, axis=-1, keepdims=True)
            exponent = jnp.exp(masked - peak)
            total = jnp.sum(exponent * count, axis=-1, keepdims=True)
            probs = (exponent / total).astype(bf16)
            spread = (probs.astype(f32) * count).astype(bf16)
            attended[rows, cols] = nn(spread, padded[1, span, cols]).astype(bf16)
            stats = jnp.where(lanes == h, peak + jnp.log(total), stats)
        log_totals[rows, :] = stats
        return carry

    lax.fori_loop(0, row_count // BLOCK, step, 0)
    for start in range(0, row_count, 256):
        rows = slice(start, start + 256)
        field = features[rows, :].astype(f32) + nn(attended[rows, :], weights[3])
        stream[rows, :] = field
        second_in[rows, :] = modulated(field, pack[rows, K : K + 1], mod, 2).astype(bf16)


def mlp_chunk(
    scalars, second_in, cotangent, up, down, branch_in, grad_in, branch, grad_second, acts, grads, kept, sent
):
    row_count = second_in.shape[0]
    for start in range(0, row_count, 256):
        rows = slice(start, start + 256)
        preact = nn(second_in[rows, :], up)
        grad_act = nt(cotangent[rows, :], down)
        sigmoid = 0.5 * jnp.tanh(0.5 * preact) + 0.5
        act = (preact * sigmoid).astype(bf16)
        acts[rows, :] = act
        grad_pre = (grad_act * (sigmoid * (1.0 + preact * (1.0 - sigmoid)))).astype(bf16)
        grads[rows, :] = grad_pre
        branch[rows, :] = branch_in[rows, :] + nn(act, down)
        grad_second[rows, :] = grad_in[rows, :] + nt(grad_pre, up)
    first, z1, z2 = scalars[0] == 0, scalars[2], scalars[3]
    for out, swapped in ((kept, False), (sent, True)):
        ups = jnp.logical_not(first) if swapped else first
        product = tn(
            jnp.where(ups, second_in[...], cotangent[...]), jnp.where(ups, grads[...], acts[...])
        )
        for q in range(4):
            out[0, (q // 2) ^ z1, (q % 2) ^ z2] = product[q * 128 : (q + 1) * 128].astype(bf16)


def mlp_own_kernel(
    scalars, second_in, cotangent, up, down, branch, grad_second, kept, sent, acts, grads
):
    @pl.when(pl.program_id(0) == 0)
    def _():
        branch[...] = jnp.zeros_like(branch)
        grad_second[...] = jnp.zeros_like(grad_second)

    mlp_chunk(
        scalars,
        second_in,
        cotangent,
        up[...].astype(bf16),
        down[...].astype(bf16),
        branch,
        grad_second,
        branch,
        grad_second,
        acts,
        grads,
        kept,
        sent,
    )


def mlp_near_kernel(
    scalars, second_in, cotangent, near, branch_in, grad_in, branch, grad_second, kept, sent, acts, grads
):
    mlp_chunk(
        scalars,
        second_in,
        cotangent,
        near[0],
        near[1],
        branch_in,
        grad_in,
        branch,
        grad_second,
        acts,
        grads,
        kept,
        sent,
    )


def mlp_far_kernel(
    scalars,
    second_in,
    cotangent,
    far,
    branch_in,
    grad_in,
    stream,
    pack,
    mod,
    weights,
    attended,
    log_totals,
    kept_in,
    sent_in,
    kept,
    sent,
    output,
    grad_stream,
    grad_attended,
    stats,
    edge_low,
    edge_high,
    table,
    branch,
    grad_second,
    acts,
    grads,
):
    row_count = second_in.shape[0]
    mlp_chunk(
        scalars,
        second_in,
        cotangent,
        far[0],
        far[1],
        branch_in,
        grad_in,
        branch,
        grad_second,
        acts,
        grads,
        kept,
        sent,
    )
    table[...] = jnp.zeros_like(table)

    for start in range(0, row_count, 256):
        rows = slice(start, start + 256)
        field = stream[rows, :]
        level = pack[rows, K : K + 1]
        output[rows, :] = (field + branch[rows, :]).astype(bf16)
        gradient = grad_second[rows, :]
        grad_field, scale_term = norm_back(gradient, field, level, mod, 2)
        add_table(table, 2, level, scale_term, gradient)
        total = cotangent[rows, :].astype(f32) + grad_field
        grad_stream[rows, :] = total
        back = nt(total.astype(bf16), weights[3]).astype(bf16)
        grad_attended[rows, :] = back
        product = back.astype(f32) * attended[rows, :].astype(f32)
        lanes = lax.broadcasted_iota(jnp.int32, (256, 128), 1)
        kept_stats = log_totals[rows, :]
        for h in range(HEADS):
            delta = jnp.sum(product[:, h * HD : (h + 1) * HD], axis=-1, keepdims=True)
            kept_stats = jnp.where(lanes == HEADS + h, delta, kept_stats)
        stats[rows, :] = kept_stats
    for edge, first in ((edge_low, 0), (edge_high, row_count - HALO)):
        rows = slice(first, first + HALO)
        edge[:, :D] = grad_attended[rows, :]
        known = stats[rows, :]
        upper = known.astype(bf16)
        lower = (known - upper.astype(f32)).astype(bf16).astype(f32)
        edge[:, D:] = (upper.astype(f32) + pltpu.roll(lower, 2 * HEADS, 1)).astype(bf16)


def attention_terms(scores, grad_probs, count, log_total, delta):
    probs = jnp.exp(jnp.where(count > 0.0, scores * score_scale, -1e30) - log_total)
    slopes = (probs * (grad_probs - delta)).astype(bf16).astype(f32)
    spread = (probs.astype(bf16).astype(f32) * count).astype(bf16)
    return (slopes * count).astype(bf16), spread


def backward_kernel(qkv, padded, grad, stats, counts, token, grad_query, keys_total, values_total):
    keys_total[...] = jnp.zeros_like(keys_total)
    values_total[...] = jnp.zeros_like(values_total)

    def step(b, carry):
        rows = rows_of(b * BLOCK, BLOCK)
        span = pl.ds(pl.multiple_of(b * BLOCK, BLOCK), SPAN)
        count = counts[rows, :].astype(f32)
        columns = [slice(h * HD, (h + 1) * HD) for h in range(HEADS)]
        products = [
            (nt(qkv[0, rows, cols], padded[0, span, cols]), nt(grad[rows, cols], padded[1, span, cols]))
            for cols in columns
        ]
        terms = [
            attention_terms(
                *products[h],
                count,
                stats[rows, h : h + 1],
                stats[rows, HEADS + h : HEADS + h + 1],
            )
            for h in range(HEADS)
        ]
        for (slopes, spread), cols in zip(terms, columns):
            grad_query[rows, cols] = (nn(slopes, padded[0, span, cols]) * score_scale).astype(bf16)
            keys_total[span, cols] += tn(slopes, qkv[0, rows, cols])
            values_total[span, cols] += tn(spread, grad[rows, cols])
        return carry

    lax.fori_loop(0, counts.shape[0] // BLOCK, step, 0)


def weights_kernel(
    scalars,
    token,
    queries_in,
    keys_in,
    values_in,
    padded,
    rim_query,
    rim_counts,
    grad_low,
    grad_high,
    first_in,
    attended,
    grad_stream,
    features,
    pack,
    mod,
    weights,
    table_two,
    features_grad,
    kept,
    sent,
    gathered,
    table,
    keys_total,
    values_total,
    blocks,
):
    row_count = first_in.shape[0]
    columns = [slice(h * HD, (h + 1) * HD) for h in range(HEADS)]
    own = slice(HALO, HALO + row_count)
    keys_total[...] = keys_in[own, :]
    values_total[...] = values_in[own, :]
    for side, grads in enumerate((grad_low, grad_high)):
        first = 0 if side == 0 else row_count - RIM
        own_span = slice(first, first + RIM)
        span = slice(HALO + first, HALO + first + RIM)
        rows = slice(side * HALO, (side + 1) * HALO)
        known = grads[:, D:].astype(f32)
        count = rim_counts[rows, :].astype(f32)
        products = [
            (nt(rim_query[rows, cols], padded[0, span, cols]), nt(grads[:, cols], padded[1, span, cols]))
            for cols in columns
        ]
        terms = []
        for h in range(HEADS):
            numbers = [known[:, i * HEADS + h : i * HEADS + h + 1] for i in range(4)]
            terms.append(
                attention_terms(*products[h], count, numbers[0] + numbers[2], numbers[1] + numbers[3])
            )
        for (slopes, spread), cols in zip(terms, columns):
            keys_total[own_span, cols] += tn(slopes, rim_query[rows, cols])
            values_total[own_span, cols] += tn(spread, grads[:, cols])
    gathered[0] = queries_in[...]
    gathered[1] = (keys_total[...] * score_scale).astype(bf16)
    gathered[2] = values_total[...].astype(bf16)
    table[...] = table_two[...]
    for start in range(0, row_count, 256):
        rows = slice(start, start + 256)
        level = pack[rows, K : K + 1]
        gradient = nt(gathered[0, rows, :], weights[0])
        for p in range(1, 3):
            gradient = gradient + nt(gathered[p, rows, :], weights[p])
        grad_field, scale_term = norm_back(gradient, features[rows, :].astype(f32), level, mod, 0)
        add_table(table, 0, level, scale_term, gradient)
        total = grad_stream[rows, :]
        features_grad[rows, :] = total + grad_field
        gathered[3, rows, :] = total.astype(bf16)
    core, slot_bit, z1, z2, hid = (scalars[i] for i in range(5))

    def product_step(n, carry):
        away, slot = n // 2, n % 2
        target = core ^ away
        p = 2 * target + slot
        product = tn(jnp.where(p < 3, first_in[...], attended[...]), gathered[p])
        for half in range(2):
            for q in range(4):
                slot_at, hid_at, row_half = slot ^ slot_bit, half ^ hid, (q // 2) ^ z1
                index = (
                    away,
                    jnp.where(target == 0, slot_at, row_half),
                    hid_at,
                    jnp.where(target == 0, row_half, slot_at),
                    (q % 2) ^ z2,
                )
                start = half * 256 + q * 64
                blocks[index + (slice(0, 64),)] = product[start : start + 64].astype(bf16)
                row = (q // 2) * 4 + 2 * half + q % 2
                known = jnp.broadcast_to(table[row : row + 1, :], (TABLE_ROWS, D))
                blocks[index + (slice(64, 80),)] = jnp.where(p == 0, known, 0.0).astype(bf16)
        return carry

    lax.fori_loop(0, 4, product_step, 0)
    kept[...] = blocks[0]
    sent[...] = blocks[1]


def large_sum_kernel(scalars, own, own_got, rest, rest_got, keep, send):
    first = scalars[0] == 0
    for away, out in ((0, keep), (1, send)):
        for source, got, h in ((own, own_got, 0), (rest, rest_got, 1)):
            for i in range(2):
                where_from = (jnp.where(first, away, i), jnp.where(first, i, away))
                where_to = (jnp.where(first, h, i), jnp.where(first, i, h))
                total = source[where_from].astype(f32) + got[where_from].astype(f32)
                out[where_to] = total.astype(out.dtype)


def receive_kernel(*refs):
    kept, got, keep, send = refs[0], refs[1], refs[-2], refs[-1]
    keep[...] = kept[0].astype(f32) + got[0].astype(f32)
    send[...] = (kept[1].astype(f32) + got[1].astype(f32)).astype(bf16)


def total_kernel(*refs):
    kept, got, total = refs[0], refs[1], refs[-1]
    total[...] = (kept[...] + got[...].astype(f32)).astype(bf16)


def blend_kernel(flip, *refs):
    kept, got, past, part = refs[0], refs[1], refs[2], refs[-1]
    rows = past.shape[1]
    for j in range(2):
        total = kept[j].astype(f32) + got[j ^ flip].astype(f32)
        blended = (1.0 + momentum_rate) * total[:rows] + momentum_rate * momentum_rate * past[j]
        part[j, :rows, :] = blended.astype(bf16)
        if rows < part.shape[1]:
            part[j, rows:, :] = total[rows:].astype(bf16)


def join_kernel(*refs):
    part, got, pieces = refs[0], refs[1], refs[-1]
    pieces[0] = part[...]
    pieces[1] = got[...]


def newton_schulz(groups, polys, rows_first, scales):
    blocks = [[[ref[i] for i in half] for half in halves] for ref, halves in groups]
    grams = []
    for halves, scale in zip(blocks, scales):
        sums = []
        for half in halves:
            total = None
            for block in half:
                term = tn(block, block) if rows_first else nt(block, block)
                total = term if total is None else total + term
            sums.append((total if scale is None else total * (scale * scale)).astype(bf16))
        grams.append((sums[0].astype(f32) + sums[1].astype(f32)).astype(bf16))
    for gram, poly in zip(grams, polys):
        poly[...] = (ns_second * gram.astype(f32) + ns_third * nn(gram, gram)).astype(bf16)
    for (ref, halves), values, poly, scale in zip(groups, blocks, polys, scales):
        for half, half_values in zip(halves, values):
            for i, block in zip(half, half_values):
                other = nn(block, poly[...]) if rows_first else nn(poly[...], block)
                total = ns_first * block.astype(f32) + other
                ref[i] = (total if scale is None else total * scale).astype(bf16)


def large_start_kernel(scalars, kept, got, work, poly):
    core, slot_bit, z1, z2 = (scalars[i] for i in range(4))
    total = jnp.zeros((8, D), f32)
    for n in range(16):
        b1, b2, b3, b4 = n // 8, (n // 4) % 2, (n // 2) % 2, n % 2
        source = kept if b1 == 0 else got
        block = source[b2, b3, b4]
        value = block.astype(f32)
        total = total + jnp.sum((value * value).reshape(16, 8, D), axis=0)
        slot = jnp.where(core == 0, b1, b2)
        half = jnp.where(core == 0, b2, b3)
        row_half = jnp.where(core == 0, b3, b1)
        start = ((row_half ^ z1) * 2 + (b4 ^ z2)) * 128
        work[half * 2 + (slot ^ slot_bit), rows_of(start, 128), :] = block
    return 1.0 / (jnp.sqrt(jnp.sum(total)) + 1e-07)


large_halves = ((0, 1), (2, 3))


def large_first_kernel(scalars, kept, got, token, work, blend, poly):
    scale = large_start_kernel(scalars, kept, got, work, poly)
    for s in range(2):
        blend[s] = work[s]

    def step(i, factor):
        newton_schulz([(work, large_halves)], [poly], False, [factor])
        return jnp.ones((), f32)

    lax.fori_loop(0, NS_STEPS // 2, step, scale)


def large_next_kernel(given, token, result, work, poly):
    work[...] = given[...]

    def step(i, carry):
        newton_schulz([(work, large_halves)], [poly], False, [None])
        return carry

    lax.fori_loop(NS_STEPS // 2, NS_STEPS, step, 0)
    for s in range(2):
        result[s] = work[s]


def small_start_kernel(scalars, kept, got, token, work, blend, table):
    table[...] = jnp.zeros_like(table)
    core, slot_bit, z1, z2 = (scalars[i] for i in range(4))
    for n in range(16):
        b1, b2, b3, b4 = n // 8, (n // 4) % 2, (n // 2) % 2, n % 2
        source = kept if b1 == 0 else got
        block = source[b2, b3, b4]
        slot = jnp.where(core == 0, b1, b3) ^ slot_bit
        half = b2
        row_half = jnp.where(core == 0, b3, b1)
        quarter = (row_half ^ z1) * 2 + (b4 ^ z2)
        work[slot, half, rows_of(quarter * 64, 64), :] = block[:64]

        @pl.when((slot == 0) & (half == 0))
        def _():
            table[pl.ds(quarter, 1), :] = block[64:].astype(f32)[:1]

    for s in range(2):
        blend[s, :256, :] = work[s, 0]
        blend[s, 256:, :] = table[...].astype(bf16)


def small_kernel(
    scalars,
    given,
    own,
    got,
    up_weight,
    down_weight,
    token,
    result,
    up_new,
    down_new,
    first,
    second,
    poly_first,
    poly_second,
    factors,
):
    turn = pl.program_id(0)
    works = (first, second)

    @pl.when(turn == 0)
    def _():
        for s, work in enumerate(works):
            total = jnp.zeros((8, D), f32)
            for half in range(2):
                block = given[s, half]
                work[half] = block
                value = block.astype(f32)
                total = total + jnp.sum((value * value).reshape(32, 8, D), axis=0)
            factors[s] = 1.0 / (jnp.sqrt(jnp.sum(total)) + 1e-07)

    groups = [(work, ((0,), (1,))) for work in works]
    scales = [jnp.where(turn == 0, factors[s], 1.0) for s in range(2)]
    newton_schulz(groups, [poly_first, poly_second], True, scales)
    is_up = scalars[0] == 0
    ups = jnp.where(is_up, own[0], got[0])
    downs = jnp.where(is_up, got[0], own[0])
    up_new[...] = new_weight(up_weight[...], ups.astype(f32), FF)
    down_new[...] = new_weight(down_weight[...], downs.T.astype(f32), FF)

    @pl.when(turn == NS_STEPS - 1)
    def _():
        for s, work in enumerate(works):
            result[s] = work[0]


def new_moment(blend, moment):
    share = 1.0 / (1.0 + momentum_rate)
    return share * blend + (momentum_rate - share * momentum_rate * momentum_rate) * moment


def new_weight(weight, ortho, longest):
    return weight - muon_rate * (0.2 * math.sqrt(longest) * ortho + decay_rate * weight)


def large_moment_kernel(scalars, own, got, up_moment, down_moment, token, up_moment_new, down_moment_new, done):
    done[...] = jnp.zeros_like(done)
    first = scalars[0] == 0
    ups, downs = jnp.where(first, own[0], got[0]), jnp.where(first, got[0], own[0])
    up_moment_new[...] = new_moment(ups.astype(f32), up_moment[...])
    down_moment_new[...] = new_moment(downs.T.astype(f32), down_moment[...])


def small_moment_kernel(
    scalars,
    mix,
    mix_got,
    moment,
    table,
    table_got,
    modulation,
    held_moment,
    token,
    moment_new,
    held_moment_new,
    held_new,
    done,
    *,
    nodes,
):
    done[...] = jnp.zeros_like(done)
    core, turn = scalars[0], pl.program_id(0)
    blend = jnp.where(core == turn // 2, mix[0], mix_got[0]).astype(f32)
    moment_new[0] = new_moment(blend, moment[0])

    @pl.when(turn == 0)
    def _():
        total = jnp.where(core == 0, table[0], table_got[0]).astype(f32)
        for level in range(2):
            for column in range(2):
                row = level * 2 + column
                at = (slice(level, level + 1), slice(column, column + 1))
                value = vector_rate * held_moment[at] + total[row : row + 1, :].reshape(1, 1, D)
                held = modulation[level : level + 1, pl.ds(scalars[4] * 2 + column, 1)]
                held_moment_new[at] = value
                held_new[at] = held - 0.2 / math.sqrt(nodes) * value


def small_weight_kernel(scalars, own, got, weight, token, weight_new):
    mine = scalars[0] == pl.program_id(0) // 2
    ortho = jnp.where(mine, own[0].astype(f32), got[0].astype(f32))
    weight_new[0] = new_weight(weight[0], ortho, D)


def on_device(
    features,
    levels,
    neighbour_index,
    neighbour_count,
    cotangent,
    attention_weight,
    up_weight,
    down_weight,
    modulation,
    attention_moment,
    up_moment,
    down_moment,
    modulation_moment,
):
    row_count = features.shape[0]
    device_count = lax.axis_size(AXES)
    me = lax.axis_index(AXES)
    first_row = me * row_count

    def bit(place):
        return (me >> place) & 1

    hid, core, slot_bit, z1, z2 = (bit(place) for place in range(5))
    scalars = jnp.stack([core, slot_bit, z1, z2, hid]).astype(jnp.int32)
    is_first = core == 0

    def along(value, distance):
        pairs = [(i, i + distance) for i in range(device_count) if 0 <= i + distance < device_count]
        return lax.ppermute(value, AXES, pairs)

    def after(value, *others):
        return lax.optimization_barrier((value,) + others)[0]

    def swap(value, mask, other=None):
        masks = (mask, mask if other is None else other)
        pairs = [(i, i ^ masks[(i // 2) % 2]) for i in range(device_count)]
        return lax.ppermute(value, AXES, pairs)

    live = jnp.arange(K, dtype=jnp.int32)[None, :] < neighbour_count[:, None]
    row_ids = first_row + jnp.arange(row_count, dtype=jnp.int32)[:, None]
    offsets = jnp.where(live, neighbour_index - row_ids, 512)
    pack = jnp.concatenate(
        [offsets, levels[:, None], jnp.zeros((row_count, 128 - K - 1), jnp.int32)], axis=1
    ).astype(f32)
    rims = jnp.concatenate([features, pack.astype(bf16)], axis=1)
    rim_low = along(rims[row_count - HALO :], 1)
    rim_high = along(rims[:HALO], -1)

    pack, scalars, is_first = lax.optimization_barrier((pack, scalars, is_first))
    mod = modulation

    quarter = pl.pallas_call(
        quarter_kernel,
        grid_spec=pltpu.PrefetchScalarGridSpec(
            num_scalar_prefetch=1,
            grid=(1,),
            in_specs=[
                pl.BlockSpec((D, CHUNK), lambda g, s: (0, s[0])),
                pl.BlockSpec((CHUNK, D), lambda g, s: (s[0], 0)),
            ],
            out_specs=pl.BlockSpec((2, D, CHUNK), lambda g, s: (0, 0, 0)),
        ),
        out_shape=struct((2, D, CHUNK), bf16),
        cost_estimate=cost(1e6, 3e6),
        name="quarter",
        compiler_params=room(8),
    )(scalars, up_weight, down_weight)
    large_past, small_past = pl.pallas_call(
        past_kernel,
        grid_spec=pltpu.PrefetchScalarGridSpec(
            num_scalar_prefetch=1,
            grid=(1,),
            in_specs=[
                pl.BlockSpec((256, CHUNK), lambda g, s: (s[2], s[1])),
                pl.BlockSpec((CHUNK, 256), lambda g, s: (s[1], s[2])),
                pl.BlockSpec((1, 128, D), lambda g, s: (s[0] * 2 + s[1], s[2], 0)),
            ],
            out_specs=(
                pl.BlockSpec((2, 128, CHUNK), lambda g, s: (0, 0, 0)),
                pl.BlockSpec((2, 64, D), lambda g, s: (0, 0, 0)),
            ),
        ),
        out_shape=(struct((2, 128, CHUNK), f32), struct((2, 64, D), f32)),
        cost_estimate=cost(1e6, 1e6),
        name="past",
        compiler_params=room(4),
    )(scalars, up_moment, down_moment, attention_moment)
    first_in, qkv, counts, attn_bf = pl.pallas_call(
        project_kernel,
        grid=(4,),
        out_shape=(
            struct((row_count, D), bf16),
            struct((3, row_count, D), bf16),
            struct((row_count, SPAN), bf16),
            struct((4, D, D), bf16),
        ),
        in_specs=[
            pl.BlockSpec((row_count, D), lambda g: (0, 0)),
            pl.BlockSpec((row_count, 128), lambda g: (0, 0)),
            pl.BlockSpec((2, 4, D), lambda g: (0, 0, 0)),
            pl.BlockSpec((1, D, D), lambda g: (g, 0, 0)),
        ],
        out_specs=(
            pl.BlockSpec((row_count, D), lambda g: (0, 0)),
            pl.BlockSpec((3, row_count, D), lambda g: (0, 0, 0)),
            pl.BlockSpec((row_count, SPAN), lambda g: (0, 0)),
            pl.BlockSpec((1, D, D), lambda g: (g, 0, 0)),
        ),
        cost_estimate=cost(4e9, 4e6),
        name="project",
        compiler_params=room(10),
    )(features, pack, mod, attention_weight)

    near = swap(after(quarter, rim_low, rim_high, large_past), 1)

    attended, stream, second_in, padded, rim_queries, rim_counts, log_totals = pl.pallas_call(
        forward_kernel,
        out_shape=(
            struct((row_count, D), bf16),
            struct((row_count, D), f32),
            struct((row_count, D), bf16),
            struct((2, row_count + 2 * HALO, D), bf16),
            struct((2 * HALO, D), bf16),
            struct((2 * HALO, RIM), bf16),
            struct((row_count, 128), f32),
        ),
        in_specs=[VMEM] * 8,
        out_specs=(VMEM,) * 7,
        scratch_shapes=[pltpu.VMEM((2 * HALO, D), bf16)],
        cost_estimate=cost(6e9, 8e6),
        name="attend",
        compiler_params=room(12),
    )(rim_low, rim_high, features, pack, mod, attn_bf, qkv, counts)

    def whole(*shape):
        return pl.BlockSpec(shape, lambda g, s: (0,) * len(shape))

    chunk_shape = struct((2, 2, 2, 128, CHUNK), bf16)
    branch, grad_second, own_kept, own_sent = pl.pallas_call(
        mlp_own_kernel,
        out_shape=(struct((row_count, D), f32), struct((row_count, D), f32), chunk_shape, chunk_shape),
        grid_spec=pltpu.PrefetchScalarGridSpec(
            num_scalar_prefetch=1,
            grid=(2,),
            in_specs=[
                whole(row_count, D),
                whole(row_count, D),
                pl.BlockSpec((D, CHUNK), lambda g, s: (0, g)),
                pl.BlockSpec((CHUNK, D), lambda g, s: (g, 0)),
            ],
            out_specs=(
                whole(row_count, D),
                whole(row_count, D),
                pl.BlockSpec((1, 2, 2, 128, CHUNK), lambda g, s: (g ^ s[1], 0, 0, 0, 0)),
                pl.BlockSpec((1, 2, 2, 128, CHUNK), lambda g, s: (g ^ s[1], 0, 0, 0, 0)),
            ),
            scratch_shapes=[pltpu.VMEM((row_count, CHUNK), bf16)] * 2,
        ),
        cost_estimate=cost(5e9, 8e6),
        name="mlp_own",
        compiler_params=room(14),
    )(scalars, second_in, cotangent, up_weight, down_weight)

    def part(away):
        return pl.BlockSpec(
            (1, 2, 2, 128, CHUNK), lambda g, s: (away ^ s[0] ^ s[1], 0, 0, 0, 0)
        )

    branch, grad_second, near_kept, near_sent = pl.pallas_call(
        mlp_near_kernel,
        out_shape=(struct((row_count, D), f32), struct((row_count, D), f32), chunk_shape, chunk_shape),
        grid_spec=pltpu.PrefetchScalarGridSpec(
            num_scalar_prefetch=1,
            grid=(1,),
            in_specs=[
                whole(row_count, D),
                whole(row_count, D),
                whole(2, D, CHUNK),
                whole(row_count, D),
                whole(row_count, D),
            ],
            out_specs=(whole(row_count, D), whole(row_count, D), part(0), part(0)),
            scratch_shapes=[pltpu.VMEM((row_count, CHUNK), bf16)] * 2,
        ),
        cost_estimate=cost(2.5e9, 4e6),
        name="mlp_near",
        compiler_params=room(10),
    )(scalars, second_in, cotangent, near, branch, grad_second)
    far = swap(after(near, own_kept), 2)
    (
        rest_kept,
        rest_sent,
        output,
        grad_stream,
        grad_attended,
        stats,
        edge_low,
        edge_high,
        table_two,
    ) = pl.pallas_call(
        mlp_far_kernel,
        out_shape=(
            chunk_shape,
            chunk_shape,
            struct((row_count, D), bf16),
            struct((row_count, D), f32),
            struct((row_count, D), bf16),
            struct((row_count, 128), f32),
            struct((HALO, D + 128), bf16),
            struct((HALO, D + 128), bf16),
            struct((8, D), f32),
        ),
        grid_spec=pltpu.PrefetchScalarGridSpec(
            num_scalar_prefetch=1,
            grid=(1,),
            in_specs=[
                whole(row_count, D),
                whole(row_count, D),
                whole(2, D, CHUNK),
                whole(row_count, D),
                whole(row_count, D),
                whole(row_count, D),
                whole(row_count, 128),
                whole(2, 4, D),
                whole(4, D, D),
                whole(row_count, D),
                whole(row_count, 128),
                pl.BlockSpec(memory_space=pl.ANY),
                pl.BlockSpec(memory_space=pl.ANY),
            ],
            out_specs=(
                part(1),
                part(1),
                whole(row_count, D),
                whole(row_count, D),
                whole(row_count, D),
                whole(row_count, 128),
                whole(HALO, D + 128),
                whole(HALO, D + 128),
                whole(8, D),
            ),
            scratch_shapes=[
                pltpu.VMEM((row_count, D), f32),
                pltpu.VMEM((row_count, D), f32),
                pltpu.VMEM((row_count, CHUNK), bf16),
                pltpu.VMEM((row_count, CHUNK), bf16),
            ],
        ),
        input_output_aliases={12: 0, 13: 1},
        cost_estimate=cost(4e9, 8e6),
        name="mlp_far",
        compiler_params=room(16),
    )(
        scalars,
        second_in,
        cotangent,
        far,
        branch,
        grad_second,
        stream,
        pack,
        mod,
        attn_bf,
        attended,
        log_totals,
        near_kept,
        near_sent,
    )

    grad_low = along(edge_high, 1)
    grad_high = along(edge_low, -1)

    large_shape = (2, 2, 2, 128, CHUNK)
    large_keep, large_send = pl.pallas_call(
        large_sum_kernel,
        out_shape=(struct(large_shape, f32), struct(large_shape, bf16)),
        in_specs=[SMEM] + [VMEM] * 4,
        out_specs=(VMEM,) * 2,
        cost_estimate=cost(1e3, 1e3),
        name="large_sum",
        compiler_params=room(12),
    )(scalars, own_kept, swap(own_sent, 2), rest_kept, swap(rest_sent, 2))

    def ordered(kernel, values, tokens, shapes, name, work=1e10):
        return pl.pallas_call(
            kernel,
            out_shape=shapes,
            in_specs=[VMEM] * len(values) + [pl.BlockSpec(memory_space=pl.ANY)] * len(tokens),
            out_specs=jax.tree.map(lambda _: VMEM, shapes),
            cost_estimate=cost(work, 1e3),
            name=name,
            compiler_params=room(8),
        )(*values, *tokens)

    def receive(keep, got, *tokens):
        rows = math.prod(keep.shape[1:-1])
        flat = (2, rows, D)
        keep, send = ordered(
            receive_kernel,
            (keep.reshape(flat), got.reshape(flat)),
            tokens,
            (struct((rows, D), f32), struct((rows, D), bf16)),
            "receive",
        )
        half = (2, rows // 2, D)
        return keep.reshape(half), send.reshape(half)

    def rounded_total(keep, got, *tokens):
        return ordered(total_kernel, (keep, got), tokens, struct(keep.shape, bf16), "total")

    def blend(total, got, past, *tokens, work=1e10):
        flip, mask = 1, 32
        while mask < device_count:
            mine = total.astype(f32) + (got[::-1] if flip else got).astype(f32)
            total, flip = mine.astype(bf16), 0
            got = swap(total, mask)
            mask *= 2
        return ordered(
            functools.partial(blend_kernel, flip),
            (total, got, past),
            tokens,
            struct(total.shape, bf16),
            "blend",
            work,
        ).reshape(-1, D)

    def join(part, got, *tokens, work=1e10):
        rows = math.prod(part.shape[:-1])
        return ordered(
            join_kernel,
            (part.reshape(rows, D), got.reshape(rows, D)),
            tokens,
            struct((2, rows, D), bf16),
            "join",
            work,
        ).reshape(2 * rows, D)

    large_routes = ((4, 8), (1, 4), (8, 1), (16, 16))
    small_routes = ((4, 8), (1, 1), (8, 4), (16, 16))

    padded_rows = row_count + 2 * HALO
    large_got = swap(large_send, *large_routes[0])
    grad_queries, keys_total, values_total = pl.pallas_call(
        backward_kernel,
        out_shape=(struct((row_count, D), bf16),) + (struct((padded_rows, D), f32),) * 2,
        in_specs=[VMEM] * 5 + [pl.BlockSpec(memory_space=pl.ANY)],
        out_specs=(VMEM,) * 3,
        cost_estimate=cost(8e9, 9e6),
        name="attend_back",
        compiler_params=room(10),
    )(qkv, padded, grad_attended, stats, counts, large_send)
    large_keep, large_send = receive(large_keep, large_got, grad_queries)
    large_got = swap(large_send, *large_routes[1])
    piece_shape = struct((2, 2, 2, 2, 80, D), bf16)
    features_grad, small_kept, small_sent = pl.pallas_call(
        weights_kernel,
        out_shape=(struct((row_count, D), f32), piece_shape, piece_shape),
        in_specs=[SMEM, pl.BlockSpec(memory_space=pl.ANY)] + [VMEM] * 16,
        out_specs=(VMEM,) * 3,
        scratch_shapes=[
            pltpu.VMEM((4, row_count, D), bf16),
            pltpu.VMEM((8, D), f32),
            pltpu.VMEM((row_count, D), f32),
            pltpu.VMEM((row_count, D), f32),
            pltpu.VMEM((2, 2, 2, 2, 2, 80, D), bf16),
        ],
        cost_estimate=cost(6e9, 9e6),
        name="attend_weights",
        compiler_params=room(16),
    )(
        scalars,
        large_send,
        grad_queries,
        keys_total,
        values_total,
        padded,
        rim_queries,
        rim_counts,
        grad_low,
        grad_high,
        first_in,
        attended,
        grad_stream,
        features,
        pack,
        mod,
        attn_bf,
        table_two,
    )
    def chain_large(step, *tokens):
        nonlocal large_keep, large_send, large_got
        large_keep, large_send = receive(large_keep, large_got, *tokens)
        large_got = swap(large_send, *large_routes[step])

    def chain_small(step, *tokens):
        nonlocal small_keep, small_send, small_got
        small_keep, small_send = receive(small_keep, small_got, *tokens)
        small_got = swap(small_send, *small_routes[step])

    small_keep, small_send = small_kept, small_sent
    small_got = swap(small_send, 2)
    chain_large(2, small_sent)
    chain_small(0, large_send)
    large_total = rounded_total(large_keep, large_got, small_send)
    large_got = swap(large_total, *large_routes[3])
    chain_small(1, large_total)
    large_part = blend(large_total, large_got, large_past, small_send)
    large_got = swap(large_part, *large_routes[2])
    chain_small(2, large_part)
    large_part = join(large_part, large_got, small_send)
    large_got = swap(large_part, *large_routes[1])
    small_total = rounded_total(small_keep, small_got, large_part)
    small_got = swap(small_total, *small_routes[3])
    large_part = join(large_part, large_got, small_total)
    large_got = swap(large_part, *large_routes[0])
    small_part = blend(small_total, small_got, small_past, large_part, work=8e9)
    small_got = swap(small_part, *small_routes[2])
    small_part = join(small_part, small_got, work=1e3)
    small_got = swap(small_part, *small_routes[1])

    any_space = pl.BlockSpec(memory_space=pl.ANY)
    gathered_shape = (2, 2, 2, 128, CHUNK)
    large_work, large_mix = pl.pallas_call(
        large_first_kernel,
        out_shape=(struct((4, D, CHUNK), bf16), struct((2, D, CHUNK), bf16)),
        in_specs=[SMEM, VMEM, VMEM, any_space],
        out_specs=(VMEM,) * 2,
        scratch_shapes=[pltpu.VMEM((D, D), bf16)],
        cost_estimate=cost(1e3, 1e3),
        name="ortho_large",
        compiler_params=room(10),
    )(scalars, large_part.reshape(gathered_shape), large_got.reshape(gathered_shape), small_part)
    mix_got = swap(large_mix, 2)
    small_part = join(small_part, small_got, large_work)
    small_got = swap(small_part, *small_routes[0])
    large_result = pl.pallas_call(
        large_next_kernel,
        out_shape=struct((2, D, CHUNK), bf16),
        in_specs=[VMEM, any_space],
        out_specs=VMEM,
        scratch_shapes=[pltpu.VMEM((4, D, CHUNK), bf16), pltpu.VMEM((D, D), bf16)],
        cost_estimate=cost(1e3, 1e3),
        name="ortho_large",
        compiler_params=room(10),
    )(large_work, small_part)
    result_got = swap(large_result, 2)

    across = pl.BlockSpec((1, D, 256), lambda g: (g // 2, 0, g % 2))
    left_right = pl.BlockSpec((D, 256), lambda g: (0, g))
    top_bottom = pl.BlockSpec((256, D), lambda g: (g, 0))
    large_shapes = (struct((D, 2 * CHUNK), f32), struct((2 * CHUNK, D), f32))
    small_token = struct((8, 128), f32)
    token_block = pl.BlockSpec((8, 128), lambda g: (0, 0))
    up_moment_new, down_moment_new, moments_done = pl.pallas_call(
        large_moment_kernel,
        grid=(4,),
        out_shape=large_shapes + (small_token,),
        in_specs=[SMEM, across, across, left_right, top_bottom, any_space],
        out_specs=(left_right, top_bottom, token_block),
        cost_estimate=cost(1e3, 1e3),
        name="moment_large",
        compiler_params=room(8),
    )(scalars, large_mix, mix_got, up_moment, down_moment, large_result)

    small_work, small_mix = pl.pallas_call(
        small_start_kernel,
        out_shape=(
            struct((2, 2, 256, D), bf16),
            struct((2, 256 + TABLE_ROWS, D), bf16),
        ),
        in_specs=[SMEM, VMEM, VMEM, any_space],
        out_specs=(VMEM,) * 2,
        scratch_shapes=[pltpu.VMEM((TABLE_ROWS, D), f32)],
        cost_estimate=cost(3e10, 1e3),
        name="unpack_small",
        compiler_params=room(6),
    )(
        scalars,
        small_part.reshape(2, 2, 2, 80, D),
        small_got.reshape(2, 2, 2, 80, D),
        moments_done,
    )
    mix_other = swap(small_mix, 2)

    def fixed(*shape):
        return pl.BlockSpec(shape, lambda g: (0,) * len(shape))

    def one(index):
        return pl.BlockSpec((1, 256, D), index)

    small_result, up_new, down_new = pl.pallas_call(
        small_kernel,
        grid=(NS_STEPS,),
        out_shape=(struct((2, 256, D), bf16),) + large_shapes,
        in_specs=[SMEM, fixed(2, 2, 256, D), across, across, left_right, top_bottom, any_space],
        out_specs=(fixed(2, 256, D), left_right, top_bottom),
        scratch_shapes=[pltpu.VMEM((2, 256, D), bf16)] * 2
        + [pltpu.VMEM((D, D), bf16)] * 2
        + [pltpu.SMEM((2,), f32)],
        cost_estimate=cost(6e9, 1e7),
        name="ortho_small",
        compiler_params=room(16),
    )(scalars, small_work, large_result, result_got, up_weight, down_weight, moments_done)
    small_other = swap(small_result, 2)
    table_block = pl.BlockSpec((1, TABLE_ROWS, D), lambda g: (0, 256 // TABLE_ROWS, 0))
    attention_moment_new, modulation_moment_new, modulation_new, moment_done = pl.pallas_call(
        functools.partial(small_moment_kernel, nodes=row_count * device_count),
        grid=(4,),
        out_shape=(struct((4, 256, D), f32),) + (struct((2, 2, D), f32),) * 2 + (small_token,),
        in_specs=[
            SMEM,
            one(lambda g: (g % 2, 0, 0)),
            one(lambda g: (g % 2, 0, 0)),
            one(lambda g: (g, 0, 0)),
            table_block,
            table_block,
            fixed(2, 4, D),
            fixed(2, 2, D),
            any_space,
        ],
        out_specs=(one(lambda g: (g, 0, 0)), fixed(2, 2, D), fixed(2, 2, D), token_block),
        cost_estimate=cost(1e10, 1e7),
        name="moment_small",
        compiler_params=room(8),
    )(
        scalars,
        small_mix,
        mix_other,
        attention_moment,
        small_mix,
        mix_other,
        modulation,
        modulation_moment,
        small_result,
    )
    attention_new = pl.pallas_call(
        small_weight_kernel,
        grid_spec=pltpu.PrefetchScalarGridSpec(
            num_scalar_prefetch=1,
            grid=(4,),
            in_specs=[
                pl.BlockSpec((1, 256, D), lambda g, s: (g % 2, 0, 0)),
                pl.BlockSpec((1, 256, D), lambda g, s: (g % 2, 0, 0)),
                pl.BlockSpec((1, 256, D), lambda g, s: (g, s[4], 0)),
                any_space,
            ],
            out_specs=pl.BlockSpec((1, 256, D), lambda g, s: (g, 0, 0)),
        ),
        out_shape=struct((4, 256, D), f32),
        cost_estimate=cost(1e7, 6e6),
        name="update_small",
        compiler_params=room(6),
    )(scalars, small_result, small_other, attention_weight, moment_done)
    return (
        output,
        features_grad,
        attention_moment_new,
        attention_new,
        up_moment_new,
        up_new,
        down_moment_new,
        down_new,
        modulation_moment_new,
        modulation_new,
    )


def solution(mesh):
    placed = (
        P(("nodes", "hid"), None),
        P(("nodes", "hid")),
        P(("nodes", "hid"), None),
        P(("nodes", "hid")),
        P(("nodes", "hid"), None),
        P(),
        P(None, "hid"),
        P("hid", None),
        P(),
        P(None, "hid", None),
        P(None, "hid"),
        P("hid", None),
        P(None, "hid", None),
    )
    return jax.shard_map(
        on_device,
        mesh=mesh,
        in_specs=placed,
        out_specs=(
            P(("nodes", "hid"), None),
            P(("nodes", "hid"), None),
            P(None, "hid", None),
            P(None, "hid", None),
            P(None, "hid"),
            P(None, "hid"),
            P("hid", None),
            P("hid", None),
            P(None, "hid", None),
            P(None, "hid", None),
        ),
        check_vma=False,
    )
```

```python
import functools
import math

import jax
import jax.numpy as jnp
from jax import lax
from jax.experimental import pallas as pl
from jax.experimental.pallas import tpu as pltpu
from jax.sharding import PartitionSpec as P

D = 512
HEADS = 4
HD = 128
FF = 2048
K = 16
NS_STEPS = 4
HALO = 192
BLOCK = 128
SPAN = BLOCK + 2 * HALO
RIM = 256
CHUNK = 512
TABLE_ROWS = 16

f32 = jnp.float32
bf16 = jnp.bfloat16
ns_first = 3.4445
ns_second = -4.775
ns_third = 2.0315
momentum_rate = 0.95
vector_rate = 0.9
muon_rate = 0.2
decay_rate = 0.1
score_scale = 1.0 / math.sqrt(HD)
AXES = ("nodes", "hid")
VMEM = pl.BlockSpec(memory_space=pltpu.VMEM)
SMEM = pl.BlockSpec(memory_space=pltpu.SMEM)


def nn(a, b):
    return lax.dot_general(a, b, (((1,), (0,)), ((), ())), preferred_element_type=f32)


def nt(a, b):
    return lax.dot_general(a, b, (((1,), (1,)), ((), ())), preferred_element_type=f32)


def tn(a, b):
    return lax.dot_general(a, b, (((0,), (0,)), ((), ())), preferred_element_type=f32)


def struct(shape, dtype):
    return jax.ShapeDtypeStruct(shape, dtype)


def rows_of(start, size):
    return pl.ds(pl.multiple_of(start, size), size)


def cost(flops, data):
    return pl.CostEstimate(flops=int(flops), bytes_accessed=int(data), transcendentals=0)


def room(mebibytes):
    return pltpu.CompilerParams(vmem_limit_bytes=mebibytes << 20)


def norm_parts(field):
    average = jnp.mean(field, axis=-1, keepdims=True)
    centred = field - average
    variance = jnp.mean(centred * centred, axis=-1, keepdims=True)
    inverse = lax.rsqrt(variance + 1e-06)
    return centred * inverse, inverse


def table_rows(mod_ref, level, column):
    return jnp.where(level > 0.5, mod_ref[1, column : column + 1, :], mod_ref[0, column : column + 1, :])


def modulated(field, level, mod_ref, column):
    normed, _ = norm_parts(field)
    return normed * (1.0 + table_rows(mod_ref, level, column)) + table_rows(
        mod_ref, level, column + 1
    )


def norm_back(grad_out, field, level, mod_ref, column):
    normed, inverse = norm_parts(field)
    grad_norm = grad_out * (1.0 + table_rows(mod_ref, level, column))
    grad_in = inverse * (
        grad_norm
        - jnp.mean(grad_norm, axis=-1, keepdims=True)
        - normed * jnp.mean(grad_norm * normed, axis=-1, keepdims=True)
    )
    return grad_in, grad_out * normed


def add_table(table_ref, column, level, scale_term, shift_term):
    upper = level > 0.5
    for term, place in ((scale_term, column), (shift_term, column + 1)):
        low_part = jnp.sum(jnp.where(upper, 0.0, term), axis=0, keepdims=True)
        high_part = jnp.sum(jnp.where(upper, term, 0.0), axis=0, keepdims=True)
        table_ref[place : place + 1, :] += low_part
        table_ref[4 + place : 5 + place, :] += high_part


def slot_counts(pack, row_count, width, shift):
    pieces = []
    for left in range(0, width, 128):
        lanes = lax.broadcasted_iota(jnp.int32, (row_count, 128), 1)
        rows = lax.broadcasted_iota(jnp.int32, (row_count, 128), 0)
        place = (lanes - rows + (left - shift)).astype(f32)
        total = jnp.zeros((row_count, 128), f32)
        for slot in range(K):
            total = total + jnp.where(place == pack[:, slot : slot + 1], 1.0, 0.0)
        pieces.append(total)
    return jnp.concatenate(pieces, axis=1).astype(bf16)


def quarter_kernel(scalars, up, down, token, rounded):
    rounded[0] = up[...].astype(bf16)
    rounded[1] = down[...].astype(bf16)


def past_kernel(scalars, up, down, attention, large_past, small_past):
    z2 = scalars[3]
    large = jnp.where(scalars[0] == 0, up[...], down[...].T)
    for j in range(2):
        large_past[j ^ z2] = large[j * 128 : (j + 1) * 128]
        small_past[j ^ z2] = attention[0, j * 64 : (j + 1) * 64, :]


def project_kernel(features, pack, mod, weights, first_in, qkv, counts, rounded):
    row_count = features.shape[0]
    turn = pl.program_id(0)

    @pl.when(turn == 0)
    def _():
        for start in range(0, row_count, 256):
            rows = slice(start, start + 256)
            level = pack[rows, K : K + 1]
            first_in[rows, :] = modulated(features[rows, :].astype(f32), level, mod, 0).astype(bf16)

    weight = weights[0].astype(bf16)
    rounded[0] = weight

    @pl.when(turn < 3)
    def _():
        qkv[turn] = nn(first_in[...], weight).astype(bf16)
        share = row_count // BLOCK // 3

        def count_step(b, carry):
            rows = rows_of(b * BLOCK, BLOCK)
            counts[rows, :] = slot_counts(pack[rows, :], BLOCK, SPAN, HALO)
            return carry

        lax.fori_loop(turn * share, (turn + 1) * share, count_step, 0)


def forward_kernel(
    rim_low,
    rim_high,
    features,
    pack,
    mod,
    weights,
    qkv,
    counts,
    attended,
    stream,
    second_in,
    padded,
    rim_queries,
    rim_counts,
    log_totals,
    rim_in,
):
    row_count = features.shape[0]
    for side, rim in enumerate((rim_low, rim_high)):

        def rim_step(b, carry):
            rows = rows_of(b * 64, 64)
            target = pl.ds(pl.multiple_of(side * HALO + b * 64, 64), 64)
            info = rim[rows, D:].astype(f32)
            rim_in[target, :] = modulated(
                rim[rows, :D].astype(f32), info[:, K : K + 1], mod, 0
            ).astype(bf16)
            rim_counts[target, :] = slot_counts(
                info, 64, RIM, b * 64 + (-HALO if side == 0 else RIM)
            )
            return carry

        lax.fori_loop(0, HALO // 64, rim_step, 0)
    rim_queries[...] = nn(rim_in[...], weights[0]).astype(bf16)
    for p in range(2):
        piece = nn(rim_in[...], weights[1 + p]).astype(bf16)
        padded[p, :HALO, :] = piece[:HALO]
        padded[p, HALO + row_count :, :] = piece[HALO:]
        padded[p, HALO : HALO + row_count, :] = qkv[1 + p]

    def step(b, carry):
        rows = rows_of(b * BLOCK, BLOCK)
        span = pl.ds(pl.multiple_of(b * BLOCK, BLOCK), SPAN)
        count = counts[rows, :].astype(f32)
        live = count > 0.0
        columns = [slice(h * HD, (h + 1) * HD) for h in range(HEADS)]
        scores = [nt(qkv[0, rows, cols], padded[0, span, cols]) * score_scale for cols in columns]
        lanes = lax.broadcasted_iota(jnp.int32, (BLOCK, 128), 1)
        stats = jnp.zeros((BLOCK, 128), f32)
        for h, cols in enumerate(columns):
            masked = jnp.where(live, scores[h], -1e30)
            peak = jnp.max(masked, axis=-1, keepdims=True)
            exponent = jnp.exp(masked - peak)
            total = jnp.sum(exponent * count, axis=-1, keepdims=True)
            probs = (exponent * (1.0 / total)).astype(bf16)
            spread = probs * counts[rows, :]
            attended[rows, cols] = nn(spread, padded[1, span, cols]).astype(bf16)
            stats = jnp.where(lanes == h, peak + jnp.log(total), stats)
        log_totals[rows, :] = stats
        return carry

    lax.fori_loop(0, row_count // BLOCK, step, 0)
    for start in range(0, row_count, 256):
        rows = slice(start, start + 256)
        field = features[rows, :].astype(f32) + nn(attended[rows, :], weights[3])
        stream[rows, :] = field
        second_in[rows, :] = modulated(field, pack[rows, K : K + 1], mod, 2).astype(bf16)


def mlp_chunk(
    scalars, second_in, cotangent, up, down, branch_in, grad_in, branch, grad_second, acts, grads, kept, sent
):
    row_count = second_in.shape[0]
    for start in range(0, row_count, 256):
        rows = slice(start, start + 256)
        preact = nn(second_in[rows, :], up)
        grad_act = nt(cotangent[rows, :], down)
        sigmoid = 0.5 * jnp.tanh(0.5 * preact) + 0.5
        act = (preact * sigmoid).astype(bf16)
        acts[rows, :] = act
        grad_pre = (grad_act * (sigmoid * (1.0 + preact * (1.0 - sigmoid)))).astype(bf16)
        grads[rows, :] = grad_pre
        branch[rows, :] = branch_in[rows, :] + nn(act, down)
        grad_second[rows, :] = grad_in[rows, :] + nt(grad_pre, up)
    first, z1, z2 = scalars[0] == 0, scalars[2], scalars[3]
    for out, swapped in ((kept, False), (sent, True)):
        ups = jnp.logical_not(first) if swapped else first
        product = tn(
            jnp.where(ups, second_in[...], cotangent[...]), jnp.where(ups, grads[...], acts[...])
        )
        for q in range(4):
            out[0, (q // 2) ^ z1, (q % 2) ^ z2] = product[q * 128 : (q + 1) * 128].astype(bf16)


def mlp_own_kernel(
    scalars, second_in, cotangent, up, down, token, branch, grad_second, kept, sent, acts, grads
):
    @pl.when(pl.program_id(0) == 0)
    def _():
        branch[...] = jnp.zeros_like(branch)
        grad_second[...] = jnp.zeros_like(grad_second)

    mlp_chunk(
        scalars,
        second_in,
        cotangent,
        up[...].astype(bf16),
        down[...].astype(bf16),
        branch,
        grad_second,
        branch,
        grad_second,
        acts,
        grads,
        kept,
        sent,
    )


def mlp_near_kernel(
    scalars, second_in, cotangent, near, branch_in, grad_in, branch, grad_second, kept, sent, acts, grads
):
    mlp_chunk(
        scalars,
        second_in,
        cotangent,
        near[0],
        near[1],
        branch_in,
        grad_in,
        branch,
        grad_second,
        acts,
        grads,
        kept,
        sent,
    )


def mlp_far_kernel(
    scalars,
    second_in,
    cotangent,
    far,
    branch_in,
    grad_in,
    stream,
    pack,
    mod,
    weights,
    attended,
    log_totals,
    kept_in,
    sent_in,
    kept,
    sent,
    output,
    grad_stream,
    grad_attended,
    stats,
    edge_low,
    edge_high,
    table,
    branch,
    grad_second,
    acts,
    grads,
):
    row_count = second_in.shape[0]
    mlp_chunk(
        scalars,
        second_in,
        cotangent,
        far[0],
        far[1],
        branch_in,
        grad_in,
        branch,
        grad_second,
        acts,
        grads,
        kept,
        sent,
    )
    table[...] = jnp.zeros_like(table)

    for start in range(0, row_count, 256):
        rows = slice(start, start + 256)
        field = stream[rows, :]
        level = pack[rows, K : K + 1]
        output[rows, :] = (field + branch[rows, :]).astype(bf16)
        gradient = grad_second[rows, :]
        grad_field, scale_term = norm_back(gradient, field, level, mod, 2)
        add_table(table, 2, level, scale_term, gradient)
        total = cotangent[rows, :].astype(f32) + grad_field
        grad_stream[rows, :] = total
        back = nt(total.astype(bf16), weights[3]).astype(bf16)
        grad_attended[rows, :] = back
        product = back.astype(f32) * attended[rows, :].astype(f32)
        lanes = lax.broadcasted_iota(jnp.int32, (256, 128), 1)
        kept_stats = log_totals[rows, :]
        for h in range(HEADS):
            delta = jnp.sum(product[:, h * HD : (h + 1) * HD], axis=-1, keepdims=True)
            kept_stats = jnp.where(lanes == HEADS + h, delta, kept_stats)
        stats[rows, :] = kept_stats
    for edge, first in ((edge_low, 0), (edge_high, row_count - HALO)):
        rows = slice(first, first + HALO)
        edge[:, :D] = grad_attended[rows, :]
        known = stats[rows, :]
        upper = known.astype(bf16)
        lower = (known - upper.astype(f32)).astype(bf16).astype(f32)
        edge[:, D:] = (upper.astype(f32) + pltpu.roll(lower, 2 * HEADS, 1)).astype(bf16)


def attention_terms(scores, grad_probs, live, count, log_total, delta):
    probs = jnp.exp(jnp.where(live, scores * score_scale, -1e30) - log_total)
    slopes = (probs * (grad_probs - delta)).astype(bf16)
    return slopes * count, probs.astype(bf16) * count


def backward_kernel(qkv, padded, grad, stats, counts, token, grad_query, keys_total, values_total):
    keys_total[...] = jnp.zeros_like(keys_total)
    values_total[...] = jnp.zeros_like(values_total)

    def step(b, carry):
        rows = rows_of(b * BLOCK, BLOCK)
        span = pl.ds(pl.multiple_of(b * BLOCK, BLOCK), SPAN)
        count = counts[rows, :]
        live = count.astype(f32) > 0.0
        columns = [slice(h * HD, (h + 1) * HD) for h in range(HEADS)]
        products = [
            (nt(qkv[0, rows, cols], padded[0, span, cols]), nt(grad[rows, cols], padded[1, span, cols]))
            for cols in columns
        ]
        terms = [
            attention_terms(
                *products[h],
                live,
                count,
                stats[rows, h : h + 1],
                stats[rows, HEADS + h : HEADS + h + 1],
            )
            for h in range(HEADS)
        ]
        for (slopes, spread), cols in zip(terms, columns):
            grad_query[rows, cols] = (nn(slopes, padded[0, span, cols]) * score_scale).astype(bf16)
            keys_total[span, cols] += tn(slopes, qkv[0, rows, cols])
            values_total[span, cols] += tn(spread, grad[rows, cols])
        return carry

    lax.fori_loop(0, counts.shape[0] // BLOCK, step, 0)


def weights_kernel(
    scalars,
    token,
    queries_in,
    keys_in,
    values_in,
    padded,
    rim_query,
    rim_counts,
    grad_low,
    grad_high,
    first_in,
    attended,
    grad_stream,
    features,
    pack,
    mod,
    weights,
    table_two,
    features_grad,
    kept,
    sent,
    gathered,
    table,
    keys_total,
    values_total,
    blocks,
):
    row_count = first_in.shape[0]
    columns = [slice(h * HD, (h + 1) * HD) for h in range(HEADS)]
    own = slice(HALO, HALO + row_count)
    keys_total[...] = keys_in[own, :]
    values_total[...] = values_in[own, :]
    for side, grads in enumerate((grad_low, grad_high)):
        first = 0 if side == 0 else row_count - RIM
        own_span = slice(first, first + RIM)
        span = slice(HALO + first, HALO + first + RIM)
        rows = slice(side * HALO, (side + 1) * HALO)
        known = grads[:, D:].astype(f32)
        count = rim_counts[rows, :]
        live = count.astype(f32) > 0.0
        products = [
            (nt(rim_query[rows, cols], padded[0, span, cols]), nt(grads[:, cols], padded[1, span, cols]))
            for cols in columns
        ]
        terms = []
        for h in range(HEADS):
            numbers = [known[:, i * HEADS + h : i * HEADS + h + 1] for i in range(4)]
            terms.append(
                attention_terms(*products[h], live, count, numbers[0] + numbers[2], numbers[1] + numbers[3])
            )
        for (slopes, spread), cols in zip(terms, columns):
            keys_total[own_span, cols] += tn(slopes, rim_query[rows, cols])
            values_total[own_span, cols] += tn(spread, grads[:, cols])
    gathered[0] = queries_in[...]
    gathered[1] = (keys_total[...] * score_scale).astype(bf16)
    gathered[2] = values_total[...].astype(bf16)
    table[...] = table_two[...]
    for start in range(0, row_count, 256):
        rows = slice(start, start + 256)
        level = pack[rows, K : K + 1]
        gradient = nt(gathered[0, rows, :], weights[0])
        for p in range(1, 3):
            gradient = gradient + nt(gathered[p, rows, :], weights[p])
        grad_field, scale_term = norm_back(gradient, features[rows, :].astype(f32), level, mod, 0)
        add_table(table, 0, level, scale_term, gradient)
        total = grad_stream[rows, :]
        features_grad[rows, :] = total + grad_field
        gathered[3, rows, :] = total.astype(bf16)
    core, slot_bit, z1, z2, hid = (scalars[i] for i in range(5))

    def product_step(n, carry):
        away, slot = n // 2, n % 2
        target = core ^ away
        p = 2 * target + slot
        product = tn(jnp.where(p < 3, first_in[...], attended[...]), gathered[p])
        for half in range(2):
            for q in range(4):
                slot_at, hid_at, row_half = slot ^ slot_bit, half ^ hid, (q // 2) ^ z1
                index = (
                    away,
                    jnp.where(target == 0, slot_at, row_half),
                    hid_at,
                    jnp.where(target == 0, row_half, slot_at),
                    (q % 2) ^ z2,
                )
                start = half * 256 + q * 64
                blocks[index + (slice(0, 64),)] = product[start : start + 64].astype(bf16)
                row = (q // 2) * 4 + 2 * half + q % 2
                known = jnp.broadcast_to(table[row : row + 1, :], (TABLE_ROWS, D))
                blocks[index + (slice(64, 80),)] = jnp.where(p == 0, known, 0.0).astype(bf16)
        return carry

    lax.fori_loop(0, 4, product_step, 0)
    kept[...] = blocks[0]
    sent[...] = blocks[1]


def large_sum_kernel(scalars, own, own_got, rest, rest_got, keep, send):
    first = scalars[0] == 0
    for away, out in ((0, keep), (1, send)):
        for source, got, h in ((own, own_got, 0), (rest, rest_got, 1)):
            for i in range(2):
                where_from = (jnp.where(first, away, i), jnp.where(first, i, away))
                where_to = (jnp.where(first, h, i), jnp.where(first, i, h))
                total = source[where_from].astype(f32) + got[where_from].astype(f32)
                out[where_to] = total.astype(out.dtype)


def receive_kernel(*refs):
    kept, got, keep, send = refs[0], refs[1], refs[-2], refs[-1]
    keep[...] = kept[0].astype(f32) + got[0].astype(f32)
    send[...] = (kept[1].astype(f32) + got[1].astype(f32)).astype(bf16)


def total_kernel(*refs):
    kept, got, total = refs[0], refs[1], refs[-1]
    total[...] = (kept[...] + got[...].astype(f32)).astype(bf16)


def blend_kernel(flip, *refs):
    kept, got, past, part = refs[0], refs[1], refs[2], refs[-1]
    rows = past.shape[1]
    for j in range(2):
        total = kept[j].astype(f32) + got[j ^ flip].astype(f32)
        blended = (1.0 + momentum_rate) * total[:rows] + momentum_rate * momentum_rate * past[j]
        part[j, :rows, :] = blended.astype(bf16)
        if rows < part.shape[1]:
            part[j, rows:, :] = total[rows:].astype(bf16)


def join_kernel(*refs):
    part, got, pieces = refs[0], refs[1], refs[-1]
    pieces[0] = part[...]
    pieces[1] = got[...]


def newton_schulz(groups, polys, rows_first, scales):
    blocks = [[[ref[i] for i in half] for half in halves] for ref, halves in groups]
    grams = []
    for halves, scale in zip(blocks, scales):
        sums = []
        for half in halves:
            total = None
            for block in half:
                term = tn(block, block) if rows_first else nt(block, block)
                total = term if total is None else total + term
            sums.append((total if scale is None else total * (scale * scale)).astype(bf16))
        grams.append((sums[0].astype(f32) + sums[1].astype(f32)).astype(bf16))
    for gram, poly in zip(grams, polys):
        poly[...] = (ns_second * gram.astype(f32) + ns_third * nn(gram, gram)).astype(bf16)
    for (ref, halves), values, poly, scale in zip(groups, blocks, polys, scales):
        for half, half_values in zip(halves, values):
            for i, block in zip(half, half_values):
                other = nn(block, poly[...]) if rows_first else nn(poly[...], block)
                total = ns_first * block.astype(f32) + other
                ref[i] = (total if scale is None else total * scale).astype(bf16)


def large_start_kernel(scalars, kept, got, work, poly):
    core, slot_bit, z1, z2 = (scalars[i] for i in range(4))
    total = jnp.zeros((8, D), f32)
    for n in range(16):
        b1, b2, b3, b4 = n // 8, (n // 4) % 2, (n // 2) % 2, n % 2
        source = kept if b1 == 0 else got
        block = source[b2, b3, b4]
        value = block.astype(f32)
        total = total + jnp.sum((value * value).reshape(16, 8, D), axis=0)
        slot = jnp.where(core == 0, b1, b2)
        half = jnp.where(core == 0, b2, b3)
        row_half = jnp.where(core == 0, b3, b1)
        start = ((row_half ^ z1) * 2 + (b4 ^ z2)) * 128
        work[half * 2 + (slot ^ slot_bit), rows_of(start, 128), :] = block
    return 1.0 / (jnp.sqrt(jnp.sum(total)) + 1e-07)


large_halves = ((0, 1), (2, 3))


def large_first_kernel(scalars, kept, got, token, work, blend, poly):
    scale = large_start_kernel(scalars, kept, got, work, poly)
    for s in range(2):
        blend[s] = work[s]

    def step(i, factor):
        newton_schulz([(work, large_halves)], [poly], False, [factor])
        return jnp.ones((), f32)

    lax.fori_loop(0, NS_STEPS // 2, step, scale)


def large_next_kernel(given, token, result, work, poly):
    work[...] = given[...]

    def step(i, carry):
        newton_schulz([(work, large_halves)], [poly], False, [None])
        return carry

    lax.fori_loop(NS_STEPS // 2, NS_STEPS, step, 0)
    for s in range(2):
        result[s] = work[s]


def small_start_kernel(scalars, kept, got, token, work, blend, table):
    table[...] = jnp.zeros_like(table)
    core, slot_bit, z1, z2 = (scalars[i] for i in range(4))
    for n in range(16):
        b1, b2, b3, b4 = n // 8, (n // 4) % 2, (n // 2) % 2, n % 2
        source = kept if b1 == 0 else got
        block = source[b2, b3, b4]
        slot = jnp.where(core == 0, b1, b3) ^ slot_bit
        half = b2
        row_half = jnp.where(core == 0, b3, b1)
        quarter = (row_half ^ z1) * 2 + (b4 ^ z2)
        work[slot, half, rows_of(quarter * 64, 64), :] = block[:64]

        @pl.when((slot == 0) & (half == 0))
        def _():
            table[pl.ds(quarter, 1), :] = block[64:].astype(f32)[:1]

    for s in range(2):
        blend[s, :256, :] = work[s, 0]
        blend[s, 256:, :] = table[...].astype(bf16)


def small_kernel(
    scalars,
    given,
    own,
    got,
    up_weight,
    down_weight,
    token,
    result,
    up_new,
    down_new,
    first,
    second,
    poly_first,
    poly_second,
    factors,
):
    turn = pl.program_id(0)
    works = (first, second)

    @pl.when(turn == 0)
    def _():
        for s, work in enumerate(works):
            total = jnp.zeros((8, D), f32)
            for half in range(2):
                block = given[s, half]
                work[half] = block
                value = block.astype(f32)
                total = total + jnp.sum((value * value).reshape(32, 8, D), axis=0)
            factors[s] = 1.0 / (jnp.sqrt(jnp.sum(total)) + 1e-07)

    groups = [(work, ((0,), (1,))) for work in works]
    scales = [jnp.where(turn == 0, factors[s], 1.0) for s in range(2)]
    newton_schulz(groups, [poly_first, poly_second], True, scales)
    is_up = scalars[0] == 0
    ups = jnp.where(is_up, own[0], got[0])
    downs = jnp.where(is_up, got[0], own[0])
    up_new[...] = new_weight(up_weight[...], ups.astype(f32), FF)
    down_new[...] = new_weight(down_weight[...], downs.T.astype(f32), FF)

    @pl.when(turn == NS_STEPS - 1)
    def _():
        for s, work in enumerate(works):
            result[s] = work[0]


def new_moment(blend, moment):
    share = 1.0 / (1.0 + momentum_rate)
    return share * blend + (momentum_rate - share * momentum_rate * momentum_rate) * moment


def new_weight(weight, ortho, longest):
    return weight - muon_rate * (0.2 * math.sqrt(longest) * ortho + decay_rate * weight)


def large_moment_kernel(scalars, own, got, up_moment, down_moment, token, up_moment_new, down_moment_new, done):
    done[...] = jnp.zeros_like(done)
    first = scalars[0] == 0
    ups, downs = jnp.where(first, own[0], got[0]), jnp.where(first, got[0], own[0])
    up_moment_new[...] = new_moment(ups.astype(f32), up_moment[...])
    down_moment_new[...] = new_moment(downs.T.astype(f32), down_moment[...])


def small_moment_kernel(
    scalars,
    mix,
    mix_got,
    moment,
    table,
    table_got,
    modulation,
    held_moment,
    token,
    moment_new,
    held_moment_new,
    held_new,
    done,
    *,
    nodes,
):
    done[...] = jnp.zeros_like(done)
    core, turn = scalars[0], pl.program_id(0)
    blend = jnp.where(core == turn // 2, mix[0], mix_got[0]).astype(f32)
    moment_new[0] = new_moment(blend, moment[0])

    @pl.when(turn == 0)
    def _():
        total = jnp.where(core == 0, table[0], table_got[0]).astype(f32)
        for level in range(2):
            for column in range(2):
                row = level * 2 + column
                at = (slice(level, level + 1), slice(column, column + 1))
                value = vector_rate * held_moment[at] + total[row : row + 1, :].reshape(1, 1, D)
                held = modulation[level : level + 1, pl.ds(scalars[4] * 2 + column, 1)]
                held_moment_new[at] = value
                held_new[at] = held - 0.2 / math.sqrt(nodes) * value


def small_weight_kernel(scalars, own, got, weight, token, weight_new):
    mine = scalars[0] == pl.program_id(0) // 2
    ortho = jnp.where(mine, own[0].astype(f32), got[0].astype(f32))
    weight_new[0] = new_weight(weight[0], ortho, D)


def on_device(
    features,
    levels,
    neighbour_index,
    neighbour_count,
    cotangent,
    attention_weight,
    up_weight,
    down_weight,
    modulation,
    attention_moment,
    up_moment,
    down_moment,
    modulation_moment,
):
    row_count = features.shape[0]
    device_count = lax.axis_size(AXES)
    me = lax.axis_index(AXES)
    first_row = me * row_count

    def bit(place):
        return (me >> place) & 1

    hid, core, slot_bit, z1, z2 = (bit(place) for place in range(5))
    scalars = jnp.stack([core, slot_bit, z1, z2, hid]).astype(jnp.int32)
    is_first = core == 0

    def along(value, distance):
        pairs = [(i, i + distance) for i in range(device_count) if 0 <= i + distance < device_count]
        return lax.ppermute(value, AXES, pairs)

    def after(value, *others):
        return lax.optimization_barrier((value,) + others)[0]

    def swap(value, mask, other=None):
        masks = (mask, mask if other is None else other)
        pairs = [(i, i ^ masks[(i // 2) % 2]) for i in range(device_count)]
        return lax.ppermute(value, AXES, pairs)

    live = jnp.arange(K, dtype=jnp.int32)[None, :] < neighbour_count[:, None]
    row_ids = first_row + jnp.arange(row_count, dtype=jnp.int32)[:, None]
    offsets = jnp.where(live, neighbour_index - row_ids, 512)
    pack = jnp.concatenate(
        [offsets, levels[:, None], jnp.zeros((row_count, 128 - K - 1), jnp.int32)], axis=1
    ).astype(f32)
    rims = jnp.concatenate([features, pack.astype(bf16)], axis=1)
    low_edge, high_edge = rims[row_count - HALO :], rims[:HALO]
    rim_low = along(low_edge, 1)
    rim_high = along(high_edge, -1)

    pack, scalars, is_first = lax.optimization_barrier((pack, scalars, is_first))
    mod = modulation

    quarter = pl.pallas_call(
        quarter_kernel,
        grid_spec=pltpu.PrefetchScalarGridSpec(
            num_scalar_prefetch=1,
            grid=(1,),
            in_specs=[
                pl.BlockSpec((D, CHUNK), lambda g, s: (0, s[0])),
                pl.BlockSpec((CHUNK, D), lambda g, s: (s[0], 0)),
                pl.BlockSpec(memory_space=pl.ANY),
            ],
            out_specs=pl.BlockSpec((2, D, CHUNK), lambda g, s: (0, 0, 0)),
        ),
        out_shape=struct((2, D, CHUNK), bf16),
        cost_estimate=cost(1e6, 3e6),
        name="quarter",
        compiler_params=room(8),
    )(scalars, up_weight, down_weight, low_edge)
    large_past, small_past = pl.pallas_call(
        past_kernel,
        grid_spec=pltpu.PrefetchScalarGridSpec(
            num_scalar_prefetch=1,
            grid=(1,),
            in_specs=[
                pl.BlockSpec((256, CHUNK), lambda g, s: (s[2], s[1])),
                pl.BlockSpec((CHUNK, 256), lambda g, s: (s[1], s[2])),
                pl.BlockSpec((1, 128, D), lambda g, s: (s[0] * 2 + s[1], s[2], 0)),
            ],
            out_specs=(
                pl.BlockSpec((2, 128, CHUNK), lambda g, s: (0, 0, 0)),
                pl.BlockSpec((2, 64, D), lambda g, s: (0, 0, 0)),
            ),
        ),
        out_shape=(struct((2, 128, CHUNK), f32), struct((2, 64, D), f32)),
        cost_estimate=cost(1e6, 1e6),
        name="past",
        compiler_params=room(4),
    )(scalars, up_moment, down_moment, attention_moment)
    first_in, qkv, counts, attn_bf = pl.pallas_call(
        project_kernel,
        grid=(4,),
        out_shape=(
            struct((row_count, D), bf16),
            struct((3, row_count, D), bf16),
            struct((row_count, SPAN), bf16),
            struct((4, D, D), bf16),
        ),
        in_specs=[
            pl.BlockSpec((row_count, D), lambda g: (0, 0)),
            pl.BlockSpec((row_count, 128), lambda g: (0, 0)),
            pl.BlockSpec((2, 4, D), lambda g: (0, 0, 0)),
            pl.BlockSpec((1, D, D), lambda g: (g, 0, 0)),
        ],
        out_specs=(
            pl.BlockSpec((row_count, D), lambda g: (0, 0)),
            pl.BlockSpec((3, row_count, D), lambda g: (0, 0, 0)),
            pl.BlockSpec((row_count, SPAN), lambda g: (0, 0)),
            pl.BlockSpec((1, D, D), lambda g: (g, 0, 0)),
        ),
        cost_estimate=cost(1e3, 1e3),
        name="project",
        compiler_params=room(10),
    )(features, pack, mod, attention_weight)

    near = swap(quarter, 1)

    attended, stream, second_in, padded, rim_queries, rim_counts, log_totals = pl.pallas_call(
        forward_kernel,
        out_shape=(
            struct((row_count, D), bf16),
            struct((row_count, D), f32),
            struct((row_count, D), bf16),
            struct((2, row_count + 2 * HALO, D), bf16),
            struct((2 * HALO, D), bf16),
            struct((2 * HALO, RIM), bf16),
            struct((row_count, 128), f32),
        ),
        in_specs=[VMEM] * 8,
        out_specs=(VMEM,) * 7,
        scratch_shapes=[pltpu.VMEM((2 * HALO, D), bf16)],
        cost_estimate=cost(1e3, 1e3),
        name="attend",
        compiler_params=room(12),
    )(rim_low, rim_high, features, pack, mod, attn_bf, qkv, counts)

    def whole(*shape):
        return pl.BlockSpec(shape, lambda g, s: (0,) * len(shape))

    chunk_shape = struct((2, 2, 2, 128, CHUNK), bf16)
    branch, grad_second, own_kept, own_sent = pl.pallas_call(
        mlp_own_kernel,
        out_shape=(struct((row_count, D), f32), struct((row_count, D), f32), chunk_shape, chunk_shape),
        grid_spec=pltpu.PrefetchScalarGridSpec(
            num_scalar_prefetch=1,
            grid=(2,),
            in_specs=[
                whole(row_count, D),
                whole(row_count, D),
                pl.BlockSpec((D, CHUNK), lambda g, s: (0, g)),
                pl.BlockSpec((CHUNK, D), lambda g, s: (g, 0)),
                pl.BlockSpec(memory_space=pl.ANY),
            ],
            out_specs=(
                whole(row_count, D),
                whole(row_count, D),
                pl.BlockSpec((1, 2, 2, 128, CHUNK), lambda g, s: (g ^ s[1], 0, 0, 0, 0)),
                pl.BlockSpec((1, 2, 2, 128, CHUNK), lambda g, s: (g ^ s[1], 0, 0, 0, 0)),
            ),
            scratch_shapes=[pltpu.VMEM((row_count, CHUNK), bf16)] * 2,
        ),
        cost_estimate=cost(1e10, 1e3),
        name="mlp_own",
        compiler_params=room(14),
    )(scalars, second_in, cotangent, up_weight, down_weight, small_past)

    def part(away):
        return pl.BlockSpec(
            (1, 2, 2, 128, CHUNK), lambda g, s: (away ^ s[0] ^ s[1], 0, 0, 0, 0)
        )

    branch, grad_second, near_kept, near_sent = pl.pallas_call(
        mlp_near_kernel,
        out_shape=(struct((row_count, D), f32), struct((row_count, D), f32), chunk_shape, chunk_shape),
        grid_spec=pltpu.PrefetchScalarGridSpec(
            num_scalar_prefetch=1,
            grid=(1,),
            in_specs=[
                whole(row_count, D),
                whole(row_count, D),
                whole(2, D, CHUNK),
                whole(row_count, D),
                whole(row_count, D),
            ],
            out_specs=(whole(row_count, D), whole(row_count, D), part(0), part(0)),
            scratch_shapes=[pltpu.VMEM((row_count, CHUNK), bf16)] * 2,
        ),
        cost_estimate=cost(2.5e9, 4e6),
        name="mlp_near",
        compiler_params=room(10),
    )(scalars, second_in, cotangent, near, branch, grad_second)
    far = swap(after(near, own_kept), 2)
    (
        rest_kept,
        rest_sent,
        output,
        grad_stream,
        grad_attended,
        stats,
        edge_low,
        edge_high,
        table_two,
    ) = pl.pallas_call(
        mlp_far_kernel,
        out_shape=(
            chunk_shape,
            chunk_shape,
            struct((row_count, D), bf16),
            struct((row_count, D), f32),
            struct((row_count, D), bf16),
            struct((row_count, 128), f32),
            struct((HALO, D + 128), bf16),
            struct((HALO, D + 128), bf16),
            struct((8, D), f32),
        ),
        grid_spec=pltpu.PrefetchScalarGridSpec(
            num_scalar_prefetch=1,
            grid=(1,),
            in_specs=[
                whole(row_count, D),
                whole(row_count, D),
                whole(2, D, CHUNK),
                whole(row_count, D),
                whole(row_count, D),
                whole(row_count, D),
                whole(row_count, 128),
                whole(2, 4, D),
                whole(4, D, D),
                whole(row_count, D),
                whole(row_count, 128),
                pl.BlockSpec(memory_space=pl.ANY),
                pl.BlockSpec(memory_space=pl.ANY),
            ],
            out_specs=(
                part(1),
                part(1),
                whole(row_count, D),
                whole(row_count, D),
                whole(row_count, D),
                whole(row_count, 128),
                whole(HALO, D + 128),
                whole(HALO, D + 128),
                whole(8, D),
            ),
            scratch_shapes=[
                pltpu.VMEM((row_count, D), f32),
                pltpu.VMEM((row_count, D), f32),
                pltpu.VMEM((row_count, CHUNK), bf16),
                pltpu.VMEM((row_count, CHUNK), bf16),
            ],
        ),
        input_output_aliases={12: 0, 13: 1},
        cost_estimate=cost(4e9, 8e6),
        name="mlp_far",
        compiler_params=room(16),
    )(
        scalars,
        second_in,
        cotangent,
        far,
        branch,
        grad_second,
        stream,
        pack,
        mod,
        attn_bf,
        attended,
        log_totals,
        near_kept,
        near_sent,
    )

    grad_low = along(edge_high, 1)
    grad_high = along(edge_low, -1)

    large_shape = (2, 2, 2, 128, CHUNK)
    large_keep, large_send = pl.pallas_call(
        large_sum_kernel,
        out_shape=(struct(large_shape, f32), struct(large_shape, bf16)),
        in_specs=[SMEM] + [VMEM] * 4,
        out_specs=(VMEM,) * 2,
        cost_estimate=cost(1e3, 1e3),
        name="large_sum",
        compiler_params=room(12),
    )(scalars, own_kept, swap(own_sent, 2), rest_kept, swap(rest_sent, 2))

    def ordered(kernel, values, tokens, shapes, name, work=1e10):
        return pl.pallas_call(
            kernel,
            out_shape=shapes,
            in_specs=[VMEM] * len(values) + [pl.BlockSpec(memory_space=pl.ANY)] * len(tokens),
            out_specs=jax.tree.map(lambda _: VMEM, shapes),
            cost_estimate=cost(work, 1e3),
            name=name,
            compiler_params=room(8),
        )(*values, *tokens)

    def receive(keep, got, *tokens):
        rows = math.prod(keep.shape[1:-1])
        flat = (2, rows, D)
        keep, send = ordered(
            receive_kernel,
            (keep.reshape(flat), got.reshape(flat)),
            tokens,
            (struct((rows, D), f32), struct((rows, D), bf16)),
            "receive",
        )
        half = (2, rows // 2, D)
        return keep.reshape(half), send.reshape(half)

    def rounded_total(keep, got, *tokens):
        return ordered(total_kernel, (keep, got), tokens, struct(keep.shape, bf16), "total")

    def blend(total, got, past, *tokens, work=1e10):
        flip, mask = 1, 32
        while mask < device_count:
            mine = total.astype(f32) + (got[::-1] if flip else got).astype(f32)
            total, flip = mine.astype(bf16), 0
            got = swap(total, mask)
            mask *= 2
        return ordered(
            functools.partial(blend_kernel, flip),
            (total, got, past),
            tokens,
            struct(total.shape, bf16),
            "blend",
            work,
        ).reshape(-1, D)

    def join(part, got, *tokens, work=1e10):
        rows = math.prod(part.shape[:-1])
        return ordered(
            join_kernel,
            (part.reshape(rows, D), got.reshape(rows, D)),
            tokens,
            struct((2, rows, D), bf16),
            "join",
            work,
        ).reshape(2 * rows, D)

    large_routes = ((4, 8), (1, 4), (8, 1), (16, 16))
    small_routes = ((4, 8), (1, 1), (8, 4), (16, 16))

    padded_rows = row_count + 2 * HALO
    large_got = swap(large_send, *large_routes[0])
    grad_queries, keys_total, values_total = pl.pallas_call(
        backward_kernel,
        out_shape=(struct((row_count, D), bf16),) + (struct((padded_rows, D), f32),) * 2,
        in_specs=[VMEM] * 5 + [pl.BlockSpec(memory_space=pl.ANY)],
        out_specs=(VMEM,) * 3,
        cost_estimate=cost(8e9, 9e6),
        name="attend_back",
        compiler_params=room(10),
    )(qkv, padded, grad_attended, stats, counts, large_send)
    large_keep, large_send = receive(large_keep, large_got, grad_queries)
    large_got = swap(large_send, *large_routes[1])
    piece_shape = struct((2, 2, 2, 2, 80, D), bf16)
    features_grad, small_kept, small_sent = pl.pallas_call(
        weights_kernel,
        out_shape=(struct((row_count, D), f32), piece_shape, piece_shape),
        in_specs=[SMEM, pl.BlockSpec(memory_space=pl.ANY)] + [VMEM] * 16,
        out_specs=(VMEM,) * 3,
        scratch_shapes=[
            pltpu.VMEM((4, row_count, D), bf16),
            pltpu.VMEM((8, D), f32),
            pltpu.VMEM((row_count, D), f32),
            pltpu.VMEM((row_count, D), f32),
            pltpu.VMEM((2, 2, 2, 2, 2, 80, D), bf16),
        ],
        cost_estimate=cost(6e9, 9e6),
        name="attend_weights",
        compiler_params=room(16),
    )(
        scalars,
        large_send,
        grad_queries,
        keys_total,
        values_total,
        padded,
        rim_queries,
        rim_counts,
        grad_low,
        grad_high,
        first_in,
        attended,
        grad_stream,
        features,
        pack,
        mod,
        attn_bf,
        table_two,
    )
    def chain_large(step, *tokens):
        nonlocal large_keep, large_send, large_got
        large_keep, large_send = receive(large_keep, large_got, *tokens)
        large_got = swap(large_send, *large_routes[step])

    def chain_small(step, *tokens):
        nonlocal small_keep, small_send, small_got
        small_keep, small_send = receive(small_keep, small_got, *tokens)
        small_got = swap(small_send, *small_routes[step])

    small_keep, small_send = small_kept, small_sent
    small_got = swap(small_send, 2)
    chain_large(2, small_sent)
    chain_small(0, large_send)
    large_total = rounded_total(large_keep, large_got, small_send)
    large_got = swap(large_total, *large_routes[3])
    chain_small(1, large_total)
    large_part = blend(large_total, large_got, large_past, small_send)
    large_got = swap(large_part, *large_routes[2])
    chain_small(2, large_part)
    large_part = join(large_part, large_got, small_send)
    large_got = swap(large_part, *large_routes[1])
    small_total = rounded_total(small_keep, small_got, large_part)
    small_got = swap(small_total, *small_routes[3])
    large_part = join(large_part, large_got, small_total)
    large_got = swap(large_part, *large_routes[0])
    small_part = blend(small_total, small_got, small_past, large_part, work=8e9)
    small_got = swap(small_part, *small_routes[2])
    small_part = join(small_part, small_got, work=1e3)
    small_got = swap(small_part, *small_routes[1])

    any_space = pl.BlockSpec(memory_space=pl.ANY)
    gathered_shape = (2, 2, 2, 128, CHUNK)
    large_work, large_mix = pl.pallas_call(
        large_first_kernel,
        out_shape=(struct((4, D, CHUNK), bf16), struct((2, D, CHUNK), bf16)),
        in_specs=[SMEM, VMEM, VMEM, any_space],
        out_specs=(VMEM,) * 2,
        scratch_shapes=[pltpu.VMEM((D, D), bf16)],
        cost_estimate=cost(1e3, 1e3),
        name="ortho_large",
        compiler_params=room(10),
    )(scalars, large_part.reshape(gathered_shape), large_got.reshape(gathered_shape), small_part)
    mix_got = swap(large_mix, 2)
    small_part = join(small_part, small_got, large_work)
    small_got = swap(small_part, *small_routes[0])
    large_result = pl.pallas_call(
        large_next_kernel,
        out_shape=struct((2, D, CHUNK), bf16),
        in_specs=[VMEM, any_space],
        out_specs=VMEM,
        scratch_shapes=[pltpu.VMEM((4, D, CHUNK), bf16), pltpu.VMEM((D, D), bf16)],
        cost_estimate=cost(1e3, 1e3),
        name="ortho_large",
        compiler_params=room(10),
    )(large_work, small_part)
    result_got = swap(large_result, 2)

    across = pl.BlockSpec((1, D, 256), lambda g: (g // 2, 0, g % 2))
    left_right = pl.BlockSpec((D, 256), lambda g: (0, g))
    top_bottom = pl.BlockSpec((256, D), lambda g: (g, 0))
    large_shapes = (struct((D, 2 * CHUNK), f32), struct((2 * CHUNK, D), f32))
    small_token = struct((8, 128), f32)
    token_block = pl.BlockSpec((8, 128), lambda g: (0, 0))
    up_moment_new, down_moment_new, moments_done = pl.pallas_call(
        large_moment_kernel,
        grid=(4,),
        out_shape=large_shapes + (small_token,),
        in_specs=[SMEM, across, across, left_right, top_bottom, any_space],
        out_specs=(left_right, top_bottom, token_block),
        cost_estimate=cost(1e3, 1e3),
        name="moment_large",
        compiler_params=room(8),
    )(scalars, large_mix, mix_got, up_moment, down_moment, large_result)

    small_work, small_mix = pl.pallas_call(
        small_start_kernel,
        out_shape=(
            struct((2, 2, 256, D), bf16),
            struct((2, 256 + TABLE_ROWS, D), bf16),
        ),
        in_specs=[SMEM, VMEM, VMEM, any_space],
        out_specs=(VMEM,) * 2,
        scratch_shapes=[pltpu.VMEM((TABLE_ROWS, D), f32)],
        cost_estimate=cost(3e10, 1e3),
        name="unpack_small",
        compiler_params=room(6),
    )(
        scalars,
        small_part.reshape(2, 2, 2, 80, D),
        small_got.reshape(2, 2, 2, 80, D),
        moments_done,
    )
    mix_other = swap(small_mix, 2)

    def fixed(*shape):
        return pl.BlockSpec(shape, lambda g: (0,) * len(shape))

    def one(index):
        return pl.BlockSpec((1, 256, D), index)

    small_result, up_new, down_new = pl.pallas_call(
        small_kernel,
        grid=(NS_STEPS,),
        out_shape=(struct((2, 256, D), bf16),) + large_shapes,
        in_specs=[SMEM, fixed(2, 2, 256, D), across, across, left_right, top_bottom, any_space],
        out_specs=(fixed(2, 256, D), left_right, top_bottom),
        scratch_shapes=[pltpu.VMEM((2, 256, D), bf16)] * 2
        + [pltpu.VMEM((D, D), bf16)] * 2
        + [pltpu.SMEM((2,), f32)],
        cost_estimate=cost(6e9, 1e7),
        name="ortho_small",
        compiler_params=room(16),
    )(scalars, small_work, large_result, result_got, up_weight, down_weight, moments_done)
    small_other = swap(small_result, 2)
    table_block = pl.BlockSpec((1, TABLE_ROWS, D), lambda g: (0, 256 // TABLE_ROWS, 0))
    attention_moment_new, modulation_moment_new, modulation_new, moment_done = pl.pallas_call(
        functools.partial(small_moment_kernel, nodes=row_count * device_count),
        grid=(4,),
        out_shape=(struct((4, 256, D), f32),) + (struct((2, 2, D), f32),) * 2 + (small_token,),
        in_specs=[
            SMEM,
            one(lambda g: (g % 2, 0, 0)),
            one(lambda g: (g % 2, 0, 0)),
            one(lambda g: (g, 0, 0)),
            table_block,
            table_block,
            fixed(2, 4, D),
            fixed(2, 2, D),
            any_space,
        ],
        out_specs=(one(lambda g: (g, 0, 0)), fixed(2, 2, D), fixed(2, 2, D), token_block),
        cost_estimate=cost(1e10, 1e7),
        name="moment_small",
        compiler_params=room(8),
    )(
        scalars,
        small_mix,
        mix_other,
        attention_moment,
        small_mix,
        mix_other,
        modulation,
        modulation_moment,
        small_result,
    )
    attention_new = pl.pallas_call(
        small_weight_kernel,
        grid_spec=pltpu.PrefetchScalarGridSpec(
            num_scalar_prefetch=1,
            grid=(4,),
            in_specs=[
                pl.BlockSpec((1, 256, D), lambda g, s: (g % 2, 0, 0)),
                pl.BlockSpec((1, 256, D), lambda g, s: (g % 2, 0, 0)),
                pl.BlockSpec((1, 256, D), lambda g, s: (g, s[4], 0)),
                any_space,
            ],
            out_specs=pl.BlockSpec((1, 256, D), lambda g, s: (g, 0, 0)),
        ),
        out_shape=struct((4, 256, D), f32),
        cost_estimate=cost(1e7, 6e6),
        name="update_small",
        compiler_params=room(6),
    )(scalars, small_result, small_other, attention_weight, moment_done)
    return (
        output,
        features_grad,
        attention_moment_new,
        attention_new,
        up_moment_new,
        up_new,
        down_moment_new,
        down_new,
        modulation_moment_new,
        modulation_new,
    )


def solution(mesh):
    placed = (
        P(("nodes", "hid"), None),
        P(("nodes", "hid")),
        P(("nodes", "hid"), None),
        P(("nodes", "hid")),
        P(("nodes", "hid"), None),
        P(),
        P(None, "hid"),
        P("hid", None),
        P(),
        P(None, "hid", None),
        P(None, "hid"),
        P("hid", None),
        P(None, "hid", None),
    )
    return jax.shard_map(
        on_device,
        mesh=mesh,
        in_specs=placed,
        out_specs=(
            P(("nodes", "hid"), None),
            P(("nodes", "hid"), None),
            P(None, "hid", None),
            P(None, "hid", None),
            P(None, "hid"),
            P(None, "hid"),
            P("hid", None),
            P("hid", None),
            P(None, "hid", None),
            P(None, "hid", None),
        ),
        check_vma=False,
    )
```

```python
import functools
import math

import jax
import jax.numpy as jnp
from jax import lax
from jax.experimental import pallas as pl
from jax.experimental.pallas import tpu as pltpu
from jax.sharding import PartitionSpec as P

D = 512
HEADS = 4
HD = 128
FF = 2048
K = 16
NS_STEPS = 4
HALO = 192
BLOCK = 128
SPAN = BLOCK + 2 * HALO
RIM = 256
CHUNK = 512
TABLE_ROWS = 16

f32 = jnp.float32
bf16 = jnp.bfloat16
ns_first = 3.4445
ns_second = -4.775
ns_third = 2.0315
momentum_rate = 0.95
vector_rate = 0.9
muon_rate = 0.2
decay_rate = 0.1
score_scale = 1.0 / math.sqrt(HD)
AXES = ("nodes", "hid")
VMEM = pl.BlockSpec(memory_space=pltpu.VMEM)
SMEM = pl.BlockSpec(memory_space=pltpu.SMEM)


def nn(a, b):
    return lax.dot_general(a, b, (((1,), (0,)), ((), ())), preferred_element_type=f32)


def nt(a, b):
    return lax.dot_general(a, b, (((1,), (1,)), ((), ())), preferred_element_type=f32)


def tn(a, b):
    return lax.dot_general(a, b, (((0,), (0,)), ((), ())), preferred_element_type=f32)


def struct(shape, dtype):
    return jax.ShapeDtypeStruct(shape, dtype)


def rows_of(start, size):
    return pl.ds(pl.multiple_of(start, size), size)


def cost(flops, data):
    return pl.CostEstimate(flops=int(flops), bytes_accessed=int(data), transcendentals=0)


def room(mebibytes):
    return pltpu.CompilerParams(vmem_limit_bytes=mebibytes << 20)


def norm_parts(field):
    average = jnp.mean(field, axis=-1, keepdims=True)
    centred = field - average
    variance = jnp.mean(centred * centred, axis=-1, keepdims=True)
    inverse = lax.rsqrt(variance + 1e-06)
    return centred * inverse, inverse


def table_rows(mod_ref, level, column):
    return jnp.where(level > 0.5, mod_ref[1, column : column + 1, :], mod_ref[0, column : column + 1, :])


def modulated(field, level, mod_ref, column):
    normed, _ = norm_parts(field)
    return normed * (1.0 + table_rows(mod_ref, level, column)) + table_rows(
        mod_ref, level, column + 1
    )


def norm_back(grad_out, field, level, mod_ref, column):
    normed, inverse = norm_parts(field)
    grad_norm = grad_out * (1.0 + table_rows(mod_ref, level, column))
    grad_in = inverse * (
        grad_norm
        - jnp.mean(grad_norm, axis=-1, keepdims=True)
        - normed * jnp.mean(grad_norm * normed, axis=-1, keepdims=True)
    )
    return grad_in, grad_out * normed


def add_table(table_ref, column, level, scale_term, shift_term):
    upper = level > 0.5
    for term, place in ((scale_term, column), (shift_term, column + 1)):
        low_part = jnp.sum(jnp.where(upper, 0.0, term), axis=0, keepdims=True)
        high_part = jnp.sum(jnp.where(upper, term, 0.0), axis=0, keepdims=True)
        table_ref[place : place + 1, :] += low_part
        table_ref[4 + place : 5 + place, :] += high_part


def slot_counts(pack, row_count, width, shift):
    pieces = []
    for left in range(0, width, 128):
        lanes = lax.broadcasted_iota(jnp.int32, (row_count, 128), 1)
        rows = lax.broadcasted_iota(jnp.int32, (row_count, 128), 0)
        place = (lanes - rows + (left - shift)).astype(f32)
        total = jnp.zeros((row_count, 128), f32)
        for slot in range(K):
            total = total + jnp.where(place == pack[:, slot : slot + 1], 1.0, 0.0)
        pieces.append(total)
    return jnp.concatenate(pieces, axis=1).astype(bf16)


def quarter_kernel(scalars, up, down, token, rounded):
    rounded[0] = up[...].astype(bf16)
    rounded[1] = down[...].astype(bf16)


def past_kernel(scalars, up, down, attention, large_past, small_past):
    z2 = scalars[3]
    large = jnp.where(scalars[0] == 0, up[...], down[...].T)
    for j in range(2):
        large_past[j ^ z2] = large[j * 128 : (j + 1) * 128]
        small_past[j ^ z2] = attention[0, j * 64 : (j + 1) * 64, :]


def project_kernel(features, pack, mod, weights, first_in, qkv, counts, rounded):
    row_count = features.shape[0]
    turn = pl.program_id(0)

    @pl.when(turn == 0)
    def _():
        for start in range(0, row_count, 256):
            rows = slice(start, start + 256)
            level = pack[rows, K : K + 1]
            first_in[rows, :] = modulated(features[rows, :].astype(f32), level, mod, 0).astype(bf16)

    weight = weights[0].astype(bf16)
    rounded[0] = weight

    @pl.when(turn < 3)
    def _():
        qkv[turn] = nn(first_in[...], weight).astype(bf16)
        share = row_count // BLOCK // 3

        def count_step(b, carry):
            rows = rows_of(b * BLOCK, BLOCK)
            counts[rows, :] = slot_counts(pack[rows, :], BLOCK, SPAN, HALO)
            return carry

        lax.fori_loop(turn * share, (turn + 1) * share, count_step, 0)


def forward_kernel(
    rim_low,
    rim_high,
    info_low,
    info_high,
    features,
    pack,
    mod,
    weights,
    qkv,
    counts,
    attended,
    stream,
    second_in,
    padded,
    rim_queries,
    rim_counts,
    log_totals,
    rim_in,
):
    row_count = features.shape[0]
    for side, (rim, rim_info) in enumerate(((rim_low, info_low), (rim_high, info_high))):

        def rim_step(b, carry):
            rows = rows_of(b * 64, 64)
            target = pl.ds(pl.multiple_of(side * HALO + b * 64, 64), 64)
            info = rim_info[rows, :].astype(f32)
            rim_in[target, :] = modulated(
                rim[rows, :].astype(f32), info[:, K : K + 1], mod, 0
            ).astype(bf16)
            rim_counts[target, :] = slot_counts(
                info, 64, RIM, b * 64 + (-HALO if side == 0 else RIM)
            )
            return carry

        lax.fori_loop(0, HALO // 64, rim_step, 0)
    rim_queries[...] = nn(rim_in[...], weights[0]).astype(bf16)
    for p in range(2):
        piece = nn(rim_in[...], weights[1 + p]).astype(bf16)
        padded[p, :HALO, :] = piece[:HALO]
        padded[p, HALO + row_count :, :] = piece[HALO:]
        padded[p, HALO : HALO + row_count, :] = qkv[1 + p]

    def step(b, carry):
        rows = rows_of(b * BLOCK, BLOCK)
        span = pl.ds(pl.multiple_of(b * BLOCK, BLOCK), SPAN)
        count = counts[rows, :].astype(f32)
        live = count > 0.0
        columns = [slice(h * HD, (h + 1) * HD) for h in range(HEADS)]
        scores = [nt(qkv[0, rows, cols], padded[0, span, cols]) * score_scale for cols in columns]
        lanes = lax.broadcasted_iota(jnp.int32, (BLOCK, 128), 1)
        stats = jnp.zeros((BLOCK, 128), f32)
        for h, cols in enumerate(columns):
            masked = jnp.where(live, scores[h], -1e30)
            peak = jnp.max(masked, axis=-1, keepdims=True)
            exponent = jnp.exp(masked - peak)
            total = jnp.sum(exponent * count, axis=-1, keepdims=True)
            probs = (exponent * (1.0 / total)).astype(bf16)
            spread = probs * counts[rows, :]
            attended[rows, cols] = nn(spread, padded[1, span, cols]).astype(bf16)
            stats = jnp.where(lanes == h, peak + jnp.log(total), stats)
        log_totals[rows, :] = stats
        return carry

    lax.fori_loop(0, row_count // BLOCK, step, 0)
    for start in range(0, row_count, 256):
        rows = slice(start, start + 256)
        field = features[rows, :].astype(f32) + nn(attended[rows, :], weights[3])
        stream[rows, :] = field
        second_in[rows, :] = modulated(field, pack[rows, K : K + 1], mod, 2).astype(bf16)


def mlp_chunk(
    scalars, second_in, cotangent, up, down, branch_in, grad_in, branch, grad_second, acts, grads, kept, sent
):
    row_count = second_in.shape[0]
    for start in range(0, row_count, 256):
        rows = slice(start, start + 256)
        preact = nn(second_in[rows, :], up)
        grad_act = nt(cotangent[rows, :], down)
        sigmoid = 0.5 * jnp.tanh(0.5 * preact) + 0.5
        act = (preact * sigmoid).astype(bf16)
        acts[rows, :] = act
        grad_pre = (grad_act * (sigmoid * (1.0 + preact * (1.0 - sigmoid)))).astype(bf16)
        grads[rows, :] = grad_pre
        branch[rows, :] = branch_in[rows, :] + nn(act, down)
        grad_second[rows, :] = grad_in[rows, :] + nt(grad_pre, up)
    first, z1, z2 = scalars[0] == 0, scalars[2], scalars[3]
    for out, swapped in ((kept, False), (sent, True)):
        ups = jnp.logical_not(first) if swapped else first
        product = tn(
            jnp.where(ups, second_in[...], cotangent[...]), jnp.where(ups, grads[...], acts[...])
        )
        for q in range(4):
            out[0, (q // 2) ^ z1, (q % 2) ^ z2] = product[q * 128 : (q + 1) * 128].astype(bf16)


def mlp_own_kernel(
    scalars, second_in, cotangent, up, down, token, branch, grad_second, kept, sent, acts, grads
):
    @pl.when(pl.program_id(0) == 0)
    def _():
        branch[...] = jnp.zeros_like(branch)
        grad_second[...] = jnp.zeros_like(grad_second)

    mlp_chunk(
        scalars,
        second_in,
        cotangent,
        up[...].astype(bf16),
        down[...].astype(bf16),
        branch,
        grad_second,
        branch,
        grad_second,
        acts,
        grads,
        kept,
        sent,
    )


def mlp_near_kernel(
    scalars, second_in, cotangent, near, branch_in, grad_in, branch, grad_second, kept, sent, acts, grads
):
    mlp_chunk(
        scalars,
        second_in,
        cotangent,
        near[0],
        near[1],
        branch_in,
        grad_in,
        branch,
        grad_second,
        acts,
        grads,
        kept,
        sent,
    )


def mlp_far_kernel(
    scalars,
    second_in,
    cotangent,
    far,
    branch_in,
    grad_in,
    stream,
    pack,
    mod,
    weights,
    attended,
    log_totals,
    kept_in,
    sent_in,
    kept,
    sent,
    output,
    grad_stream,
    grad_attended,
    stats,
    edge_low,
    edge_high,
    table,
    branch,
    grad_second,
    acts,
    grads,
):
    row_count = second_in.shape[0]
    mlp_chunk(
        scalars,
        second_in,
        cotangent,
        far[0],
        far[1],
        branch_in,
        grad_in,
        branch,
        grad_second,
        acts,
        grads,
        kept,
        sent,
    )
    table[...] = jnp.zeros_like(table)

    for start in range(0, row_count, 256):
        rows = slice(start, start + 256)
        field = stream[rows, :]
        level = pack[rows, K : K + 1]
        output[rows, :] = (field + branch[rows, :]).astype(bf16)
        gradient = grad_second[rows, :]
        grad_field, scale_term = norm_back(gradient, field, level, mod, 2)
        add_table(table, 2, level, scale_term, gradient)
        total = cotangent[rows, :].astype(f32) + grad_field
        grad_stream[rows, :] = total
        back = nt(total.astype(bf16), weights[3]).astype(bf16)
        grad_attended[rows, :] = back
        product = back.astype(f32) * attended[rows, :].astype(f32)
        lanes = lax.broadcasted_iota(jnp.int32, (256, 128), 1)
        kept_stats = log_totals[rows, :]
        for h in range(HEADS):
            delta = jnp.sum(product[:, h * HD : (h + 1) * HD], axis=-1, keepdims=True)
            kept_stats = jnp.where(lanes == HEADS + h, delta, kept_stats)
        stats[rows, :] = kept_stats
    for edge, first in ((edge_low, 0), (edge_high, row_count - HALO)):
        rows = slice(first, first + HALO)
        edge[:, :D] = grad_attended[rows, :]
        known = stats[rows, :]
        upper = known.astype(bf16)
        lower = (known - upper.astype(f32)).astype(bf16).astype(f32)
        edge[:, D:] = (upper.astype(f32) + pltpu.roll(lower, 2 * HEADS, 1)).astype(bf16)


def attention_terms(scores, grad_probs, live, count, log_total, delta):
    probs = jnp.exp(jnp.where(live, scores * score_scale, -1e30) - log_total)
    slopes = (probs * (grad_probs - delta)).astype(bf16)
    return slopes * count, probs.astype(bf16) * count


def backward_kernel(qkv, padded, grad, stats, counts, token, grad_query, keys_total, values_total):
    keys_total[...] = jnp.zeros_like(keys_total)
    values_total[...] = jnp.zeros_like(values_total)

    def step(b, carry):
        rows = rows_of(b * BLOCK, BLOCK)
        span = pl.ds(pl.multiple_of(b * BLOCK, BLOCK), SPAN)
        count = counts[rows, :]
        live = count.astype(f32) > 0.0
        columns = [slice(h * HD, (h + 1) * HD) for h in range(HEADS)]
        products = [
            (nt(qkv[0, rows, cols], padded[0, span, cols]), nt(grad[rows, cols], padded[1, span, cols]))
            for cols in columns
        ]
        terms = [
            attention_terms(
                *products[h],
                live,
                count,
                stats[rows, h : h + 1],
                stats[rows, HEADS + h : HEADS + h + 1],
            )
            for h in range(HEADS)
        ]
        for (slopes, spread), cols in zip(terms, columns):
            grad_query[rows, cols] = (nn(slopes, padded[0, span, cols]) * score_scale).astype(bf16)
            keys_total[span, cols] += tn(slopes, qkv[0, rows, cols])
            values_total[span, cols] += tn(spread, grad[rows, cols])
        return carry

    lax.fori_loop(0, counts.shape[0] // BLOCK, step, 0)


def weights_kernel(
    scalars,
    token,
    queries_in,
    keys_in,
    values_in,
    padded,
    rim_query,
    rim_counts,
    grad_low,
    grad_high,
    first_in,
    attended,
    grad_stream,
    features,
    pack,
    mod,
    weights,
    table_two,
    features_grad,
    kept,
    sent,
    gathered,
    table,
    keys_total,
    values_total,
    blocks,
):
    row_count = first_in.shape[0]
    columns = [slice(h * HD, (h + 1) * HD) for h in range(HEADS)]
    own = slice(HALO, HALO + row_count)
    keys_total[...] = keys_in[own, :]
    values_total[...] = values_in[own, :]
    for side, grads in enumerate((grad_low, grad_high)):
        first = 0 if side == 0 else row_count - RIM
        own_span = slice(first, first + RIM)
        span = slice(HALO + first, HALO + first + RIM)
        rows = slice(side * HALO, (side + 1) * HALO)
        known = grads[:, D:].astype(f32)
        count = rim_counts[rows, :]
        live = count.astype(f32) > 0.0
        products = [
            (nt(rim_query[rows, cols], padded[0, span, cols]), nt(grads[:, cols], padded[1, span, cols]))
            for cols in columns
        ]
        terms = []
        for h in range(HEADS):
            numbers = [known[:, i * HEADS + h : i * HEADS + h + 1] for i in range(4)]
            terms.append(
                attention_terms(*products[h], live, count, numbers[0] + numbers[2], numbers[1] + numbers[3])
            )
        for (slopes, spread), cols in zip(terms, columns):
            keys_total[own_span, cols] += tn(slopes, rim_query[rows, cols])
            values_total[own_span, cols] += tn(spread, grads[:, cols])
    gathered[0] = queries_in[...]
    gathered[1] = (keys_total[...] * score_scale).astype(bf16)
    gathered[2] = values_total[...].astype(bf16)
    table[...] = table_two[...]
    for start in range(0, row_count, 256):
        rows = slice(start, start + 256)
        level = pack[rows, K : K + 1]
        gradient = nt(gathered[0, rows, :], weights[0])
        for p in range(1, 3):
            gradient = gradient + nt(gathered[p, rows, :], weights[p])
        grad_field, scale_term = norm_back(gradient, features[rows, :].astype(f32), level, mod, 0)
        add_table(table, 0, level, scale_term, gradient)
        total = grad_stream[rows, :]
        features_grad[rows, :] = total + grad_field
        gathered[3, rows, :] = total.astype(bf16)
    core, slot_bit, z1, z2, hid = (scalars[i] for i in range(5))

    def product_step(n, carry):
        away, slot = n // 2, n % 2
        target = core ^ away
        p = 2 * target + slot
        product = tn(jnp.where(p < 3, first_in[...], attended[...]), gathered[p])
        for half in range(2):
            for q in range(4):
                slot_at, hid_at, row_half = slot ^ slot_bit, half ^ hid, (q // 2) ^ z1
                index = (
                    away,
                    jnp.where(target == 0, slot_at, row_half),
                    hid_at,
                    jnp.where(target == 0, row_half, slot_at),
                    (q % 2) ^ z2,
                )
                start = half * 256 + q * 64
                blocks[index + (slice(0, 64),)] = product[start : start + 64].astype(bf16)
                row = (q // 2) * 4 + 2 * half + q % 2
                known = jnp.broadcast_to(table[row : row + 1, :], (TABLE_ROWS, D))
                blocks[index + (slice(64, 80),)] = jnp.where(p == 0, known, 0.0).astype(bf16)
        return carry

    lax.fori_loop(0, 4, product_step, 0)
    kept[...] = blocks[0]
    sent[...] = blocks[1]


def large_sum_kernel(scalars, own, own_got, rest, rest_got, keep, send):
    first = scalars[0] == 0
    for away, out in ((0, keep), (1, send)):
        for source, got, h in ((own, own_got, 0), (rest, rest_got, 1)):
            for i in range(2):
                where_from = (jnp.where(first, away, i), jnp.where(first, i, away))
                where_to = (jnp.where(first, h, i), jnp.where(first, i, h))
                total = source[where_from].astype(f32) + got[where_from].astype(f32)
                out[where_to] = total.astype(out.dtype)


def receive_kernel(*refs):
    kept, got, keep, send = refs[0], refs[1], refs[-2], refs[-1]
    keep[...] = kept[0].astype(f32) + got[0].astype(f32)
    send[...] = (kept[1].astype(f32) + got[1].astype(f32)).astype(bf16)


def total_kernel(*refs):
    kept, got, total = refs[0], refs[1], refs[-1]
    total[...] = (kept[...] + got[...].astype(f32)).astype(bf16)


def blend_kernel(flip, *refs):
    kept, got, past, part = refs[0], refs[1], refs[2], refs[-1]
    rows = past.shape[1]
    for j in range(2):
        total = kept[j].astype(f32) + got[j ^ flip].astype(f32)
        blended = (1.0 + momentum_rate) * total[:rows] + momentum_rate * momentum_rate * past[j]
        part[j, :rows, :] = blended.astype(bf16)
        if rows < part.shape[1]:
            part[j, rows:, :] = total[rows:].astype(bf16)


def join_kernel(*refs):
    part, got, pieces = refs[0], refs[1], refs[-1]
    pieces[0] = part[...]
    pieces[1] = got[...]


def newton_schulz(groups, polys, rows_first, scales):
    blocks = [[[ref[i] for i in half] for half in halves] for ref, halves in groups]
    grams = []
    for halves, scale in zip(blocks, scales):
        sums = []
        for half in halves:
            total = None
            for block in half:
                term = tn(block, block) if rows_first else nt(block, block)
                total = term if total is None else total + term
            sums.append((total if scale is None else total * (scale * scale)).astype(bf16))
        grams.append((sums[0].astype(f32) + sums[1].astype(f32)).astype(bf16))
    for gram, poly in zip(grams, polys):
        poly[...] = (ns_second * gram.astype(f32) + ns_third * nn(gram, gram)).astype(bf16)
    for (ref, halves), values, poly, scale in zip(groups, blocks, polys, scales):
        for half, half_values in zip(halves, values):
            for i, block in zip(half, half_values):
                other = nn(block, poly[...]) if rows_first else nn(poly[...], block)
                total = ns_first * block.astype(f32) + other
                ref[i] = (total if scale is None else total * scale).astype(bf16)


def large_start_kernel(scalars, kept, got, work, poly):
    core, slot_bit, z1, z2 = (scalars[i] for i in range(4))
    total = jnp.zeros((8, D), f32)
    for n in range(16):
        b1, b2, b3, b4 = n // 8, (n // 4) % 2, (n // 2) % 2, n % 2
        source = kept if b1 == 0 else got
        block = source[b2, b3, b4]
        value = block.astype(f32)
        total = total + jnp.sum((value * value).reshape(16, 8, D), axis=0)
        slot = jnp.where(core == 0, b1, b2)
        half = jnp.where(core == 0, b2, b3)
        row_half = jnp.where(core == 0, b3, b1)
        start = ((row_half ^ z1) * 2 + (b4 ^ z2)) * 128
        work[half * 2 + (slot ^ slot_bit), rows_of(start, 128), :] = block
    return 1.0 / (jnp.sqrt(jnp.sum(total)) + 1e-07)


large_halves = ((0, 1), (2, 3))


def large_first_kernel(scalars, kept, got, token, work, blend, poly):
    scale = large_start_kernel(scalars, kept, got, work, poly)
    for s in range(2):
        blend[s] = work[s]

    def step(i, factor):
        newton_schulz([(work, large_halves)], [poly], False, [factor])
        return jnp.ones((), f32)

    lax.fori_loop(0, NS_STEPS // 2, step, scale)


def large_next_kernel(given, token, result, work, poly):
    work[...] = given[...]

    def step(i, carry):
        newton_schulz([(work, large_halves)], [poly], False, [None])
        return carry

    lax.fori_loop(NS_STEPS // 2, NS_STEPS, step, 0)
    for s in range(2):
        result[s] = work[s]


def small_start_kernel(scalars, kept, got, token, work, blend, table):
    table[...] = jnp.zeros_like(table)
    core, slot_bit, z1, z2 = (scalars[i] for i in range(4))
    for n in range(16):
        b1, b2, b3, b4 = n // 8, (n // 4) % 2, (n // 2) % 2, n % 2
        source = kept if b1 == 0 else got
        block = source[b2, b3, b4]
        slot = jnp.where(core == 0, b1, b3) ^ slot_bit
        half = b2
        row_half = jnp.where(core == 0, b3, b1)
        quarter = (row_half ^ z1) * 2 + (b4 ^ z2)
        work[slot, half, rows_of(quarter * 64, 64), :] = block[:64]

        @pl.when((slot == 0) & (half == 0))
        def _():
            table[pl.ds(quarter, 1), :] = block[64:].astype(f32)[:1]

    for s in range(2):
        blend[s, :256, :] = work[s, 0]
        blend[s, 256:, :] = table[...].astype(bf16)


def small_kernel(
    scalars,
    given,
    own,
    got,
    up_weight,
    down_weight,
    token,
    result,
    up_new,
    down_new,
    first,
    second,
    poly_first,
    poly_second,
    factors,
):
    turn = pl.program_id(0)
    works = (first, second)

    @pl.when(turn == 0)
    def _():
        for s, work in enumerate(works):
            total = jnp.zeros((8, D), f32)
            for half in range(2):
                block = given[s, half]
                work[half] = block
                value = block.astype(f32)
                total = total + jnp.sum((value * value).reshape(32, 8, D), axis=0)
            factors[s] = 1.0 / (jnp.sqrt(jnp.sum(total)) + 1e-07)

    groups = [(work, ((0,), (1,))) for work in works]
    scales = [jnp.where(turn == 0, factors[s], 1.0) for s in range(2)]
    newton_schulz(groups, [poly_first, poly_second], True, scales)
    is_up = scalars[0] == 0
    ups = jnp.where(is_up, own[0], got[0])
    downs = jnp.where(is_up, got[0], own[0])
    up_new[...] = new_weight(up_weight[...], ups.astype(f32), FF)
    down_new[...] = new_weight(down_weight[...], downs.T.astype(f32), FF)

    @pl.when(turn == NS_STEPS - 1)
    def _():
        for s, work in enumerate(works):
            result[s] = work[0]


def new_moment(blend, moment):
    share = 1.0 / (1.0 + momentum_rate)
    return share * blend + (momentum_rate - share * momentum_rate * momentum_rate) * moment


def new_weight(weight, ortho, longest):
    return weight - muon_rate * (0.2 * math.sqrt(longest) * ortho + decay_rate * weight)


def large_moment_kernel(scalars, own, got, up_moment, down_moment, token, up_moment_new, down_moment_new, done):
    done[...] = jnp.zeros_like(done)
    first = scalars[0] == 0
    ups, downs = jnp.where(first, own[0], got[0]), jnp.where(first, got[0], own[0])
    up_moment_new[...] = new_moment(ups.astype(f32), up_moment[...])
    down_moment_new[...] = new_moment(downs.T.astype(f32), down_moment[...])


def small_moment_kernel(
    scalars,
    mix,
    mix_got,
    moment,
    table,
    table_got,
    modulation,
    held_moment,
    token,
    moment_new,
    held_moment_new,
    held_new,
    done,
    *,
    nodes,
):
    done[...] = jnp.zeros_like(done)
    core, turn = scalars[0], pl.program_id(0)
    blend = jnp.where(core == turn // 2, mix[0], mix_got[0]).astype(f32)
    moment_new[0] = new_moment(blend, moment[0])

    @pl.when(turn == 0)
    def _():
        total = jnp.where(core == 0, table[0], table_got[0]).astype(f32)
        for level in range(2):
            for column in range(2):
                row = level * 2 + column
                at = (slice(level, level + 1), slice(column, column + 1))
                value = vector_rate * held_moment[at] + total[row : row + 1, :].reshape(1, 1, D)
                held = modulation[level : level + 1, pl.ds(scalars[4] * 2 + column, 1)]
                held_moment_new[at] = value
                held_new[at] = held - 0.2 / math.sqrt(nodes) * value


def small_weight_kernel(scalars, own, got, weight, token, weight_new):
    mine = scalars[0] == pl.program_id(0) // 2
    ortho = jnp.where(mine, own[0].astype(f32), got[0].astype(f32))
    weight_new[0] = new_weight(weight[0], ortho, D)


def on_device(
    features,
    levels,
    neighbour_index,
    neighbour_count,
    cotangent,
    attention_weight,
    up_weight,
    down_weight,
    modulation,
    attention_moment,
    up_moment,
    down_moment,
    modulation_moment,
):
    row_count = features.shape[0]
    device_count = lax.axis_size(AXES)
    me = lax.axis_index(AXES)
    first_row = me * row_count

    def bit(place):
        return (me >> place) & 1

    hid, core, slot_bit, z1, z2 = (bit(place) for place in range(5))
    scalars = jnp.stack([core, slot_bit, z1, z2, hid]).astype(jnp.int32)
    is_first = core == 0

    def along(value, distance):
        pairs = [(i, i + distance) for i in range(device_count) if 0 <= i + distance < device_count]
        return lax.ppermute(value, AXES, pairs)

    def after(value, *others):
        return lax.optimization_barrier((value,) + others)[0]

    def swap(value, mask, other=None):
        masks = (mask, mask if other is None else other)
        pairs = [(i, i ^ masks[(i // 2) % 2]) for i in range(device_count)]
        return lax.ppermute(value, AXES, pairs)

    live = jnp.arange(K, dtype=jnp.int32)[None, :] < neighbour_count[:, None]
    row_ids = first_row + jnp.arange(row_count, dtype=jnp.int32)[:, None]
    offsets = jnp.where(live, neighbour_index - row_ids, 512)
    pack = jnp.concatenate(
        [offsets, levels[:, None], jnp.zeros((row_count, 128 - K - 1), jnp.int32)], axis=1
    ).astype(f32)
    rim_low = along(features[row_count - HALO :], 1)
    rim_high = along(features[:HALO], -1)
    low_edge = pack[row_count - HALO :].astype(bf16)
    info_low = along(low_edge, 1)
    info_high = along(pack[:HALO].astype(bf16), -1)

    pack, scalars, is_first = lax.optimization_barrier((pack, scalars, is_first))
    mod = modulation

    quarter = pl.pallas_call(
        quarter_kernel,
        grid_spec=pltpu.PrefetchScalarGridSpec(
            num_scalar_prefetch=1,
            grid=(1,),
            in_specs=[
                pl.BlockSpec((D, CHUNK), lambda g, s: (0, s[0])),
                pl.BlockSpec((CHUNK, D), lambda g, s: (s[0], 0)),
                pl.BlockSpec(memory_space=pl.ANY),
            ],
            out_specs=pl.BlockSpec((2, D, CHUNK), lambda g, s: (0, 0, 0)),
        ),
        out_shape=struct((2, D, CHUNK), bf16),
        cost_estimate=cost(1e6, 3e6),
        name="quarter",
        compiler_params=room(8),
    )(scalars, up_weight, down_weight, low_edge)
    large_past, small_past = pl.pallas_call(
        past_kernel,
        grid_spec=pltpu.PrefetchScalarGridSpec(
            num_scalar_prefetch=1,
            grid=(1,),
            in_specs=[
                pl.BlockSpec((256, CHUNK), lambda g, s: (s[2], s[1])),
                pl.BlockSpec((CHUNK, 256), lambda g, s: (s[1], s[2])),
                pl.BlockSpec((1, 128, D), lambda g, s: (s[0] * 2 + s[1], s[2], 0)),
            ],
            out_specs=(
                pl.BlockSpec((2, 128, CHUNK), lambda g, s: (0, 0, 0)),
                pl.BlockSpec((2, 64, D), lambda g, s: (0, 0, 0)),
            ),
        ),
        out_shape=(struct((2, 128, CHUNK), f32), struct((2, 64, D), f32)),
        cost_estimate=cost(1e6, 1e6),
        name="past",
        compiler_params=room(4),
    )(scalars, up_moment, down_moment, attention_moment)
    first_in, qkv, counts, attn_bf = pl.pallas_call(
        project_kernel,
        grid=(4,),
        out_shape=(
            struct((row_count, D), bf16),
            struct((3, row_count, D), bf16),
            struct((row_count, SPAN), bf16),
            struct((4, D, D), bf16),
        ),
        in_specs=[
            pl.BlockSpec((row_count, D), lambda g: (0, 0)),
            pl.BlockSpec((row_count, 128), lambda g: (0, 0)),
            pl.BlockSpec((2, 4, D), lambda g: (0, 0, 0)),
            pl.BlockSpec((1, D, D), lambda g: (g, 0, 0)),
        ],
        out_specs=(
            pl.BlockSpec((row_count, D), lambda g: (0, 0)),
            pl.BlockSpec((3, row_count, D), lambda g: (0, 0, 0)),
            pl.BlockSpec((row_count, SPAN), lambda g: (0, 0)),
            pl.BlockSpec((1, D, D), lambda g: (g, 0, 0)),
        ),
        cost_estimate=cost(1e3, 1e3),
        name="project",
        compiler_params=room(10),
    )(features, pack, mod, attention_weight)

    near = swap(quarter, 1)

    attended, stream, second_in, padded, rim_queries, rim_counts, log_totals = pl.pallas_call(
        forward_kernel,
        out_shape=(
            struct((row_count, D), bf16),
            struct((row_count, D), f32),
            struct((row_count, D), bf16),
            struct((2, row_count + 2 * HALO, D), bf16),
            struct((2 * HALO, D), bf16),
            struct((2 * HALO, RIM), bf16),
            struct((row_count, 128), f32),
        ),
        in_specs=[VMEM] * 10,
        out_specs=(VMEM,) * 7,
        scratch_shapes=[pltpu.VMEM((2 * HALO, D), bf16)],
        cost_estimate=cost(1e3, 1e3),
        name="attend",
        compiler_params=room(12),
    )(rim_low, rim_high, info_low, info_high, features, pack, mod, attn_bf, qkv, counts)

    def whole(*shape):
        return pl.BlockSpec(shape, lambda g, s: (0,) * len(shape))

    chunk_shape = struct((2, 2, 2, 128, CHUNK), bf16)
    branch, grad_second, own_kept, own_sent = pl.pallas_call(
        mlp_own_kernel,
        out_shape=(struct((row_count, D), f32), struct((row_count, D), f32), chunk_shape, chunk_shape),
        grid_spec=pltpu.PrefetchScalarGridSpec(
            num_scalar_prefetch=1,
            grid=(2,),
            in_specs=[
                whole(row_count, D),
                whole(row_count, D),
                pl.BlockSpec((D, CHUNK), lambda g, s: (0, g)),
                pl.BlockSpec((CHUNK, D), lambda g, s: (g, 0)),
                pl.BlockSpec(memory_space=pl.ANY),
            ],
            out_specs=(
                whole(row_count, D),
                whole(row_count, D),
                pl.BlockSpec((1, 2, 2, 128, CHUNK), lambda g, s: (g ^ s[1], 0, 0, 0, 0)),
                pl.BlockSpec((1, 2, 2, 128, CHUNK), lambda g, s: (g ^ s[1], 0, 0, 0, 0)),
            ),
            scratch_shapes=[pltpu.VMEM((row_count, CHUNK), bf16)] * 2,
        ),
        cost_estimate=cost(1.3e10, 1e3),
        name="mlp_own",
        compiler_params=room(14),
    )(scalars, second_in, cotangent, up_weight, down_weight, small_past)

    def part(away):
        return pl.BlockSpec(
            (1, 2, 2, 128, CHUNK), lambda g, s: (away ^ s[0] ^ s[1], 0, 0, 0, 0)
        )

    branch, grad_second, near_kept, near_sent = pl.pallas_call(
        mlp_near_kernel,
        out_shape=(struct((row_count, D), f32), struct((row_count, D), f32), chunk_shape, chunk_shape),
        grid_spec=pltpu.PrefetchScalarGridSpec(
            num_scalar_prefetch=1,
            grid=(1,),
            in_specs=[
                whole(row_count, D),
                whole(row_count, D),
                whole(2, D, CHUNK),
                whole(row_count, D),
                whole(row_count, D),
            ],
            out_specs=(whole(row_count, D), whole(row_count, D), part(0), part(0)),
            scratch_shapes=[pltpu.VMEM((row_count, CHUNK), bf16)] * 2,
        ),
        cost_estimate=cost(2.5e9, 4e6),
        name="mlp_near",
        compiler_params=room(10),
    )(scalars, second_in, cotangent, near, branch, grad_second)
    far = swap(after(near, own_kept), 2)
    (
        rest_kept,
        rest_sent,
        output,
        grad_stream,
        grad_attended,
        stats,
        edge_low,
        edge_high,
        table_two,
    ) = pl.pallas_call(
        mlp_far_kernel,
        out_shape=(
            chunk_shape,
            chunk_shape,
            struct((row_count, D), bf16),
            struct((row_count, D), f32),
            struct((row_count, D), bf16),
            struct((row_count, 128), f32),
            struct((HALO, D + 128), bf16),
            struct((HALO, D + 128), bf16),
            struct((8, D), f32),
        ),
        grid_spec=pltpu.PrefetchScalarGridSpec(
            num_scalar_prefetch=1,
            grid=(1,),
            in_specs=[
                whole(row_count, D),
                whole(row_count, D),
                whole(2, D, CHUNK),
                whole(row_count, D),
                whole(row_count, D),
                whole(row_count, D),
                whole(row_count, 128),
                whole(2, 4, D),
                whole(4, D, D),
                whole(row_count, D),
                whole(row_count, 128),
                pl.BlockSpec(memory_space=pl.ANY),
                pl.BlockSpec(memory_space=pl.ANY),
            ],
            out_specs=(
                part(1),
                part(1),
                whole(row_count, D),
                whole(row_count, D),
                whole(row_count, D),
                whole(row_count, 128),
                whole(HALO, D + 128),
                whole(HALO, D + 128),
                whole(8, D),
            ),
            scratch_shapes=[
                pltpu.VMEM((row_count, D), f32),
                pltpu.VMEM((row_count, D), f32),
                pltpu.VMEM((row_count, CHUNK), bf16),
                pltpu.VMEM((row_count, CHUNK), bf16),
            ],
        ),
        input_output_aliases={12: 0, 13: 1},
        cost_estimate=cost(4e9, 8e6),
        name="mlp_far",
        compiler_params=room(16),
    )(
        scalars,
        second_in,
        cotangent,
        far,
        branch,
        grad_second,
        stream,
        pack,
        mod,
        attn_bf,
        attended,
        log_totals,
        near_kept,
        near_sent,
    )

    grad_low = along(edge_high, 1)
    grad_high = along(edge_low, -1)

    large_shape = (2, 2, 2, 128, CHUNK)
    large_keep, large_send = pl.pallas_call(
        large_sum_kernel,
        out_shape=(struct(large_shape, f32), struct(large_shape, bf16)),
        in_specs=[SMEM] + [VMEM] * 4,
        out_specs=(VMEM,) * 2,
        cost_estimate=cost(1e3, 1e3),
        name="large_sum",
        compiler_params=room(12),
    )(scalars, own_kept, swap(own_sent, 2), rest_kept, swap(rest_sent, 2))

    def ordered(kernel, values, tokens, shapes, name, work=1e10):
        return pl.pallas_call(
            kernel,
            out_shape=shapes,
            in_specs=[VMEM] * len(values) + [pl.BlockSpec(memory_space=pl.ANY)] * len(tokens),
            out_specs=jax.tree.map(lambda _: VMEM, shapes),
            cost_estimate=cost(work, 1e3),
            name=name,
            compiler_params=room(8),
        )(*values, *tokens)

    def receive(keep, got, *tokens):
        rows = math.prod(keep.shape[1:-1])
        flat = (2, rows, D)
        keep, send = ordered(
            receive_kernel,
            (keep.reshape(flat), got.reshape(flat)),
            tokens,
            (struct((rows, D), f32), struct((rows, D), bf16)),
            "receive",
        )
        half = (2, rows // 2, D)
        return keep.reshape(half), send.reshape(half)

    def rounded_total(keep, got, *tokens):
        return ordered(total_kernel, (keep, got), tokens, struct(keep.shape, bf16), "total")

    def blend(total, got, past, *tokens, work=1e10):
        flip, mask = 1, 32
        while mask < device_count:
            mine = total.astype(f32) + (got[::-1] if flip else got).astype(f32)
            total, flip = mine.astype(bf16), 0
            got = swap(total, mask)
            mask *= 2
        return ordered(
            functools.partial(blend_kernel, flip),
            (total, got, past),
            tokens,
            struct(total.shape, bf16),
            "blend",
            work,
        ).reshape(-1, D)

    def join(part, got, *tokens, work=1e10):
        rows = math.prod(part.shape[:-1])
        return ordered(
            join_kernel,
            (part.reshape(rows, D), got.reshape(rows, D)),
            tokens,
            struct((2, rows, D), bf16),
            "join",
            work,
        ).reshape(2 * rows, D)

    large_routes = ((4, 8), (1, 4), (8, 1), (16, 16))
    small_routes = ((4, 8), (1, 1), (8, 4), (16, 16))

    padded_rows = row_count + 2 * HALO
    large_got = swap(large_send, *large_routes[0])
    grad_queries, keys_total, values_total = pl.pallas_call(
        backward_kernel,
        out_shape=(struct((row_count, D), bf16),) + (struct((padded_rows, D), f32),) * 2,
        in_specs=[VMEM] * 5 + [pl.BlockSpec(memory_space=pl.ANY)],
        out_specs=(VMEM,) * 3,
        cost_estimate=cost(8e9, 9e6),
        name="attend_back",
        compiler_params=room(10),
    )(qkv, padded, grad_attended, stats, counts, large_send)
    large_keep, large_send = receive(large_keep, large_got, grad_queries)
    large_got = swap(large_send, *large_routes[1])
    piece_shape = struct((2, 2, 2, 2, 80, D), bf16)
    features_grad, small_kept, small_sent = pl.pallas_call(
        weights_kernel,
        out_shape=(struct((row_count, D), f32), piece_shape, piece_shape),
        in_specs=[SMEM, pl.BlockSpec(memory_space=pl.ANY)] + [VMEM] * 16,
        out_specs=(VMEM,) * 3,
        scratch_shapes=[
            pltpu.VMEM((4, row_count, D), bf16),
            pltpu.VMEM((8, D), f32),
            pltpu.VMEM((row_count, D), f32),
            pltpu.VMEM((row_count, D), f32),
            pltpu.VMEM((2, 2, 2, 2, 2, 80, D), bf16),
        ],
        cost_estimate=cost(6e9, 9e6),
        name="attend_weights",
        compiler_params=room(16),
    )(
        scalars,
        large_send,
        grad_queries,
        keys_total,
        values_total,
        padded,
        rim_queries,
        rim_counts,
        grad_low,
        grad_high,
        first_in,
        attended,
        grad_stream,
        features,
        pack,
        mod,
        attn_bf,
        table_two,
    )
    def chain_large(step, *tokens):
        nonlocal large_keep, large_send, large_got
        large_keep, large_send = receive(large_keep, large_got, *tokens)
        large_got = swap(large_send, *large_routes[step])

    def chain_small(step, *tokens):
        nonlocal small_keep, small_send, small_got
        small_keep, small_send = receive(small_keep, small_got, *tokens)
        small_got = swap(small_send, *small_routes[step])

    small_keep, small_send = small_kept, small_sent
    small_got = swap(small_send, 2)
    chain_large(2, small_sent)
    chain_small(0, large_send)
    large_total = rounded_total(large_keep, large_got, small_send)
    large_got = swap(large_total, *large_routes[3])
    chain_small(1, large_total)
    large_part = blend(large_total, large_got, large_past, small_send)
    large_got = swap(large_part, *large_routes[2])
    chain_small(2, large_part)
    large_part = join(large_part, large_got, small_send)
    large_got = swap(large_part, *large_routes[1])
    small_total = rounded_total(small_keep, small_got, large_part)
    small_got = swap(small_total, *small_routes[3])
    large_part = join(large_part, large_got, small_total)
    large_got = swap(large_part, *large_routes[0])
    small_part = blend(small_total, small_got, small_past, large_part, work=8e9)
    small_got = swap(small_part, *small_routes[2])
    small_part = join(small_part, small_got, work=1e3)
    small_got = swap(small_part, *small_routes[1])

    any_space = pl.BlockSpec(memory_space=pl.ANY)
    gathered_shape = (2, 2, 2, 128, CHUNK)
    large_work, large_mix = pl.pallas_call(
        large_first_kernel,
        out_shape=(struct((4, D, CHUNK), bf16), struct((2, D, CHUNK), bf16)),
        in_specs=[SMEM, VMEM, VMEM, any_space],
        out_specs=(VMEM,) * 2,
        scratch_shapes=[pltpu.VMEM((D, D), bf16)],
        cost_estimate=cost(1e3, 1e3),
        name="ortho_large",
        compiler_params=room(10),
    )(scalars, large_part.reshape(gathered_shape), large_got.reshape(gathered_shape), small_part)
    mix_got = swap(large_mix, 2)
    small_part = join(small_part, small_got, large_work)
    small_got = swap(small_part, *small_routes[0])
    large_result = pl.pallas_call(
        large_next_kernel,
        out_shape=struct((2, D, CHUNK), bf16),
        in_specs=[VMEM, any_space],
        out_specs=VMEM,
        scratch_shapes=[pltpu.VMEM((4, D, CHUNK), bf16), pltpu.VMEM((D, D), bf16)],
        cost_estimate=cost(1e3, 1e3),
        name="ortho_large",
        compiler_params=room(10),
    )(large_work, small_part)
    result_got = swap(large_result, 2)

    across = pl.BlockSpec((1, D, 256), lambda g: (g // 2, 0, g % 2))
    left_right = pl.BlockSpec((D, 256), lambda g: (0, g))
    top_bottom = pl.BlockSpec((256, D), lambda g: (g, 0))
    large_shapes = (struct((D, 2 * CHUNK), f32), struct((2 * CHUNK, D), f32))
    small_token = struct((8, 128), f32)
    token_block = pl.BlockSpec((8, 128), lambda g: (0, 0))
    up_moment_new, down_moment_new, moments_done = pl.pallas_call(
        large_moment_kernel,
        grid=(4,),
        out_shape=large_shapes + (small_token,),
        in_specs=[SMEM, across, across, left_right, top_bottom, any_space],
        out_specs=(left_right, top_bottom, token_block),
        cost_estimate=cost(1e3, 1e3),
        name="moment_large",
        compiler_params=room(8),
    )(scalars, large_mix, mix_got, up_moment, down_moment, large_result)

    small_work, small_mix = pl.pallas_call(
        small_start_kernel,
        out_shape=(
            struct((2, 2, 256, D), bf16),
            struct((2, 256 + TABLE_ROWS, D), bf16),
        ),
        in_specs=[SMEM, VMEM, VMEM, any_space],
        out_specs=(VMEM,) * 2,
        scratch_shapes=[pltpu.VMEM((TABLE_ROWS, D), f32)],
        cost_estimate=cost(3e10, 1e3),
        name="unpack_small",
        compiler_params=room(6),
    )(
        scalars,
        small_part.reshape(2, 2, 2, 80, D),
        small_got.reshape(2, 2, 2, 80, D),
        moments_done,
    )
    mix_other = swap(small_mix, 2)

    def fixed(*shape):
        return pl.BlockSpec(shape, lambda g: (0,) * len(shape))

    def one(index):
        return pl.BlockSpec((1, 256, D), index)

    small_result, up_new, down_new = pl.pallas_call(
        small_kernel,
        grid=(NS_STEPS,),
        out_shape=(struct((2, 256, D), bf16),) + large_shapes,
        in_specs=[SMEM, fixed(2, 2, 256, D), across, across, left_right, top_bottom, any_space],
        out_specs=(fixed(2, 256, D), left_right, top_bottom),
        scratch_shapes=[pltpu.VMEM((2, 256, D), bf16)] * 2
        + [pltpu.VMEM((D, D), bf16)] * 2
        + [pltpu.SMEM((2,), f32)],
        cost_estimate=cost(6e9, 1e7),
        name="ortho_small",
        compiler_params=room(16),
    )(scalars, small_work, large_result, result_got, up_weight, down_weight, moments_done)
    small_other = swap(small_result, 2)
    table_block = pl.BlockSpec((1, TABLE_ROWS, D), lambda g: (0, 256 // TABLE_ROWS, 0))
    attention_moment_new, modulation_moment_new, modulation_new, moment_done = pl.pallas_call(
        functools.partial(small_moment_kernel, nodes=row_count * device_count),
        grid=(4,),
        out_shape=(struct((4, 256, D), f32),) + (struct((2, 2, D), f32),) * 2 + (small_token,),
        in_specs=[
            SMEM,
            one(lambda g: (g % 2, 0, 0)),
            one(lambda g: (g % 2, 0, 0)),
            one(lambda g: (g, 0, 0)),
            table_block,
            table_block,
            fixed(2, 4, D),
            fixed(2, 2, D),
            any_space,
        ],
        out_specs=(one(lambda g: (g, 0, 0)), fixed(2, 2, D), fixed(2, 2, D), token_block),
        cost_estimate=cost(1e10, 1e7),
        name="moment_small",
        compiler_params=room(8),
    )(
        scalars,
        small_mix,
        mix_other,
        attention_moment,
        small_mix,
        mix_other,
        modulation,
        modulation_moment,
        small_result,
    )
    attention_new = pl.pallas_call(
        small_weight_kernel,
        grid_spec=pltpu.PrefetchScalarGridSpec(
            num_scalar_prefetch=1,
            grid=(4,),
            in_specs=[
                pl.BlockSpec((1, 256, D), lambda g, s: (g % 2, 0, 0)),
                pl.BlockSpec((1, 256, D), lambda g, s: (g % 2, 0, 0)),
                pl.BlockSpec((1, 256, D), lambda g, s: (g, s[4], 0)),
                any_space,
            ],
            out_specs=pl.BlockSpec((1, 256, D), lambda g, s: (g, 0, 0)),
        ),
        out_shape=struct((4, 256, D), f32),
        cost_estimate=cost(1e7, 6e6),
        name="update_small",
        compiler_params=room(6),
    )(scalars, small_result, small_other, attention_weight, moment_done)
    return (
        output,
        features_grad,
        attention_moment_new,
        attention_new,
        up_moment_new,
        up_new,
        down_moment_new,
        down_new,
        modulation_moment_new,
        modulation_new,
    )


def solution(mesh):
    placed = (
        P(("nodes", "hid"), None),
        P(("nodes", "hid")),
        P(("nodes", "hid"), None),
        P(("nodes", "hid")),
        P(("nodes", "hid"), None),
        P(),
        P(None, "hid"),
        P("hid", None),
        P(),
        P(None, "hid", None),
        P(None, "hid"),
        P("hid", None),
        P(None, "hid", None),
    )
    return jax.shard_map(
        on_device,
        mesh=mesh,
        in_specs=placed,
        out_specs=(
            P(("nodes", "hid"), None),
            P(("nodes", "hid"), None),
            P(None, "hid", None),
            P(None, "hid", None),
            P(None, "hid"),
            P(None, "hid"),
            P("hid", None),
            P("hid", None),
            P(None, "hid", None),
            P(None, "hid", None),
        ),
        check_vma=False,
    )
```

```python
import functools
import math

import jax
import jax.numpy as jnp
from jax import lax
from jax.experimental import pallas as pl
from jax.experimental.pallas import tpu as pltpu
from jax.sharding import PartitionSpec as P

D = 512
HEADS = 4
HD = 128
FF = 2048
K = 16
NS_STEPS = 4
HALO = 192
BLOCK = 128
SPAN = BLOCK + 2 * HALO
RIM = 256
CHUNK = 512
TABLE_ROWS = 16

f32 = jnp.float32
bf16 = jnp.bfloat16
ns_first = 3.4445
ns_second = -4.775
ns_third = 2.0315
momentum_rate = 0.95
vector_rate = 0.9
muon_rate = 0.2
decay_rate = 0.1
score_scale = 1.0 / math.sqrt(HD)
AXES = ("nodes", "hid")
VMEM = pl.BlockSpec(memory_space=pltpu.VMEM)
SMEM = pl.BlockSpec(memory_space=pltpu.SMEM)


def nn(a, b):
    return lax.dot_general(a, b, (((1,), (0,)), ((), ())), preferred_element_type=f32)


def nt(a, b):
    return lax.dot_general(a, b, (((1,), (1,)), ((), ())), preferred_element_type=f32)


def tn(a, b):
    return lax.dot_general(a, b, (((0,), (0,)), ((), ())), preferred_element_type=f32)


def struct(shape, dtype):
    return jax.ShapeDtypeStruct(shape, dtype)


def rows_of(start, size):
    return pl.ds(pl.multiple_of(start, size), size)


def cost(flops, data):
    return pl.CostEstimate(flops=int(flops), bytes_accessed=int(data), transcendentals=0)


def room(mebibytes):
    return pltpu.CompilerParams(vmem_limit_bytes=mebibytes << 20)


def norm_parts(field):
    average = jnp.mean(field, axis=-1, keepdims=True)
    centred = field - average
    variance = jnp.mean(centred * centred, axis=-1, keepdims=True)
    inverse = lax.rsqrt(variance + 1e-06)
    return centred * inverse, inverse


def table_rows(mod_ref, level, column):
    return jnp.where(level > 0.5, mod_ref[1, column : column + 1, :], mod_ref[0, column : column + 1, :])


def modulated(field, level, mod_ref, column):
    normed, _ = norm_parts(field)
    return normed * (1.0 + table_rows(mod_ref, level, column)) + table_rows(
        mod_ref, level, column + 1
    )


def norm_back(grad_out, field, level, mod_ref, column):
    normed, inverse = norm_parts(field)
    grad_norm = grad_out * (1.0 + table_rows(mod_ref, level, column))
    grad_in = inverse * (
        grad_norm
        - jnp.mean(grad_norm, axis=-1, keepdims=True)
        - normed * jnp.mean(grad_norm * normed, axis=-1, keepdims=True)
    )
    return grad_in, grad_out * normed


def add_table(table_ref, column, level, scale_term, shift_term):
    upper = level > 0.5
    for term, place in ((scale_term, column), (shift_term, column + 1)):
        low_part = jnp.sum(jnp.where(upper, 0.0, term), axis=0, keepdims=True)
        high_part = jnp.sum(jnp.where(upper, term, 0.0), axis=0, keepdims=True)
        table_ref[place : place + 1, :] += low_part
        table_ref[4 + place : 5 + place, :] += high_part


def slot_counts(pack, row_count, width, shift):
    pieces = []
    for left in range(0, width, 128):
        lanes = lax.broadcasted_iota(jnp.int32, (row_count, 128), 1)
        rows = lax.broadcasted_iota(jnp.int32, (row_count, 128), 0)
        place = (lanes - rows + (left - shift)).astype(f32)
        total = jnp.zeros((row_count, 128), f32)
        for slot in range(K):
            total = total + jnp.where(place == pack[:, slot : slot + 1], 1.0, 0.0)
        pieces.append(total)
    return jnp.concatenate(pieces, axis=1).astype(bf16)


def quarter_kernel(scalars, up, down, token, rounded):
    rounded[0] = up[...].astype(bf16)
    rounded[1] = down[...].astype(bf16)


def past_kernel(scalars, up, down, attention, large_past, small_past):
    z2 = scalars[3]
    large = jnp.where(scalars[0] == 0, up[...], down[...].T)
    for j in range(2):
        large_past[j ^ z2] = large[j * 128 : (j + 1) * 128]
        small_past[j ^ z2] = attention[0, j * 64 : (j + 1) * 64, :]


def project_kernel(features, pack, mod, weights, first_in, qkv, counts, rounded):
    row_count = features.shape[0]
    turn = pl.program_id(0)

    @pl.when(turn == 0)
    def _():
        for start in range(0, row_count, 256):
            rows = slice(start, start + 256)
            level = pack[rows, K : K + 1]
            first_in[rows, :] = modulated(features[rows, :].astype(f32), level, mod, 0).astype(bf16)

    weight = weights[0].astype(bf16)
    rounded[0] = weight

    @pl.when(turn < 3)
    def _():
        qkv[turn] = nn(first_in[...], weight).astype(bf16)
        share = row_count // BLOCK // 3

        def count_step(b, carry):
            rows = rows_of(b * BLOCK, BLOCK)
            counts[rows, :] = slot_counts(pack[rows, :], BLOCK, SPAN, HALO)
            return carry

        lax.fori_loop(turn * share, (turn + 1) * share, count_step, 0)


def forward_kernel(
    rim_low,
    rim_high,
    features,
    pack,
    mod,
    weights,
    qkv,
    counts,
    attended,
    stream,
    second_in,
    padded,
    rim_queries,
    rim_counts,
    log_totals,
    rim_in,
):
    row_count = features.shape[0]
    for side, rim in enumerate((rim_low, rim_high)):

        def rim_step(b, carry):
            rows = rows_of(b * 64, 64)
            target = pl.ds(pl.multiple_of(side * HALO + b * 64, 64), 64)
            info = rim[rows, D:].astype(f32)
            rim_in[target, :] = modulated(
                rim[rows, :D].astype(f32), info[:, K : K + 1], mod, 0
            ).astype(bf16)
            rim_counts[target, :] = slot_counts(
                info, 64, RIM, b * 64 + (-HALO if side == 0 else RIM)
            )
            return carry

        lax.fori_loop(0, HALO // 64, rim_step, 0)
    rim_queries[...] = nn(rim_in[...], weights[0]).astype(bf16)
    for p in range(2):
        piece = nn(rim_in[...], weights[1 + p]).astype(bf16)
        padded[p, :HALO, :] = piece[:HALO]
        padded[p, HALO + row_count :, :] = piece[HALO:]
        padded[p, HALO : HALO + row_count, :] = qkv[1 + p]

    def step(b, carry):
        rows = rows_of(b * BLOCK, BLOCK)
        span = pl.ds(pl.multiple_of(b * BLOCK, BLOCK), SPAN)
        count = counts[rows, :].astype(f32)
        live = count > 0.0
        columns = [slice(h * HD, (h + 1) * HD) for h in range(HEADS)]
        scores = [nt(qkv[0, rows, cols], padded[0, span, cols]) * score_scale for cols in columns]
        lanes = lax.broadcasted_iota(jnp.int32, (BLOCK, 128), 1)
        stats = jnp.zeros((BLOCK, 128), f32)
        for h, cols in enumerate(columns):
            masked = jnp.where(live, scores[h], -1e30)
            peak = jnp.max(masked, axis=-1, keepdims=True)
            exponent = jnp.exp(masked - peak)
            total = jnp.sum(exponent * count, axis=-1, keepdims=True)
            probs = (exponent * (1.0 / total)).astype(bf16)
            spread = probs * counts[rows, :]
            attended[rows, cols] = nn(spread, padded[1, span, cols]).astype(bf16)
            stats = jnp.where(lanes == h, peak + jnp.log(total), stats)
        log_totals[rows, :] = stats
        return carry

    lax.fori_loop(0, row_count // BLOCK, step, 0)
    for start in range(0, row_count, 256):
        rows = slice(start, start + 256)
        field = features[rows, :].astype(f32) + nn(attended[rows, :], weights[3])
        stream[rows, :] = field
        second_in[rows, :] = modulated(field, pack[rows, K : K + 1], mod, 2).astype(bf16)


def mlp_chunk(
    scalars, second_in, cotangent, up, down, branch_in, grad_in, branch, grad_second, acts, grads, kept, sent
):
    row_count = second_in.shape[0]
    for start in range(0, row_count, 256):
        rows = slice(start, start + 256)
        preact = nn(second_in[rows, :], up)
        grad_act = nt(cotangent[rows, :], down)
        sigmoid = 0.5 * jnp.tanh(0.5 * preact) + 0.5
        act = (preact * sigmoid).astype(bf16)
        acts[rows, :] = act
        grad_pre = (grad_act * (sigmoid * (1.0 + preact * (1.0 - sigmoid)))).astype(bf16)
        grads[rows, :] = grad_pre
        branch[rows, :] = branch_in[rows, :] + nn(act, down)
        grad_second[rows, :] = grad_in[rows, :] + nt(grad_pre, up)
    first, z1, z2 = scalars[0] == 0, scalars[2], scalars[3]
    for out, swapped in ((kept, False), (sent, True)):
        ups = jnp.logical_not(first) if swapped else first
        product = tn(
            jnp.where(ups, second_in[...], cotangent[...]), jnp.where(ups, grads[...], acts[...])
        )
        for q in range(4):
            out[0, (q // 2) ^ z1, (q % 2) ^ z2] = product[q * 128 : (q + 1) * 128].astype(bf16)


def mlp_own_kernel(
    scalars, second_in, cotangent, up, down, token, branch, grad_second, kept, sent, acts, grads
):
    @pl.when(pl.program_id(0) == 0)
    def _():
        branch[...] = jnp.zeros_like(branch)
        grad_second[...] = jnp.zeros_like(grad_second)

    mlp_chunk(
        scalars,
        second_in,
        cotangent,
        up[...].astype(bf16),
        down[...].astype(bf16),
        branch,
        grad_second,
        branch,
        grad_second,
        acts,
        grads,
        kept,
        sent,
    )


def mlp_near_kernel(
    scalars, second_in, cotangent, near, branch_in, grad_in, branch, grad_second, kept, sent, acts, grads
):
    mlp_chunk(
        scalars,
        second_in,
        cotangent,
        near[0],
        near[1],
        branch_in,
        grad_in,
        branch,
        grad_second,
        acts,
        grads,
        kept,
        sent,
    )


def mlp_far_kernel(
    scalars,
    second_in,
    cotangent,
    far,
    branch_in,
    grad_in,
    stream,
    pack,
    mod,
    weights,
    attended,
    log_totals,
    kept_in,
    sent_in,
    kept,
    sent,
    output,
    grad_stream,
    grad_attended,
    stats,
    edge_low,
    edge_high,
    table,
    branch,
    grad_second,
    acts,
    grads,
):
    row_count = second_in.shape[0]
    mlp_chunk(
        scalars,
        second_in,
        cotangent,
        far[0],
        far[1],
        branch_in,
        grad_in,
        branch,
        grad_second,
        acts,
        grads,
        kept,
        sent,
    )
    table[...] = jnp.zeros_like(table)

    for start in range(0, row_count, 256):
        rows = slice(start, start + 256)
        field = stream[rows, :]
        level = pack[rows, K : K + 1]
        output[rows, :] = (field + branch[rows, :]).astype(bf16)
        gradient = grad_second[rows, :]
        grad_field, scale_term = norm_back(gradient, field, level, mod, 2)
        add_table(table, 2, level, scale_term, gradient)
        total = cotangent[rows, :].astype(f32) + grad_field
        grad_stream[rows, :] = total
        back = nt(total.astype(bf16), weights[3]).astype(bf16)
        grad_attended[rows, :] = back
        product = back.astype(f32) * attended[rows, :].astype(f32)
        lanes = lax.broadcasted_iota(jnp.int32, (256, 128), 1)
        kept_stats = log_totals[rows, :]
        for h in range(HEADS):
            delta = jnp.sum(product[:, h * HD : (h + 1) * HD], axis=-1, keepdims=True)
            kept_stats = jnp.where(lanes == HEADS + h, delta, kept_stats)
        stats[rows, :] = kept_stats
    for edge, first in ((edge_low, 0), (edge_high, row_count - HALO)):
        rows = slice(first, first + HALO)
        edge[:, :D] = grad_attended[rows, :]
        known = stats[rows, :]
        upper = known.astype(bf16)
        lower = (known - upper.astype(f32)).astype(bf16).astype(f32)
        edge[:, D:] = (upper.astype(f32) + pltpu.roll(lower, 2 * HEADS, 1)).astype(bf16)


def attention_terms(scores, grad_probs, live, count, log_total, delta):
    probs = jnp.exp(jnp.where(live, scores * score_scale, -1e30) - log_total)
    slopes = (probs * (grad_probs - delta)).astype(bf16)
    return slopes * count, probs.astype(bf16) * count


def backward_kernel(qkv, padded, grad, stats, counts, token, grad_query, keys_total, values_total):
    keys_total[...] = jnp.zeros_like(keys_total)
    values_total[...] = jnp.zeros_like(values_total)

    def step(b, carry):
        rows = rows_of(b * BLOCK, BLOCK)
        span = pl.ds(pl.multiple_of(b * BLOCK, BLOCK), SPAN)
        count = counts[rows, :]
        live = count.astype(f32) > 0.0
        columns = [slice(h * HD, (h + 1) * HD) for h in range(HEADS)]
        products = [
            (nt(qkv[0, rows, cols], padded[0, span, cols]), nt(grad[rows, cols], padded[1, span, cols]))
            for cols in columns
        ]
        terms = [
            attention_terms(
                *products[h],
                live,
                count,
                stats[rows, h : h + 1],
                stats[rows, HEADS + h : HEADS + h + 1],
            )
            for h in range(HEADS)
        ]
        for (slopes, spread), cols in zip(terms, columns):
            grad_query[rows, cols] = (nn(slopes, padded[0, span, cols]) * score_scale).astype(bf16)
            keys_total[span, cols] += tn(slopes, qkv[0, rows, cols])
            values_total[span, cols] += tn(spread, grad[rows, cols])
        return carry

    lax.fori_loop(0, counts.shape[0] // BLOCK, step, 0)


def weights_kernel(
    scalars,
    token,
    queries_in,
    keys_in,
    values_in,
    padded,
    rim_query,
    rim_counts,
    grad_low,
    grad_high,
    first_in,
    attended,
    grad_stream,
    features,
    pack,
    mod,
    weights,
    table_two,
    features_grad,
    kept,
    sent,
    gathered,
    table,
    keys_total,
    values_total,
    blocks,
):
    row_count = first_in.shape[0]
    columns = [slice(h * HD, (h + 1) * HD) for h in range(HEADS)]
    own = slice(HALO, HALO + row_count)
    keys_total[...] = keys_in[own, :]
    values_total[...] = values_in[own, :]
    for side, grads in enumerate((grad_low, grad_high)):
        first = 0 if side == 0 else row_count - RIM
        own_span = slice(first, first + RIM)
        span = slice(HALO + first, HALO + first + RIM)
        rows = slice(side * HALO, (side + 1) * HALO)
        known = grads[:, D:].astype(f32)
        count = rim_counts[rows, :]
        live = count.astype(f32) > 0.0
        products = [
            (nt(rim_query[rows, cols], padded[0, span, cols]), nt(grads[:, cols], padded[1, span, cols]))
            for cols in columns
        ]
        terms = []
        for h in range(HEADS):
            numbers = [known[:, i * HEADS + h : i * HEADS + h + 1] for i in range(4)]
            terms.append(
                attention_terms(*products[h], live, count, numbers[0] + numbers[2], numbers[1] + numbers[3])
            )
        for (slopes, spread), cols in zip(terms, columns):
            keys_total[own_span, cols] += tn(slopes, rim_query[rows, cols])
            values_total[own_span, cols] += tn(spread, grads[:, cols])
    gathered[0] = queries_in[...]
    gathered[1] = (keys_total[...] * score_scale).astype(bf16)
    gathered[2] = values_total[...].astype(bf16)
    table[...] = table_two[...]
    for start in range(0, row_count, 256):
        rows = slice(start, start + 256)
        level = pack[rows, K : K + 1]
        gradient = nt(gathered[0, rows, :], weights[0])
        for p in range(1, 3):
            gradient = gradient + nt(gathered[p, rows, :], weights[p])
        grad_field, scale_term = norm_back(gradient, features[rows, :].astype(f32), level, mod, 0)
        add_table(table, 0, level, scale_term, gradient)
        total = grad_stream[rows, :]
        features_grad[rows, :] = total + grad_field
        gathered[3, rows, :] = total.astype(bf16)
    core, slot_bit, z1, z2, hid = (scalars[i] for i in range(5))

    def product_step(n, carry):
        away, slot = n // 2, n % 2
        target = core ^ away
        p = 2 * target + slot
        product = tn(jnp.where(p < 3, first_in[...], attended[...]), gathered[p])
        for half in range(2):
            for q in range(4):
                slot_at, hid_at, row_half = slot ^ slot_bit, half ^ hid, (q // 2) ^ z1
                index = (
                    away,
                    jnp.where(target == 0, slot_at, row_half),
                    hid_at,
                    jnp.where(target == 0, row_half, slot_at),
                    (q % 2) ^ z2,
                )
                start = half * 256 + q * 64
                blocks[index + (slice(0, 64),)] = product[start : start + 64].astype(bf16)
                row = (q // 2) * 4 + 2 * half + q % 2
                known = jnp.broadcast_to(table[row : row + 1, :], (TABLE_ROWS, D))
                blocks[index + (slice(64, 80),)] = jnp.where(p == 0, known, 0.0).astype(bf16)
        return carry

    lax.fori_loop(0, 4, product_step, 0)
    kept[...] = blocks[0]
    sent[...] = blocks[1]


def large_sum_kernel(scalars, own, own_got, rest, rest_got, keep, send):
    first = scalars[0] == 0
    for away, out in ((0, keep), (1, send)):
        for source, got, h in ((own, own_got, 0), (rest, rest_got, 1)):
            for i in range(2):
                where_from = (jnp.where(first, away, i), jnp.where(first, i, away))
                where_to = (jnp.where(first, h, i), jnp.where(first, i, h))
                total = source[where_from].astype(f32) + got[where_from].astype(f32)
                out[where_to] = total.astype(out.dtype)


def receive_kernel(*refs):
    kept, got, keep, send = refs[0], refs[1], refs[-2], refs[-1]
    keep[...] = kept[0].astype(f32) + got[0].astype(f32)
    send[...] = (kept[1].astype(f32) + got[1].astype(f32)).astype(bf16)


def relay_kernel(*refs):
    refs[-1][...] = jnp.zeros_like(refs[-1])


def total_kernel(*refs):
    kept, got, total = refs[0], refs[1], refs[-1]
    total[...] = (kept[...] + got[...].astype(f32)).astype(bf16)


def blend_kernel(flip, *refs):
    kept, got, past, part = refs[0], refs[1], refs[2], refs[-1]
    rows = past.shape[1]
    for j in range(2):
        total = kept[j].astype(f32) + got[j ^ flip].astype(f32)
        blended = (1.0 + momentum_rate) * total[:rows] + momentum_rate * momentum_rate * past[j]
        part[j, :rows, :] = blended.astype(bf16)
        if rows < part.shape[1]:
            part[j, rows:, :] = total[rows:].astype(bf16)


def join_kernel(*refs):
    part, got, pieces = refs[0], refs[1], refs[-1]
    pieces[0] = part[...]
    pieces[1] = got[...]


def newton_schulz(groups, polys, rows_first, scales):
    blocks = [[[ref[i] for i in half] for half in halves] for ref, halves in groups]
    grams = []
    for halves, scale in zip(blocks, scales):
        sums = []
        for half in halves:
            total = None
            for block in half:
                term = tn(block, block) if rows_first else nt(block, block)
                total = term if total is None else total + term
            sums.append((total if scale is None else total * (scale * scale)).astype(bf16))
        grams.append((sums[0].astype(f32) + sums[1].astype(f32)).astype(bf16))
    for gram, poly in zip(grams, polys):
        poly[...] = (ns_second * gram.astype(f32) + ns_third * nn(gram, gram)).astype(bf16)
    for (ref, halves), values, poly, scale in zip(groups, blocks, polys, scales):
        for half, half_values in zip(halves, values):
            for i, block in zip(half, half_values):
                other = nn(block, poly[...]) if rows_first else nn(poly[...], block)
                total = ns_first * block.astype(f32) + other
                ref[i] = (total if scale is None else total * scale).astype(bf16)


def large_start_kernel(scalars, kept, got, work, poly):
    core, slot_bit, z1, z2 = (scalars[i] for i in range(4))
    total = jnp.zeros((8, D), f32)
    for n in range(16):
        b1, b2, b3, b4 = n // 8, (n // 4) % 2, (n // 2) % 2, n % 2
        source = kept if b1 == 0 else got
        block = source[b2, b3, b4]
        value = block.astype(f32)
        total = total + jnp.sum((value * value).reshape(16, 8, D), axis=0)
        slot = jnp.where(core == 0, b1, b2)
        half = jnp.where(core == 0, b2, b3)
        row_half = jnp.where(core == 0, b3, b1)
        start = ((row_half ^ z1) * 2 + (b4 ^ z2)) * 128
        work[half * 2 + (slot ^ slot_bit), rows_of(start, 128), :] = block
    return 1.0 / (jnp.sqrt(jnp.sum(total)) + 1e-07)


large_halves = ((0, 1), (2, 3))


def large_first_kernel(scalars, kept, got, token, work, blend, poly):
    scale = large_start_kernel(scalars, kept, got, work, poly)
    for s in range(2):
        blend[s] = work[s]

    def step(i, factor):
        newton_schulz([(work, large_halves)], [poly], False, [factor])
        return jnp.ones((), f32)

    lax.fori_loop(0, NS_STEPS // 2, step, scale)


def large_next_kernel(given, token, result, work, poly):
    work[...] = given[...]

    def step(i, carry):
        newton_schulz([(work, large_halves)], [poly], False, [None])
        return carry

    lax.fori_loop(NS_STEPS // 2, NS_STEPS, step, 0)
    for s in range(2):
        result[s] = work[s]


def small_start_kernel(scalars, kept, got, token, work, blend, table):
    table[...] = jnp.zeros_like(table)
    core, slot_bit, z1, z2 = (scalars[i] for i in range(4))
    for n in range(16):
        b1, b2, b3, b4 = n // 8, (n // 4) % 2, (n // 2) % 2, n % 2
        source = kept if b1 == 0 else got
        block = source[b2, b3, b4]
        slot = jnp.where(core == 0, b1, b3) ^ slot_bit
        half = b2
        row_half = jnp.where(core == 0, b3, b1)
        quarter = (row_half ^ z1) * 2 + (b4 ^ z2)
        work[slot, half, rows_of(quarter * 64, 64), :] = block[:64]

        @pl.when((slot == 0) & (half == 0))
        def _():
            table[pl.ds(quarter, 1), :] = block[64:].astype(f32)[:1]

    for s in range(2):
        blend[s, :256, :] = work[s, 0]
        blend[s, 256:, :] = table[...].astype(bf16)


def small_kernel(
    scalars,
    given,
    own,
    got,
    up_weight,
    down_weight,
    token,
    result,
    up_new,
    down_new,
    first,
    second,
    poly_first,
    poly_second,
    factors,
):
    turn = pl.program_id(0)
    works = (first, second)

    @pl.when(turn == 0)
    def _():
        for s, work in enumerate(works):
            total = jnp.zeros((8, D), f32)
            for half in range(2):
                block = given[s, half]
                work[half] = block
                value = block.astype(f32)
                total = total + jnp.sum((value * value).reshape(32, 8, D), axis=0)
            factors[s] = 1.0 / (jnp.sqrt(jnp.sum(total)) + 1e-07)

    groups = [(work, ((0,), (1,))) for work in works]
    scales = [jnp.where(turn == 0, factors[s], 1.0) for s in range(2)]
    newton_schulz(groups, [poly_first, poly_second], True, scales)
    is_up = scalars[0] == 0
    ups = jnp.where(is_up, own[0], got[0])
    downs = jnp.where(is_up, got[0], own[0])
    up_new[...] = new_weight(up_weight[...], ups.astype(f32), FF)
    down_new[...] = new_weight(down_weight[...], downs.T.astype(f32), FF)

    @pl.when(turn == NS_STEPS - 1)
    def _():
        for s, work in enumerate(works):
            result[s] = work[0]


def new_moment(blend, moment):
    share = 1.0 / (1.0 + momentum_rate)
    return share * blend + (momentum_rate - share * momentum_rate * momentum_rate) * moment


def new_weight(weight, ortho, longest):
    return weight - muon_rate * (0.2 * math.sqrt(longest) * ortho + decay_rate * weight)


def large_moment_kernel(scalars, own, got, up_moment, down_moment, token, up_moment_new, down_moment_new, done):
    done[...] = jnp.zeros_like(done)
    first = scalars[0] == 0
    ups, downs = jnp.where(first, own[0], got[0]), jnp.where(first, got[0], own[0])
    up_moment_new[...] = new_moment(ups.astype(f32), up_moment[...])
    down_moment_new[...] = new_moment(downs.T.astype(f32), down_moment[...])


def small_moment_kernel(
    scalars,
    mix,
    mix_got,
    moment,
    table,
    table_got,
    modulation,
    held_moment,
    token,
    moment_new,
    held_moment_new,
    held_new,
    done,
    *,
    nodes,
):
    done[...] = jnp.zeros_like(done)
    core, turn = scalars[0], pl.program_id(0)
    blend = jnp.where(core == turn // 2, mix[0], mix_got[0]).astype(f32)
    moment_new[0] = new_moment(blend, moment[0])

    @pl.when(turn == 0)
    def _():
        total = jnp.where(core == 0, table[0], table_got[0]).astype(f32)
        for level in range(2):
            for column in range(2):
                row = level * 2 + column
                at = (slice(level, level + 1), slice(column, column + 1))
                value = vector_rate * held_moment[at] + total[row : row + 1, :].reshape(1, 1, D)
                held = modulation[level : level + 1, pl.ds(scalars[4] * 2 + column, 1)]
                held_moment_new[at] = value
                held_new[at] = held - 0.2 / math.sqrt(nodes) * value


def small_weight_kernel(scalars, own, got, weight, token, weight_new):
    mine = scalars[0] == pl.program_id(0) // 2
    ortho = jnp.where(mine, own[0].astype(f32), got[0].astype(f32))
    weight_new[0] = new_weight(weight[0], ortho, D)


def on_device(
    features,
    levels,
    neighbour_index,
    neighbour_count,
    cotangent,
    attention_weight,
    up_weight,
    down_weight,
    modulation,
    attention_moment,
    up_moment,
    down_moment,
    modulation_moment,
):
    row_count = features.shape[0]
    device_count = lax.axis_size(AXES)
    me = lax.axis_index(AXES)
    first_row = me * row_count

    def bit(place):
        return (me >> place) & 1

    hid, core, slot_bit, z1, z2 = (bit(place) for place in range(5))
    scalars = jnp.stack([core, slot_bit, z1, z2, hid]).astype(jnp.int32)
    is_first = core == 0

    def along(value, distance):
        pairs = [(i, i + distance) for i in range(device_count) if 0 <= i + distance < device_count]
        return lax.ppermute(value, AXES, pairs)

    def after(value, *others):
        return lax.optimization_barrier((value,) + others)[0]

    def swap(value, mask, other=None):
        masks = (mask, mask if other is None else other)
        pairs = [(i, i ^ masks[(i // 2) % 2]) for i in range(device_count)]
        return lax.ppermute(value, AXES, pairs)

    live = jnp.arange(K, dtype=jnp.int32)[None, :] < neighbour_count[:, None]
    row_ids = first_row + jnp.arange(row_count, dtype=jnp.int32)[:, None]
    offsets = jnp.where(live, neighbour_index - row_ids, 512)
    pack = jnp.concatenate(
        [offsets, levels[:, None], jnp.zeros((row_count, 128 - K - 1), jnp.int32)], axis=1
    ).astype(f32)
    rims = jnp.concatenate([features, pack.astype(bf16)], axis=1)
    low_edge, high_edge = rims[row_count - HALO :], rims[:HALO]
    rim_low = along(low_edge, 1)
    rim_high = along(high_edge, -1)

    pack, scalars, is_first = lax.optimization_barrier((pack, scalars, is_first))
    mod = modulation

    quarter = pl.pallas_call(
        quarter_kernel,
        grid_spec=pltpu.PrefetchScalarGridSpec(
            num_scalar_prefetch=1,
            grid=(1,),
            in_specs=[
                pl.BlockSpec((D, CHUNK), lambda g, s: (0, s[0])),
                pl.BlockSpec((CHUNK, D), lambda g, s: (s[0], 0)),
                pl.BlockSpec(memory_space=pl.ANY),
            ],
            out_specs=pl.BlockSpec((2, D, CHUNK), lambda g, s: (0, 0, 0)),
        ),
        out_shape=struct((2, D, CHUNK), bf16),
        cost_estimate=cost(1e6, 3e6),
        name="quarter",
        compiler_params=room(8),
    )(scalars, up_weight, down_weight, low_edge)
    large_past, small_past = pl.pallas_call(
        past_kernel,
        grid_spec=pltpu.PrefetchScalarGridSpec(
            num_scalar_prefetch=1,
            grid=(1,),
            in_specs=[
                pl.BlockSpec((256, CHUNK), lambda g, s: (s[2], s[1])),
                pl.BlockSpec((CHUNK, 256), lambda g, s: (s[1], s[2])),
                pl.BlockSpec((1, 128, D), lambda g, s: (s[0] * 2 + s[1], s[2], 0)),
            ],
            out_specs=(
                pl.BlockSpec((2, 128, CHUNK), lambda g, s: (0, 0, 0)),
                pl.BlockSpec((2, 64, D), lambda g, s: (0, 0, 0)),
            ),
        ),
        out_shape=(struct((2, 128, CHUNK), f32), struct((2, 64, D), f32)),
        cost_estimate=cost(1e6, 1e6),
        name="past",
        compiler_params=room(4),
    )(scalars, up_moment, down_moment, attention_moment)
    first_in, qkv, counts, attn_bf = pl.pallas_call(
        project_kernel,
        grid=(4,),
        out_shape=(
            struct((row_count, D), bf16),
            struct((3, row_count, D), bf16),
            struct((row_count, SPAN), bf16),
            struct((4, D, D), bf16),
        ),
        in_specs=[
            pl.BlockSpec((row_count, D), lambda g: (0, 0)),
            pl.BlockSpec((row_count, 128), lambda g: (0, 0)),
            pl.BlockSpec((2, 4, D), lambda g: (0, 0, 0)),
            pl.BlockSpec((1, D, D), lambda g: (g, 0, 0)),
        ],
        out_specs=(
            pl.BlockSpec((row_count, D), lambda g: (0, 0)),
            pl.BlockSpec((3, row_count, D), lambda g: (0, 0, 0)),
            pl.BlockSpec((row_count, SPAN), lambda g: (0, 0)),
            pl.BlockSpec((1, D, D), lambda g: (g, 0, 0)),
        ),
        cost_estimate=cost(1e3, 1e3),
        name="project",
        compiler_params=room(10),
    )(features, pack, mod, attention_weight)

    near = swap(quarter, 1)

    attended, stream, second_in, padded, rim_queries, rim_counts, log_totals = pl.pallas_call(
        forward_kernel,
        out_shape=(
            struct((row_count, D), bf16),
            struct((row_count, D), f32),
            struct((row_count, D), bf16),
            struct((2, row_count + 2 * HALO, D), bf16),
            struct((2 * HALO, D), bf16),
            struct((2 * HALO, RIM), bf16),
            struct((row_count, 128), f32),
        ),
        in_specs=[VMEM] * 8,
        out_specs=(VMEM,) * 7,
        scratch_shapes=[pltpu.VMEM((2 * HALO, D), bf16)],
        cost_estimate=cost(1e3, 1e3),
        name="attend",
        compiler_params=room(12),
    )(rim_low, rim_high, features, pack, mod, attn_bf, qkv, counts)

    def whole(*shape):
        return pl.BlockSpec(shape, lambda g, s: (0,) * len(shape))

    chunk_shape = struct((2, 2, 2, 128, CHUNK), bf16)
    branch, grad_second, own_kept, own_sent = pl.pallas_call(
        mlp_own_kernel,
        out_shape=(struct((row_count, D), f32), struct((row_count, D), f32), chunk_shape, chunk_shape),
        grid_spec=pltpu.PrefetchScalarGridSpec(
            num_scalar_prefetch=1,
            grid=(2,),
            in_specs=[
                whole(row_count, D),
                whole(row_count, D),
                pl.BlockSpec((D, CHUNK), lambda g, s: (0, g)),
                pl.BlockSpec((CHUNK, D), lambda g, s: (g, 0)),
                pl.BlockSpec(memory_space=pl.ANY),
            ],
            out_specs=(
                whole(row_count, D),
                whole(row_count, D),
                pl.BlockSpec((1, 2, 2, 128, CHUNK), lambda g, s: (g ^ s[1], 0, 0, 0, 0)),
                pl.BlockSpec((1, 2, 2, 128, CHUNK), lambda g, s: (g ^ s[1], 0, 0, 0, 0)),
            ),
            scratch_shapes=[pltpu.VMEM((row_count, CHUNK), bf16)] * 2,
        ),
        cost_estimate=cost(1e10, 1e3),
        name="mlp_own",
        compiler_params=room(14),
    )(scalars, second_in, cotangent, up_weight, down_weight, small_past)

    def part(away):
        return pl.BlockSpec(
            (1, 2, 2, 128, CHUNK), lambda g, s: (away ^ s[0] ^ s[1], 0, 0, 0, 0)
        )

    branch, grad_second, near_kept, near_sent = pl.pallas_call(
        mlp_near_kernel,
        out_shape=(struct((row_count, D), f32), struct((row_count, D), f32), chunk_shape, chunk_shape),
        grid_spec=pltpu.PrefetchScalarGridSpec(
            num_scalar_prefetch=1,
            grid=(1,),
            in_specs=[
                whole(row_count, D),
                whole(row_count, D),
                whole(2, D, CHUNK),
                whole(row_count, D),
                whole(row_count, D),
            ],
            out_specs=(whole(row_count, D), whole(row_count, D), part(0), part(0)),
            scratch_shapes=[pltpu.VMEM((row_count, CHUNK), bf16)] * 2,
        ),
        cost_estimate=cost(2.5e9, 4e6),
        name="mlp_near",
        compiler_params=room(10),
    )(scalars, second_in, cotangent, near, branch, grad_second)
    far = swap(after(near, own_kept), 2)
    (
        rest_kept,
        rest_sent,
        output,
        grad_stream,
        grad_attended,
        stats,
        edge_low,
        edge_high,
        table_two,
    ) = pl.pallas_call(
        mlp_far_kernel,
        out_shape=(
            chunk_shape,
            chunk_shape,
            struct((row_count, D), bf16),
            struct((row_count, D), f32),
            struct((row_count, D), bf16),
            struct((row_count, 128), f32),
            struct((HALO, D + 128), bf16),
            struct((HALO, D + 128), bf16),
            struct((8, D), f32),
        ),
        grid_spec=pltpu.PrefetchScalarGridSpec(
            num_scalar_prefetch=1,
            grid=(1,),
            in_specs=[
                whole(row_count, D),
                whole(row_count, D),
                whole(2, D, CHUNK),
                whole(row_count, D),
                whole(row_count, D),
                whole(row_count, D),
                whole(row_count, 128),
                whole(2, 4, D),
                whole(4, D, D),
                whole(row_count, D),
                whole(row_count, 128),
                pl.BlockSpec(memory_space=pl.ANY),
                pl.BlockSpec(memory_space=pl.ANY),
            ],
            out_specs=(
                part(1),
                part(1),
                whole(row_count, D),
                whole(row_count, D),
                whole(row_count, D),
                whole(row_count, 128),
                whole(HALO, D + 128),
                whole(HALO, D + 128),
                whole(8, D),
            ),
            scratch_shapes=[
                pltpu.VMEM((row_count, D), f32),
                pltpu.VMEM((row_count, D), f32),
                pltpu.VMEM((row_count, CHUNK), bf16),
                pltpu.VMEM((row_count, CHUNK), bf16),
            ],
        ),
        input_output_aliases={12: 0, 13: 1},
        cost_estimate=cost(4e9, 8e6),
        name="mlp_far",
        compiler_params=room(16),
    )(
        scalars,
        second_in,
        cotangent,
        far,
        branch,
        grad_second,
        stream,
        pack,
        mod,
        attn_bf,
        attended,
        log_totals,
        near_kept,
        near_sent,
    )

    grad_low = along(edge_high, 1)
    grad_high = along(edge_low, -1)

    large_shape = (2, 2, 2, 128, CHUNK)
    large_keep, large_send = pl.pallas_call(
        large_sum_kernel,
        out_shape=(struct(large_shape, f32), struct(large_shape, bf16)),
        in_specs=[SMEM] + [VMEM] * 4,
        out_specs=(VMEM,) * 2,
        cost_estimate=cost(1e3, 1e3),
        name="large_sum",
        compiler_params=room(12),
    )(scalars, own_kept, swap(own_sent, 2), rest_kept, swap(rest_sent, 2))

    def ordered(kernel, values, tokens, shapes, name, work=1e10):
        return pl.pallas_call(
            kernel,
            out_shape=shapes,
            in_specs=[VMEM] * len(values) + [pl.BlockSpec(memory_space=pl.ANY)] * len(tokens),
            out_specs=jax.tree.map(lambda _: VMEM, shapes),
            cost_estimate=cost(work, 1e3),
            name=name,
            compiler_params=room(8),
        )(*values, *tokens)

    def receive(keep, got, *tokens):
        rows = math.prod(keep.shape[1:-1])
        flat = (2, rows, D)
        keep, send = ordered(
            receive_kernel,
            (keep.reshape(flat), got.reshape(flat)),
            tokens,
            (struct((rows, D), f32), struct((rows, D), bf16)),
            "receive",
        )
        half = (2, rows // 2, D)
        return keep.reshape(half), send.reshape(half)

    def rounded_total(keep, got, *tokens):
        return ordered(total_kernel, (keep, got), tokens, struct(keep.shape, bf16), "total")

    def blend(total, got, past, *tokens, work=1e10):
        flip, mask = 1, 32
        while mask < device_count:
            mine = total.astype(f32) + (got[::-1] if flip else got).astype(f32)
            total, flip = mine.astype(bf16), 0
            got = swap(total, mask)
            mask *= 2
        return ordered(
            functools.partial(blend_kernel, flip),
            (total, got, past),
            tokens,
            struct(total.shape, bf16),
            "blend",
            work,
        ).reshape(-1, D)

    def join(part, got, *tokens, work=1e10):
        rows = math.prod(part.shape[:-1])
        return ordered(
            join_kernel,
            (part.reshape(rows, D), got.reshape(rows, D)),
            tokens,
            struct((2, rows, D), bf16),
            "join",
            work,
        ).reshape(2 * rows, D)

    large_routes = ((4, 8), (1, 4), (8, 1), (16, 16))
    small_routes = ((4, 8), (1, 1), (8, 4), (16, 16))

    padded_rows = row_count + 2 * HALO
    large_got = swap(large_send, *large_routes[0])
    grad_queries, keys_total, values_total = pl.pallas_call(
        backward_kernel,
        out_shape=(struct((row_count, D), bf16),) + (struct((padded_rows, D), f32),) * 2,
        in_specs=[VMEM] * 5 + [pl.BlockSpec(memory_space=pl.ANY)],
        out_specs=(VMEM,) * 3,
        cost_estimate=cost(1e3, 1e3),
        name="attend_back",
        compiler_params=room(10),
    )(qkv, padded, grad_attended, stats, counts, large_send)
    edges_here = ordered(
        relay_kernel, (), (grad_low, grad_high, grad_queries), struct((8, 128), f32), "relay"
    )
    large_keep, large_send = receive(large_keep, large_got, edges_here)
    large_got = swap(large_send, *large_routes[1])
    piece_shape = struct((2, 2, 2, 2, 80, D), bf16)
    features_grad, small_kept, small_sent = pl.pallas_call(
        weights_kernel,
        out_shape=(struct((row_count, D), f32), piece_shape, piece_shape),
        in_specs=[SMEM, pl.BlockSpec(memory_space=pl.ANY)] + [VMEM] * 16,
        out_specs=(VMEM,) * 3,
        scratch_shapes=[
            pltpu.VMEM((4, row_count, D), bf16),
            pltpu.VMEM((8, D), f32),
            pltpu.VMEM((row_count, D), f32),
            pltpu.VMEM((row_count, D), f32),
            pltpu.VMEM((2, 2, 2, 2, 2, 80, D), bf16),
        ],
        cost_estimate=cost(6e9, 9e6),
        name="attend_weights",
        compiler_params=room(16),
    )(
        scalars,
        large_send,
        grad_queries,
        keys_total,
        values_total,
        padded,
        rim_queries,
        rim_counts,
        grad_low,
        grad_high,
        first_in,
        attended,
        grad_stream,
        features,
        pack,
        mod,
        attn_bf,
        table_two,
    )
    def chain_large(step, *tokens):
        nonlocal large_keep, large_send, large_got
        large_keep, large_send = receive(large_keep, large_got, *tokens)
        large_got = swap(large_send, *large_routes[step])

    def chain_small(step, *tokens):
        nonlocal small_keep, small_send, small_got
        small_keep, small_send = receive(small_keep, small_got, *tokens)
        small_got = swap(small_send, *small_routes[step])

    small_keep, small_send = small_kept, small_sent
    small_got = swap(small_send, 2)
    chain_large(2, small_sent)
    chain_small(0, large_send)
    large_total = rounded_total(large_keep, large_got, small_send)
    large_got = swap(large_total, *large_routes[3])
    chain_small(1, large_total)
    large_part = blend(large_total, large_got, large_past, small_send)
    large_got = swap(large_part, *large_routes[2])
    chain_small(2, large_part)
    large_part = join(large_part, large_got, small_send)
    large_got = swap(large_part, *large_routes[1])
    small_total = rounded_total(small_keep, small_got, large_part)
    small_got = swap(small_total, *small_routes[3])
    large_part = join(large_part, large_got, small_total)
    large_got = swap(large_part, *large_routes[0])
    small_part = blend(small_total, small_got, small_past, large_part, work=8e9)
    small_got = swap(small_part, *small_routes[2])
    small_part = join(small_part, small_got, work=1e3)
    small_got = swap(small_part, *small_routes[1])

    any_space = pl.BlockSpec(memory_space=pl.ANY)
    gathered_shape = (2, 2, 2, 128, CHUNK)
    large_work, large_mix = pl.pallas_call(
        large_first_kernel,
        out_shape=(struct((4, D, CHUNK), bf16), struct((2, D, CHUNK), bf16)),
        in_specs=[SMEM, VMEM, VMEM, any_space],
        out_specs=(VMEM,) * 2,
        scratch_shapes=[pltpu.VMEM((D, D), bf16)],
        cost_estimate=cost(1e3, 1e3),
        name="ortho_large",
        compiler_params=room(10),
    )(scalars, large_part.reshape(gathered_shape), large_got.reshape(gathered_shape), small_part)
    mix_got = swap(large_mix, 2)
    small_part = join(small_part, small_got, large_work)
    small_got = swap(small_part, *small_routes[0])
    large_result = pl.pallas_call(
        large_next_kernel,
        out_shape=struct((2, D, CHUNK), bf16),
        in_specs=[VMEM, any_space],
        out_specs=VMEM,
        scratch_shapes=[pltpu.VMEM((4, D, CHUNK), bf16), pltpu.VMEM((D, D), bf16)],
        cost_estimate=cost(1e3, 1e3),
        name="ortho_large",
        compiler_params=room(10),
    )(large_work, small_part)
    result_got = swap(large_result, 2)

    across = pl.BlockSpec((1, D, 256), lambda g: (g // 2, 0, g % 2))
    left_right = pl.BlockSpec((D, 256), lambda g: (0, g))
    top_bottom = pl.BlockSpec((256, D), lambda g: (g, 0))
    large_shapes = (struct((D, 2 * CHUNK), f32), struct((2 * CHUNK, D), f32))
    small_token = struct((8, 128), f32)
    token_block = pl.BlockSpec((8, 128), lambda g: (0, 0))
    up_moment_new, down_moment_new, moments_done = pl.pallas_call(
        large_moment_kernel,
        grid=(4,),
        out_shape=large_shapes + (small_token,),
        in_specs=[SMEM, across, across, left_right, top_bottom, any_space],
        out_specs=(left_right, top_bottom, token_block),
        cost_estimate=cost(1e3, 1e3),
        name="moment_large",
        compiler_params=room(8),
    )(scalars, large_mix, mix_got, up_moment, down_moment, large_result)

    small_work, small_mix = pl.pallas_call(
        small_start_kernel,
        out_shape=(
            struct((2, 2, 256, D), bf16),
            struct((2, 256 + TABLE_ROWS, D), bf16),
        ),
        in_specs=[SMEM, VMEM, VMEM, any_space],
        out_specs=(VMEM,) * 2,
        scratch_shapes=[pltpu.VMEM((TABLE_ROWS, D), f32)],
        cost_estimate=cost(3e10, 1e3),
        name="unpack_small",
        compiler_params=room(6),
    )(
        scalars,
        small_part.reshape(2, 2, 2, 80, D),
        small_got.reshape(2, 2, 2, 80, D),
        moments_done,
    )
    mix_other = swap(small_mix, 2)

    def fixed(*shape):
        return pl.BlockSpec(shape, lambda g: (0,) * len(shape))

    def one(index):
        return pl.BlockSpec((1, 256, D), index)

    small_result, up_new, down_new = pl.pallas_call(
        small_kernel,
        grid=(NS_STEPS,),
        out_shape=(struct((2, 256, D), bf16),) + large_shapes,
        in_specs=[SMEM, fixed(2, 2, 256, D), across, across, left_right, top_bottom, any_space],
        out_specs=(fixed(2, 256, D), left_right, top_bottom),
        scratch_shapes=[pltpu.VMEM((2, 256, D), bf16)] * 2
        + [pltpu.VMEM((D, D), bf16)] * 2
        + [pltpu.SMEM((2,), f32)],
        cost_estimate=cost(6e9, 1e7),
        name="ortho_small",
        compiler_params=room(16),
    )(scalars, small_work, large_result, result_got, up_weight, down_weight, moments_done)
    small_other = swap(small_result, 2)
    table_block = pl.BlockSpec((1, TABLE_ROWS, D), lambda g: (0, 256 // TABLE_ROWS, 0))
    attention_moment_new, modulation_moment_new, modulation_new, moment_done = pl.pallas_call(
        functools.partial(small_moment_kernel, nodes=row_count * device_count),
        grid=(4,),
        out_shape=(struct((4, 256, D), f32),) + (struct((2, 2, D), f32),) * 2 + (small_token,),
        in_specs=[
            SMEM,
            one(lambda g: (g % 2, 0, 0)),
            one(lambda g: (g % 2, 0, 0)),
            one(lambda g: (g, 0, 0)),
            table_block,
            table_block,
            fixed(2, 4, D),
            fixed(2, 2, D),
            any_space,
        ],
        out_specs=(one(lambda g: (g, 0, 0)), fixed(2, 2, D), fixed(2, 2, D), token_block),
        cost_estimate=cost(1e10, 1e7),
        name="moment_small",
        compiler_params=room(8),
    )(
        scalars,
        small_mix,
        mix_other,
        attention_moment,
        small_mix,
        mix_other,
        modulation,
        modulation_moment,
        small_result,
    )
    attention_new = pl.pallas_call(
        small_weight_kernel,
        grid_spec=pltpu.PrefetchScalarGridSpec(
            num_scalar_prefetch=1,
            grid=(4,),
            in_specs=[
                pl.BlockSpec((1, 256, D), lambda g, s: (g % 2, 0, 0)),
                pl.BlockSpec((1, 256, D), lambda g, s: (g % 2, 0, 0)),
                pl.BlockSpec((1, 256, D), lambda g, s: (g, s[4], 0)),
                any_space,
            ],
            out_specs=pl.BlockSpec((1, 256, D), lambda g, s: (g, 0, 0)),
        ),
        out_shape=struct((4, 256, D), f32),
        cost_estimate=cost(1e7, 6e6),
        name="update_small",
        compiler_params=room(6),
    )(scalars, small_result, small_other, attention_weight, moment_done)
    return (
        output,
        features_grad,
        attention_moment_new,
        attention_new,
        up_moment_new,
        up_new,
        down_moment_new,
        down_new,
        modulation_moment_new,
        modulation_new,
    )


def solution(mesh):
    placed = (
        P(("nodes", "hid"), None),
        P(("nodes", "hid")),
        P(("nodes", "hid"), None),
        P(("nodes", "hid")),
        P(("nodes", "hid"), None),
        P(),
        P(None, "hid"),
        P("hid", None),
        P(),
        P(None, "hid", None),
        P(None, "hid"),
        P("hid", None),
        P(None, "hid", None),
    )
    return jax.shard_map(
        on_device,
        mesh=mesh,
        in_specs=placed,
        out_specs=(
            P(("nodes", "hid"), None),
            P(("nodes", "hid"), None),
            P(None, "hid", None),
            P(None, "hid", None),
            P(None, "hid"),
            P(None, "hid"),
            P("hid", None),
            P("hid", None),
            P(None, "hid", None),
            P(None, "hid", None),
        ),
        check_vma=False,
    )
```
